512 devices in a mesh: row: 16 (over z, core), col: 32 (over x, y).
Axes of the slice: x: 4, y: 8, z: 8, core: 2. Of those that a mesh axis runs over, the one named last changes fastest.
Arguments:
- tokens: bfloat16 [512, 8192], P('col', 'row'), may hold values from -24 to 24
- scales: float32 [8192], P('row'), may hold values from 0.25 to 4
- gate_weight: bfloat16 [8192, 16384], P('row', 'col'), may hold values from -0.0625 to 0.0625
- up_weight: bfloat16 [8192, 16384], P('row', 'col'), may hold values from -0.0625 to 0.0625
- down_weight: bfloat16 [16384, 8192], P('col', 'row'), may hold values from -0.046875 to 0.046875
- gate_mask: int32 [64, 128], P('row', 'col'), may hold values 0 or 1
- up_mask: int32 [64, 128], P('row', 'col'), may hold values 0 or 1
- down_mask: int32 [128, 64], P('col', 'row'), may hold values 0 or 1
- cotangent: bfloat16 [512, 8192], P('col', 'row'), may hold values from -4 to 4
Outputs:
- output: bfloat16 [512, 8192], P('col', 'row')
- input_grad: bfloat16 [512, 8192], P('col', 'row')
- gate_grad: bfloat16 [8192, 16384], P('row', 'col')
- up_grad: bfloat16 [8192, 16384], P('row', 'col')
- down_grad: bfloat16 [16384, 8192], P('col', 'row')
The draws below stay inside these ranges and needn't reach their ends.
Inputs may be any that keep to these rules, and one draw needn't show every extreme that they name: gate_mask is 1 where a 128 x 128 tile of gate_weight is kept and 0 where it is pruned. up_mask is 1 where a tile of up_weight is kept and 0 where it is pruned. down_mask is 1 where a tile of down_weight is kept and 0 where it is pruned.
All inputs are finite; a program needn't handle non-finite values. No bound on the sum of `gate_mask` or of `up_mask` or of `down_mask` on one device may be relied on, other than what follows from the above.
Results may differ from the reference program's by a relative error of at most 0.039.
Values may be sent and summed in bfloat16 or wider, within the bound.
No kernel may reach another device: no remote copies, remote signals or barrier semaphores. Data moves between devices by JAX's collectives and lax.ppermute only.
A program may use at most 64 MiB of HBM per device.

```python
import math
import jax
import jax.numpy as jnp
from jax import lax

D = 8192
FF = 16384
TILE = 128
TOKENS = 512
N_ROW = 16


def draw_tokens(key, part):
    position = jnp.arange(D, dtype=jnp.float32) / float(D - 1)
    channel_size = jnp.exp(math.log(4.0) * position)
    values = jnp.clip(jax.random.normal(key, (TOKENS, D), jnp.float32), -6.0, 6.0)
    return (values * channel_size[None, :]).astype(jnp.bfloat16)


def place_ends(entries, own_key, least, largest):
    longest = entries.shape.index(max(entries.shape))
    spots = []
    for shift in (0, 1):
        where = [jax.random.randint(jax.random.fold_in(own_key, axis), (), 0, length) for axis, length in enumerate(entries.shape)]
        where[longest] = (where[longest] + shift) % entries.shape[longest]
        spots.append(tuple(where))
    return entries.at[spots[0]].set(least).at[spots[1]].set(largest)


def shard_levels(own_key, extent, cuts, low, largest):
    def one(dim, parts):
        draws = jax.random.uniform(jax.random.fold_in(jax.random.fold_in(own_key, 6), dim), (parts,), jnp.float32, low / len(cuts), largest / len(cuts))
        return jnp.repeat(jnp.exp(draws), extent[dim] // parts).reshape((-1,) + (1,) * (len(extent) - dim - 1))

    level = one(*cuts[0])
    for cut in cuts[1:]:
        level = level * one(*cut)
    return level


def gaussian(key, shape, deviation, reach, shards=(), kind=jnp.bfloat16):
    values = jax.random.normal(key, shape, jnp.float32) * deviation
    if len(shards) > 0:
        values = shard_levels(key, shape, shards, -0.22, 0.18) * values
    return jnp.clip(values, min=-reach, max=reach).astype(kind)


def setup_inputs(seed: int = 0) -> dict:
    arg_keys = jax.random.split(jax.random.key(seed), 10)
    return {
        "tokens": draw_tokens(jax.random.fold_in(arg_keys[9], 71), 0),
        "scales": jnp.clip(jnp.exp(math.log(4.0) - 2.7725887 * jax.random.uniform(arg_keys[1], (D,), jnp.float32) ** shard_levels(arg_keys[1], (D,), ((0, 16),), -0.2, 0.2)), 0.25, 4.0),
        "gate_weight": gaussian(arg_keys[2], (D, FF), D ** -0.5, 0.0625, ((0, 16), (1, 32))),
        "up_weight": gaussian(arg_keys[3], (D, FF), D ** -0.5, 0.0625, ((0, 16), (1, 32))),
        "down_weight": gaussian(arg_keys[4], (FF, D), FF ** -0.5, 0.046875, ((0, 32), (1, 16))),
        "gate_mask": place_ends((jax.random.randint(arg_keys[5], (D // TILE, FF // TILE), 0, 2) < 1).astype(jnp.int32), jax.random.fold_in(arg_keys[5], 1), 0, 1),
        "up_mask": place_ends((jax.random.randint(arg_keys[6], (D // TILE, FF // TILE), 0, 2) < 1).astype(jnp.int32), jax.random.fold_in(arg_keys[6], 1), 0, 1),
        "down_mask": place_ends((jax.random.randint(arg_keys[7], (FF // TILE, D // TILE), 0, 2) < 1).astype(jnp.int32), jax.random.fold_in(arg_keys[7], 1), 0, 1),
        "cotangent": gaussian(arg_keys[8], (TOKENS, D), 0.25, 4.0, ((0, 32), (1, 16))),
    }


clip_ratio = 1.5

def expand(mask):
    return jnp.repeat(jnp.repeat(mask, TILE, axis=0), TILE, axis=1).astype(jnp.float32)

def row_blocks(left, right):
    block_width = D // N_ROW
    left_blocks = left.reshape(left.shape[0], N_ROW, block_width).transpose(1, 0, 2)
    right_blocks = right.reshape(N_ROW, block_width, right.shape[1])

    def add_block(running, blocks):
        rounded = jnp.dot(blocks[0], blocks[1], preferred_element_type=jnp.float32).astype(jnp.bfloat16)
        return (running + rounded.astype(jnp.float32), None)
    initial = jnp.zeros((left.shape[0], right.shape[1]), jnp.float32)
    total, unused = lax.scan(add_block, initial, (left_blocks, right_blocks))
    return total

def reference(tokens, scales, gate_weight, up_weight, down_weight, gate_mask, up_mask, down_mask, cotangent):
    smoothed = tokens.astype(jnp.float32) / scales
    mean_square = lax.optimization_barrier(jnp.mean(smoothed * smoothed, axis=1, keepdims=True))
    limits = clip_ratio * jnp.sqrt(mean_square + 1e-06)
    squashed = jnp.tanh(smoothed / limits)
    quantized = (limits * squashed).astype(jnp.bfloat16)
    gate_keep = expand(gate_mask)
    up_keep = expand(up_mask)
    down_keep = expand(down_mask)
    gate_kept = (scales[:, None] * gate_weight.astype(jnp.float32) * gate_keep).astype(jnp.bfloat16)
    up_kept = (scales[:, None] * up_weight.astype(jnp.float32) * up_keep).astype(jnp.bfloat16)
    down_kept = (down_weight.astype(jnp.float32) * down_keep).astype(jnp.bfloat16)
    both_kept = jnp.concatenate([gate_kept, up_kept], axis=1)
    gate_up = row_blocks(quantized, both_kept)
    gate_pre = gate_up[:, :FF]
    up_pre = gate_up[:, FF:]
    sigmoid_gate = jax.nn.sigmoid(gate_pre)
    silu_gate = gate_pre * sigmoid_gate
    hidden = (silu_gate * up_pre).astype(jnp.bfloat16)
    output = jnp.dot(hidden, down_kept, preferred_element_type=jnp.float32).astype(jnp.bfloat16)
    hidden_grad = row_blocks(cotangent, down_kept.T)
    gate_dir = (hidden_grad * up_pre * sigmoid_gate * (1.0 + gate_pre * (1.0 - sigmoid_gate))).astype(jnp.bfloat16)
    up_dir = (hidden_grad * silu_gate).astype(jnp.bfloat16)
    both_dirs = jnp.concatenate([gate_dir, up_dir], axis=1)
    quant_grad = jnp.dot(both_dirs, both_kept.T, preferred_element_type=jnp.float32)
    input_grad = (quant_grad * (1.0 - squashed * squashed) / scales).astype(jnp.bfloat16)
    gate_grad = (scales[:, None] * jnp.dot(quantized.T, gate_dir, preferred_element_type=jnp.float32) * gate_keep).astype(jnp.bfloat16)
    up_grad = (scales[:, None] * jnp.dot(quantized.T, up_dir, preferred_element_type=jnp.float32) * up_keep).astype(jnp.bfloat16)
    down_grad = (jnp.dot(hidden.T, cotangent, preferred_element_type=jnp.float32) * down_keep).astype(jnp.bfloat16)
    return (output, input_grad, gate_grad, up_grad, down_grad)
```

```python
import jax
import jax.numpy as jnp
from jax import lax
from jax.sharding import Mesh, PartitionSpec as P

D = 8192
TILE = 128
ROW = ("z", "core")
COL = ("x", "y")
N_Z, N_CORE, N_X, N_Y = 8, 2, 4, 8
N_ROW = N_Z * N_CORE
N_COL = N_X * N_Y


clip_ratio = 1.5


def expand(mask):
    return jnp.repeat(jnp.repeat(mask, TILE, axis=0), TILE, axis=1).astype(jnp.float32)


def matmul(left, right):
    return jnp.dot(left, right, preferred_element_type=jnp.float32)


def contract_last(left, right):
    return lax.dot_general(
        left, right, (((1,), (1,)), ((), ())), preferred_element_type=jnp.float32
    )


def contract_first(left, right):
    return lax.dot_general(
        left, right, (((0,), (0,)), ((), ())), preferred_element_type=jnp.float32
    )


def to_everyone(block, axis, size):
    copies = jnp.broadcast_to(block[None], (size,) + block.shape)
    return lax.all_to_all(copies, axis, 0, 0, tiled=True)


def exchange_sum(total, axis, size):
    rows = total.shape[0] // size
    parts = lax.all_to_all(
        total.reshape(size, rows, total.shape[1]), axis, 0, 0, tiled=True
    )
    return jnp.sum(parts.astype(jnp.float32), axis=0)


def swap_cores(block):
    return lax.ppermute(block, "core", [(0, 1), (1, 0)])


def half_of(block, which):
    rows = block.shape[0] // N_CORE
    return lax.dynamic_slice_in_dim(block, which * rows, rows, 0)


def join_halves(own, other, core):
    return jnp.where(
        core == 0,
        jnp.concatenate([own, other], axis=0),
        jnp.concatenate([other, own], axis=0),
    )


def per_device(
    tokens, scales, gate_weight, up_weight, down_weight, gate_mask, up_mask, down_mask, cotangent
):
    hidden_width = gate_weight.shape[1]
    width = tokens.shape[1]
    core = lax.axis_index("core")
    gate_keep = expand(gate_mask)
    up_keep = expand(up_mask)
    down_keep = expand(down_mask)
    gate_kept = (scales[:, None] * gate_weight.astype(jnp.float32) * gate_keep).astype(jnp.bfloat16)
    up_kept = (scales[:, None] * up_weight.astype(jnp.float32) * up_keep).astype(jnp.bfloat16)
    down_kept = down_weight * down_keep.astype(jnp.bfloat16)
    both_kept = jnp.concatenate([gate_kept, up_kept], axis=1)

    smoothed = tokens.astype(jnp.float32) / scales
    squares = to_everyone(jnp.sum(smoothed * smoothed, axis=1)[None], ROW, N_ROW)
    squares = jnp.sum(squares.reshape(N_ROW, -1), axis=0)
    limits = clip_ratio * jnp.sqrt(squares / D + 1e-06)[:, None]
    squashed = jnp.tanh(smoothed / limits)
    quantized = (limits * squashed).astype(jnp.bfloat16)

    both_in = jnp.concatenate([quantized, cotangent], axis=1)
    both_in = to_everyone(both_in, COL, N_COL).reshape(-1, 2 * width)

    def partial_sums(rows):
        gate_up = matmul(rows[:, :width], both_kept)
        hidden_grad = contract_last(rows[:, width:], down_kept)
        return jnp.concatenate([gate_up, hidden_grad], axis=1)

    theirs = swap_cores(partial_sums(half_of(both_in, 1 - core)).astype(jnp.bfloat16))
    own = partial_sums(half_of(both_in, core))
    pair_sum = (own + theirs.astype(jnp.float32)).astype(jnp.bfloat16)
    pre = exchange_sum(pair_sum, "z", N_Z)

    gate_pre = pre[:, :hidden_width]
    up_pre = pre[:, hidden_width : 2 * hidden_width]
    hidden_grad = pre[:, 2 * hidden_width :]
    sigmoid_gate = jax.nn.sigmoid(gate_pre)
    silu_gate = gate_pre * sigmoid_gate
    hidden = (silu_gate * up_pre).astype(jnp.bfloat16)
    gate_dir = (
        hidden_grad * up_pre * sigmoid_gate * (1.0 + gate_pre * (1.0 - sigmoid_gate))
    ).astype(jnp.bfloat16)
    up_dir = (hidden_grad * silu_gate).astype(jnp.bfloat16)
    mid = jnp.concatenate([gate_dir, up_dir, hidden], axis=1)

    own_mid = to_everyone(mid, "z", N_Z).reshape(-1, 3 * hidden_width)
    other_mid = swap_cores(own_mid)

    def back_sums(rows):
        output = matmul(rows[:, 2 * hidden_width :], down_kept)
        quant_grad = contract_last(rows[:, : 2 * hidden_width], both_kept)
        return jnp.concatenate([output, quant_grad], axis=1).astype(jnp.bfloat16)

    back = join_halves(back_sums(own_mid), back_sums(other_mid), core)
    back = exchange_sum(back, "x", N_X).astype(jnp.bfloat16)
    back = exchange_sum(back, "y", N_Y)
    output = back[:, :width].astype(jnp.bfloat16)
    input_grad = (back[:, width:] * (1.0 - squashed * squashed) / scales).astype(jnp.bfloat16)

    own_in = half_of(both_in, core)
    other_in = half_of(both_in, 1 - core)
    weight_product = contract_first(
        own_in[:, :width], own_mid[:, : 2 * hidden_width]
    ) + contract_first(other_in[:, :width], other_mid[:, : 2 * hidden_width])
    down_product = contract_first(own_mid[:, 2 * hidden_width :], own_in[:, width:]) + (
        contract_first(other_mid[:, 2 * hidden_width :], other_in[:, width:])
    )
    gate_grad = (scales[:, None] * weight_product[:, :hidden_width] * gate_keep).astype(
        jnp.bfloat16
    )
    up_grad = (scales[:, None] * weight_product[:, hidden_width:] * up_keep).astype(jnp.bfloat16)
    down_grad = (down_product * down_keep).astype(jnp.bfloat16)
    return (output, input_grad, gate_grad, up_grad, down_grad)


def solution(mesh):
    fine = Mesh(mesh.devices.reshape(N_Z, N_CORE, N_X, N_Y), ROW + COL)
    placed = (
        P(COL, ROW),
        P(ROW),
        P(ROW, COL),
        P(ROW, COL),
        P(COL, ROW),
        P(ROW, COL),
        P(ROW, COL),
        P(COL, ROW),
        P(COL, ROW),
    )
    return jax.shard_map(
        per_device,
        mesh=fine,
        in_specs=placed,
        out_specs=(
            P(COL, ROW),
            P(COL, ROW),
            P(ROW, COL),
            P(ROW, COL),
            P(COL, ROW),
        ),
        check_vma=False,
    )
```

```python
import jax
import jax.numpy as jnp
from jax import lax
from jax.experimental import pallas as pl
from jax.experimental.pallas import tpu as pltpu
from jax.sharding import Mesh, PartitionSpec as P

D = 8192
TILE = 128
ROW = ("z", "core")
COL = ("x", "y")
N_Z, N_CORE, N_X, N_Y = 8, 2, 4, 8
N_ROW = N_Z * N_CORE
N_COL = N_X * N_Y


clip_ratio = 1.5


def expand(mask):
    return jnp.repeat(jnp.repeat(mask, TILE, axis=0), TILE, axis=1).astype(jnp.float32)


def matmul(left, right):
    return jnp.dot(left, right, preferred_element_type=jnp.float32)


def contract_last(left, right):
    return lax.dot_general(
        left, right, (((1,), (1,)), ((), ())), preferred_element_type=jnp.float32
    )


def contract_first(left, right):
    return lax.dot_general(
        left, right, (((0,), (0,)), ((), ())), preferred_element_type=jnp.float32
    )


def swap_cores(block):
    return lax.ppermute(block, "core", [(0, 1), (1, 0)])


def exchange(parts, axis):
    return lax.all_to_all(parts, axis, 0, 0, tiled=True)


def add_parts(parts):
    total = parts[0].astype(jnp.float32)
    for i in range(1, parts.shape[0]):
        total = total + parts[i].astype(jnp.float32)
    return total


def local_kernel(body, outs, args, scalars=0, flops=0):
    moved = sum(a.size * a.dtype.itemsize for a in list(args) + list(outs))
    many = len(outs) > 1
    return pl.pallas_call(
        body,
        out_shape=outs if many else outs[0],
        in_specs=[pl.BlockSpec(memory_space=pltpu.SMEM)] * scalars
        + [pl.BlockSpec(memory_space=pltpu.VMEM)] * (len(args) - scalars),
        out_specs=[pl.BlockSpec(memory_space=pltpu.VMEM)] * len(outs)
        if many
        else pl.BlockSpec(memory_space=pltpu.VMEM),
        compiler_params=pltpu.CompilerParams(vmem_limit_bytes=24 << 20),
        cost_estimate=pl.CostEstimate(flops=flops, transcendentals=0, bytes_accessed=moved),
    )(*args)


def shape(dims, dtype):
    return jax.ShapeDtypeStruct(dims, dtype)


def squares_kernel(tokens, scales, copies):
    smoothed = tokens[...].astype(jnp.float32) / scales[...]
    squares = smoothed * smoothed
    lanes = copies.shape[2]
    total = squares[:, :lanes]
    for start in range(lanes, squares.shape[1], lanes):
        total = total + squares[:, start : start + lanes]
    for i in range(copies.shape[0]):
        copies[i] = total


def quantize_kernel(squares, tokens, scales, cotangent, copies, slope):
    width = tokens.shape[1]
    mean_square = jnp.sum(add_parts(squares), axis=1, keepdims=True) / D
    limits = clip_ratio * jnp.sqrt(mean_square + 1e-06)
    squashed = jnp.tanh(tokens[...].astype(jnp.float32) / scales[...] / limits)
    quantized = (limits * squashed).astype(jnp.bfloat16)
    slope[...] = (1.0 - squashed * squashed) / scales[...]
    for i in range(copies.shape[0]):
        copies[i, :, :width] = quantized
        copies[i, :, width:] = cotangent[...]


def forward_kernel(half, both_in, both_kept, down_kept, sums):
    rows = sums.shape[0]
    width = both_kept.shape[0]
    split = both_kept.shape[1]
    picked = pl.ds(pl.multiple_of(half[0] * rows, rows), rows)
    sums[:, :split] = matmul(both_in[picked, :width], both_kept[...]).astype(sums.dtype)
    sums[:, split:] = contract_last(both_in[picked, width:], down_kept[...]).astype(sums.dtype)


def pair_kernel(own, theirs, sums):
    sums[...] = (own[...] + theirs[...].astype(jnp.float32)).astype(sums.dtype)


def swiglu_kernel(parts, copies):
    pre = add_parts(parts)
    width = pre.shape[1] // 3
    gate_pre = pre[:, :width]
    up_pre = pre[:, width : 2 * width]
    hidden_grad = pre[:, 2 * width :]
    sigmoid_gate = 1.0 / (1.0 + jnp.exp(-gate_pre))
    silu_gate = gate_pre * sigmoid_gate
    gate_dir = hidden_grad * up_pre * sigmoid_gate * (1.0 + gate_pre * (1.0 - sigmoid_gate))
    up_dir = hidden_grad * silu_gate
    hidden = silu_gate * up_pre
    for k, value in enumerate((gate_dir, up_dir, hidden)):
        rounded = value.astype(copies.dtype)
        for i in range(copies.shape[0]):
            copies[i, :, k * width : (k + 1) * width] = rounded


def back_sums(mid, both_kept, down_kept, store):
    split = both_kept.shape[1]
    store(0, matmul(mid[:, split:], down_kept[...]))
    store(1, contract_last(mid[:, :split], both_kept[...]))


def own_back_kernel(mid, both_kept, down_kept, back):
    width = back.shape[1] // 2

    def store(k, value):
        back[:, k * width : (k + 1) * width] = value.astype(back.dtype)

    back_sums(mid, both_kept, down_kept, store)


def other_back_kernel(core, mid, own, both_kept, down_kept, back):
    rows = own.shape[0]
    width = back.shape[1] // 2
    own_rows = pl.ds(pl.multiple_of(core[0] * rows, rows), rows)
    other_rows = pl.ds(pl.multiple_of((1 - core[0]) * rows, rows), rows)
    back[own_rows, :] = own[...]

    def store(k, value):
        back[other_rows, k * width : (k + 1) * width] = value.astype(back.dtype)

    back_sums(mid, both_kept, down_kept, store)


def add_kernel(parts, total):
    total[...] = add_parts(parts).astype(total.dtype)


def finish_kernel(parts, slope, output, input_grad):
    total = add_parts(parts)
    width = output.shape[1]
    output[...] = total[:, :width].astype(output.dtype)
    input_grad[...] = (total[:, width:] * slope[...]).astype(input_grad.dtype)


def per_device(
    tokens, scales, gate_weight, up_weight, down_weight, gate_mask, up_mask, down_mask, cotangent
):
    hidden_width = gate_weight.shape[1]
    own_tokens, width = tokens.shape
    all_tokens = own_tokens * N_COL
    half_tokens = all_tokens // N_CORE
    mid_tokens = half_tokens // N_Z
    bf16, f32 = jnp.bfloat16, jnp.float32
    core = lax.axis_index("core").astype(jnp.int32).reshape(1)
    gate_keep = expand(gate_mask)
    up_keep = expand(up_mask)
    down_keep = expand(down_mask)
    gate_kept = (scales[:, None] * gate_weight.astype(jnp.float32) * gate_keep).astype(jnp.bfloat16)
    up_kept = (scales[:, None] * up_weight.astype(jnp.float32) * up_keep).astype(jnp.bfloat16)
    down_kept = down_weight * down_keep.astype(jnp.bfloat16)
    both_kept = jnp.concatenate([gate_kept, up_kept], axis=1)
    scale_row = scales[None, :]

    squares = local_kernel(
        squares_kernel, [shape((N_ROW, own_tokens, TILE), f32)], [tokens, scale_row]
    )
    squares = exchange(squares, ROW)
    copies, slope = local_kernel(
        quantize_kernel,
        [shape((N_Y, own_tokens, 2 * width), bf16), shape((own_tokens, width), f32)],
        [squares, tokens, scale_row, cotangent],
    )
    both_in = exchange(copies, "y").reshape(1, N_Y * own_tokens, 2 * width)
    both_in = exchange(jnp.broadcast_to(both_in, (N_X,) + both_in.shape[1:]), "x")
    both_in = both_in.reshape(all_tokens, 2 * width)

    flops = 6 * half_tokens * width * hidden_width
    theirs = local_kernel(
        forward_kernel,
        [shape((half_tokens, 3 * hidden_width), bf16)],
        [1 - core, both_in, both_kept, down_kept],
        1,
        flops,
    )
    theirs = swap_cores(theirs)
    own = local_kernel(
        forward_kernel,
        [shape((half_tokens, 3 * hidden_width), f32)],
        [core, both_in, both_kept, down_kept],
        1,
        flops,
    )
    pair_sum = local_kernel(
        pair_kernel, [shape((half_tokens, 3 * hidden_width), bf16)], [own, theirs]
    )
    parts = exchange(pair_sum.reshape(N_Z, mid_tokens, -1), "z")
    mid = local_kernel(swiglu_kernel, [shape(parts.shape, bf16)], [parts])
    own_mid = exchange(mid, "z").reshape(half_tokens, -1)
    other_mid = swap_cores(own_mid)
    own_back = local_kernel(
        own_back_kernel,
        [shape((half_tokens, 2 * width), bf16)],
        [own_mid, both_kept, down_kept],
        0,
        flops,
    )
    back = local_kernel(
        other_back_kernel,
        [shape((all_tokens, 2 * width), bf16)],
        [core, other_mid, own_back, both_kept, down_kept],
        1,
        flops,
    )
    back = exchange(back.reshape(N_X, all_tokens // N_X, -1), "x")
    back = local_kernel(add_kernel, [shape(back.shape[1:], bf16)], [back])
    back = exchange(back.reshape(N_Y, own_tokens, -1), "y")
    output, input_grad = local_kernel(
        finish_kernel, [shape((own_tokens, width), bf16)] * 2, [back, slope]
    )

    own_in = lax.dynamic_slice_in_dim(both_in, core[0] * half_tokens, half_tokens, 0)
    other_in = lax.dynamic_slice_in_dim(both_in, (1 - core[0]) * half_tokens, half_tokens, 0)
    weight_product = contract_first(
        own_in[:, :width], own_mid[:, : 2 * hidden_width]
    ) + contract_first(other_in[:, :width], other_mid[:, : 2 * hidden_width])
    down_product = contract_first(own_mid[:, 2 * hidden_width :], own_in[:, width:]) + (
        contract_first(other_mid[:, 2 * hidden_width :], other_in[:, width:])
    )
    gate_grad = (scales[:, None] * weight_product[:, :hidden_width] * gate_keep).astype(
        jnp.bfloat16
    )
    up_grad = (scales[:, None] * weight_product[:, hidden_width:] * up_keep).astype(jnp.bfloat16)
    down_grad = (down_product * down_keep).astype(jnp.bfloat16)
    return (output, input_grad, gate_grad, up_grad, down_grad)


def solution(mesh):
    fine = Mesh(mesh.devices.reshape(N_Z, N_CORE, N_X, N_Y), ROW + COL)
    placed = (
        P(COL, ROW),
        P(ROW),
        P(ROW, COL),
        P(ROW, COL),
        P(COL, ROW),
        P(ROW, COL),
        P(ROW, COL),
        P(COL, ROW),
        P(COL, ROW),
    )
    return jax.shard_map(
        per_device,
        mesh=fine,
        in_specs=placed,
        out_specs=(
            P(COL, ROW),
            P(COL, ROW),
            P(ROW, COL),
            P(ROW, COL),
            P(COL, ROW),
        ),
        check_vma=False,
    )
```

```python
import functools

import jax
import jax.numpy as jnp
from jax import lax
from jax.experimental import pallas as pl
from jax.experimental.pallas import tpu as pltpu
from jax.sharding import Mesh, PartitionSpec as P

D = 8192
TILE = 128
ROW = ("z", "core")
COL = ("x", "y")
N_Z, N_CORE, N_X, N_Y = 8, 2, 4, 8
N_ROW = N_Z * N_CORE
N_COL = N_X * N_Y


clip_ratio = 1.5


def matmul(left, right):
    return jnp.dot(left, right, preferred_element_type=jnp.float32)


def contract_last(left, right):
    return lax.dot_general(
        left, right, (((1,), (1,)), ((), ())), preferred_element_type=jnp.float32
    )


def contract_first(left, right):
    return lax.dot_general(
        left, right, (((0,), (0,)), ((), ())), preferred_element_type=jnp.float32
    )


def swap_cores(block):
    return lax.ppermute(block, "core", [(0, 1), (1, 0)])


def exchange(parts, axis):
    return lax.all_to_all(parts, axis, 0, 0, tiled=True)


def add_parts(parts):
    total = parts[0].astype(jnp.float32)
    for i in range(1, parts.shape[0]):
        total = total + parts[i].astype(jnp.float32)
    return total


def local_kernel(body, outs, args, scalars=0, flops=0, apart=(), stored=(), scratch=(), room=32):
    moved = sum(a.size * a.dtype.itemsize for a in list(args) + list(outs))
    spaces = [pltpu.SMEM if i < scalars else pltpu.VMEM for i in range(len(args))]
    for i in apart:
        spaces[i] = pl.ANY
    for i in stored:
        spaces[i] = pltpu.HBM
    specs = [pl.BlockSpec(memory_space=pltpu.VMEM)] * len(outs)
    return pl.pallas_call(
        body,
        out_shape=outs if len(outs) > 1 else outs[0],
        in_specs=[pl.BlockSpec(memory_space=space) for space in spaces],
        out_specs=specs if len(outs) > 1 else specs[0],
        scratch_shapes=list(scratch),
        compiler_params=pltpu.CompilerParams(vmem_limit_bytes=room << 20),
        cost_estimate=pl.CostEstimate(flops=flops, transcendentals=0, bytes_accessed=moved),
    )(*args)


def shape(dims, dtype):
    return jax.ShapeDtypeStruct(dims, dtype)


def squares_kernel(
    core, tokens, scales, cotangent, copies, smoothed, scales_here, cotangent_here, tokens_here, arrived
):
    del core
    moves = [
        pltpu.make_async_copy(tokens, tokens_here, arrived.at[0]),
        pltpu.make_async_copy(scales, scales_here, arrived.at[1]),
        pltpu.make_async_copy(cotangent, cotangent_here, arrived.at[2]),
    ]
    for move in moves:
        move.start()
    for move in moves:
        move.wait()
    value = tokens_here[...].astype(jnp.float32) / scales_here[...]
    smoothed[...] = value
    squares = value * value
    lanes = copies.shape[2]
    total = squares[:, :lanes]
    for start in range(lanes, squares.shape[1], lanes):
        total = total + squares[:, start : start + lanes]
    for i in range(copies.shape[0]):
        copies[i] = total


def prepare_kernel(
    gate_mask, up_mask, down_mask, scales, gate, up, down, both_kept, down_kept
):
    width = gate.shape[1]
    for i in range(gate.shape[0] // TILE):
        rows = slice(i * TILE, (i + 1) * TILE)
        scale = scales[rows, :]
        for j in range(width // TILE):
            columns = slice(j * TILE, (j + 1) * TILE)
            shifted = slice(width + j * TILE, width + (j + 1) * TILE)
            gate_keep = gate_mask[i, j].astype(jnp.float32)
            up_keep = up_mask[i, j].astype(jnp.float32)
            down_keep = down_mask[i, j].astype(jnp.float32)
            both_kept[rows, columns] = (
                scale * gate[rows, columns].astype(jnp.float32) * gate_keep
            ).astype(both_kept.dtype)
            both_kept[rows, shifted] = (
                scale * up[rows, columns].astype(jnp.float32) * up_keep
            ).astype(both_kept.dtype)
            down_kept[rows, columns] = (
                down[rows, columns].astype(jnp.float32) * down_keep
            ).astype(down_kept.dtype)


def quantize_kernel(squares, smoothed, scales, cotangent, both_kept, down_kept, copies, slope):
    del both_kept, down_kept
    width = smoothed.shape[1]
    mean_square = jnp.sum(add_parts(squares), axis=1, keepdims=True) / D
    limits = clip_ratio * jnp.sqrt(mean_square + 1e-06)
    squashed = jnp.tanh(smoothed[...] / limits)
    quantized = (limits * squashed).astype(jnp.bfloat16)
    slope[...] = (1.0 - squashed * squashed) / scales[...]
    for i in range(copies.shape[0]):
        copies[i, :, :width] = quantized
        copies[i, :, width:] = cotangent[...]


def forward_kernel(other, core, both_in, both_kept, down_kept, sums):
    rows = sums.shape[0]
    width = both_kept.shape[0]
    split = both_kept.shape[1]
    half = 1 - core[0] if other else core[0]
    picked = pl.ds(pl.multiple_of(half * rows, rows), rows)
    sums[:, :split] = matmul(both_in[picked, :width], both_kept[...]).astype(sums.dtype)
    sums[:, split:] = contract_last(both_in[picked, width:], down_kept[...]).astype(sums.dtype)


def pair_kernel(own, theirs, sums):
    sums[...] = (own[...] + theirs[...].astype(jnp.float32)).astype(sums.dtype)


def swiglu_kernel(parts, copies):
    pre = add_parts(parts)
    width = pre.shape[1] // 3
    gate_pre = pre[:, :width]
    up_pre = pre[:, width : 2 * width]
    hidden_grad = pre[:, 2 * width :]
    sigmoid_gate = 1.0 / (1.0 + jnp.exp(-gate_pre))
    silu_gate = gate_pre * sigmoid_gate
    gate_dir = hidden_grad * up_pre * sigmoid_gate * (1.0 + gate_pre * (1.0 - sigmoid_gate))
    up_dir = hidden_grad * silu_gate
    hidden = silu_gate * up_pre
    for k, value in enumerate((gate_dir, up_dir, hidden)):
        rounded = value.astype(copies.dtype)
        for i in range(copies.shape[0]):
            copies[i, :, k * width : (k + 1) * width] = rounded


def back_sums(mid, both_kept, down_kept, store):
    split = both_kept.shape[1]
    store(0, matmul(mid[:, split:], down_kept[...]))
    store(1, contract_last(mid[:, :split], both_kept[...]))


def own_back_kernel(mid, both_kept, down_kept, back):
    width = back.shape[1] // 2

    def store(k, value):
        back[:, k * width : (k + 1) * width] = value.astype(back.dtype)

    back_sums(mid, both_kept, down_kept, store)


def other_back_kernel(
    core,
    gate_mask,
    up_mask,
    down_mask,
    both_in,
    own_mid,
    other_mid,
    own,
    both_kept,
    down_kept,
    scales,
    back,
    gate_grad,
    up_grad,
    down_grad,
):
    rows = own.shape[0]
    width = back.shape[1] // 2
    split = both_kept.shape[1]
    own_rows = pl.ds(pl.multiple_of(core[0] * rows, rows), rows)
    other_rows = pl.ds(pl.multiple_of((1 - core[0]) * rows, rows), rows)
    back[own_rows, :] = own[...]

    def store(k, value):
        back[other_rows, k * width : (k + 1) * width] = value.astype(back.dtype)

    back_sums(other_mid, both_kept, down_kept, store)

    for i in range(width // TILE):
        block = slice(i * TILE, (i + 1) * TILE)
        product = contract_first(both_in[own_rows, block], own_mid[:, :split])
        product = product + contract_first(both_in[other_rows, block], other_mid[:, :split])
        for j in range(split // TILE):
            mask, grad = (gate_mask, gate_grad) if j < split // TILE // 2 else (up_mask, up_grad)
            column = j % (split // TILE // 2)
            tile = product[:, j * TILE : (j + 1) * TILE]
            keep = mask[i, column].astype(jnp.float32)
            grad[block, column * TILE : (column + 1) * TILE] = (
                scales[block, :] * tile * keep
            ).astype(grad.dtype)
    for i in range((other_mid.shape[1] - split) // TILE):
        units = slice(split + i * TILE, split + (i + 1) * TILE)
        product = contract_first(own_mid[:, units], both_in[own_rows, width:])
        product = product + contract_first(other_mid[:, units], both_in[other_rows, width:])
        for j in range(width // TILE):
            columns = slice(j * TILE, (j + 1) * TILE)
            keep = down_mask[i, j].astype(jnp.float32)
            down_grad[i * TILE : (i + 1) * TILE, columns] = (product[:, columns] * keep).astype(
                down_grad.dtype
            )


def finish_kernel(parts, slope, output, input_grad):
    total = add_parts(parts)
    width = output.shape[1]
    output[...] = total[:, :width].astype(output.dtype)
    input_grad[...] = (total[:, width:] * slope[...]).astype(input_grad.dtype)


def per_device(
    tokens, scales, gate_weight, up_weight, down_weight, gate_mask, up_mask, down_mask, cotangent
):
    hidden_width = gate_weight.shape[1]
    own_tokens, width = tokens.shape
    all_tokens = own_tokens * N_COL
    half_tokens = all_tokens // N_CORE
    mid_tokens = half_tokens // N_Z
    bf16, f32 = jnp.bfloat16, jnp.float32
    core = lax.axis_index("core").astype(jnp.int32).reshape(1)
    masks = [gate_mask, up_mask, down_mask]
    scale_lanes = jnp.broadcast_to(scales[:, None], (width, TILE))

    squares, smoothed, scales_here, cotangent_here = local_kernel(
        squares_kernel,
        [
            shape((N_ROW, own_tokens, TILE), f32),
            shape((own_tokens, width), f32),
            shape((1, width), f32),
            shape((own_tokens, width), bf16),
        ],
        [core, tokens, scales[None, :], cotangent],
        1,
        stored=(1, 2, 3),
        room=60,
        scratch=[pltpu.VMEM((own_tokens, width), bf16), pltpu.SemaphoreType.DMA((3,))],
    )
    squares = exchange(squares, ROW)
    both_kept, down_kept = local_kernel(
        prepare_kernel,
        [shape((width, 2 * hidden_width), bf16), shape((hidden_width, width), bf16)],
        masks + [scale_lanes, gate_weight, up_weight, down_weight],
        3,
    )
    copies, slope = local_kernel(
        quantize_kernel,
        [shape((N_COL, own_tokens, 2 * width), bf16), shape((own_tokens, width), f32)],
        [squares, smoothed, scales_here, cotangent_here, both_kept, down_kept],
        apart=(4, 5),
    )
    both_in = exchange(copies, COL).reshape(all_tokens, 2 * width)

    flops = 6 * half_tokens * width * hidden_width
    theirs = local_kernel(
        functools.partial(forward_kernel, True),
        [shape((half_tokens, 3 * hidden_width), bf16)],
        [core, both_in, both_kept, down_kept],
        1,
        flops,
    )
    theirs = swap_cores(theirs)
    own = local_kernel(
        functools.partial(forward_kernel, False),
        [shape((half_tokens, 3 * hidden_width), f32)],
        [core, both_in, both_kept, down_kept],
        1,
        flops,
    )
    pair_sum = local_kernel(
        pair_kernel, [shape((half_tokens, 3 * hidden_width), bf16)], [own, theirs]
    )
    parts = exchange(pair_sum.reshape(N_Z, mid_tokens, -1), "z")
    mid = local_kernel(swiglu_kernel, [shape(parts.shape, bf16)], [parts])
    own_mid = exchange(mid, "z").reshape(half_tokens, -1)
    other_mid = swap_cores(own_mid)
    own_back = local_kernel(
        own_back_kernel,
        [shape((half_tokens, 2 * width), bf16)],
        [own_mid, both_kept, down_kept],
        0,
        flops,
    )
    back, gate_grad, up_grad, down_grad = local_kernel(
        other_back_kernel,
        [
            shape((all_tokens, 2 * width), bf16),
            shape(gate_weight.shape, bf16),
            shape(up_weight.shape, bf16),
            shape(down_weight.shape, bf16),
        ],
        [core]
        + masks
        + [both_in, own_mid, other_mid, own_back, both_kept, down_kept, scale_lanes],
        4,
        4 * flops,
    )
    back = exchange(back.reshape(N_COL, own_tokens, -1), COL)
    output, input_grad = local_kernel(
        finish_kernel, [shape((own_tokens, width), bf16)] * 2, [back, slope]
    )
    return (output, input_grad, gate_grad, up_grad, down_grad)


def solution(mesh):
    fine = Mesh(mesh.devices.reshape(N_Z, N_CORE, N_X, N_Y), ROW + COL)
    placed = (
        P(COL, ROW),
        P(ROW),
        P(ROW, COL),
        P(ROW, COL),
        P(COL, ROW),
        P(ROW, COL),
        P(ROW, COL),
        P(COL, ROW),
        P(COL, ROW),
    )
    return jax.shard_map(
        per_device,
        mesh=fine,
        in_specs=placed,
        out_specs=(
            P(COL, ROW),
            P(COL, ROW),
            P(ROW, COL),
            P(ROW, COL),
            P(COL, ROW),
        ),
        check_vma=False,
    )
```

```python
import functools

import jax
import jax.numpy as jnp
from jax import lax
from jax.experimental import pallas as pl
from jax.experimental.pallas import tpu as pltpu
from jax.sharding import Mesh, PartitionSpec as P

D = 8192
TILE = 128
ROW = ("z", "core")
COL = ("x", "y")
N_Z, N_CORE, N_X, N_Y = 8, 2, 4, 8
N_ROW = N_Z * N_CORE
N_COL = N_X * N_Y


clip_ratio = 1.5


def matmul(left, right):
    return jnp.dot(left, right, preferred_element_type=jnp.float32)


def contract_last(left, right):
    return lax.dot_general(
        left, right, (((1,), (1,)), ((), ())), preferred_element_type=jnp.float32
    )


def contract_first(left, right):
    return lax.dot_general(
        left, right, (((0,), (0,)), ((), ())), preferred_element_type=jnp.float32
    )


def swap_cores(block):
    return lax.ppermute(block, "core", [(0, 1), (1, 0)])


def exchange(parts, axis):
    return lax.all_to_all(parts, axis, 0, 0, tiled=True)


def add_parts(parts):
    total = parts[0].astype(jnp.float32)
    for i in range(1, parts.shape[0]):
        total = total + parts[i].astype(jnp.float32)
    return total


def local_kernel(body, outs, args, scalars=0, flops=0, apart=(), stored=(), scratch=(), room=32):
    moved = sum(a.size * a.dtype.itemsize for a in list(args) + list(outs))
    spaces = [pltpu.SMEM if i < scalars else pltpu.VMEM for i in range(len(args))]
    for i in apart:
        spaces[i] = pl.ANY
    for i in stored:
        spaces[i] = pltpu.HBM
    specs = [pl.BlockSpec(memory_space=pltpu.VMEM)] * len(outs)
    return pl.pallas_call(
        body,
        out_shape=outs if len(outs) > 1 else outs[0],
        in_specs=[pl.BlockSpec(memory_space=space) for space in spaces],
        out_specs=specs if len(outs) > 1 else specs[0],
        scratch_shapes=list(scratch),
        compiler_params=pltpu.CompilerParams(vmem_limit_bytes=room << 20),
        cost_estimate=pl.CostEstimate(flops=flops, transcendentals=0, bytes_accessed=moved),
    )(*args)


def shape(dims, dtype):
    return jax.ShapeDtypeStruct(dims, dtype)


def squares_kernel(
    core, tokens, scales, cotangent, copies, smoothed, scales_here, cotangent_here, tokens_here, arrived
):
    del core
    moves = [
        pltpu.make_async_copy(tokens, tokens_here, arrived.at[0]),
        pltpu.make_async_copy(scales, scales_here, arrived.at[1]),
        pltpu.make_async_copy(cotangent, cotangent_here, arrived.at[2]),
    ]
    for move in moves:
        move.start()
    for move in moves:
        move.wait()
    value = tokens_here[...].astype(jnp.float32) / scales_here[...]
    smoothed[...] = value
    squares = value * value
    lanes = copies.shape[2]
    total = squares[:, :lanes]
    for start in range(lanes, squares.shape[1], lanes):
        total = total + squares[:, start : start + lanes]
    for i in range(copies.shape[0]):
        copies[i] = total


def prepare_kernel(
    gate_mask,
    up_mask,
    down_mask,
    scales,
    gate,
    up,
    down,
    both_kept,
    down_kept,
    ready,
    gate_keeps,
    up_keeps,
    down_keeps,
    gate_here,
    up_here,
    down_here,
    arrived,
):
    sources = (gate_mask, up_mask, down_mask, gate, up, down)
    places = (gate_keeps, up_keeps, down_keeps, gate_here, up_here, down_here)
    moves = [
        pltpu.make_async_copy(source, place, arrived.at[k])
        for k, (source, place) in enumerate(zip(sources, places))
    ]
    for move in moves:
        move.start()
    for move in moves[:4]:
        move.wait()
    width = gate.shape[1]
    count = gate.shape[0] // TILE
    tiles = [
        (i, j, slice(i * TILE, (i + 1) * TILE), slice(j * TILE, (j + 1) * TILE))
        for i in range(count)
        for j in range(width // TILE)
    ]
    for i, j, rows, columns in tiles:
        keep = gate_keeps[i, j].astype(jnp.float32)
        kept = scales[rows, :] * gate_here[rows, columns].astype(jnp.float32) * keep
        both_kept[rows, columns] = kept.astype(both_kept.dtype)
    moves[4].wait()
    for i, j, rows, columns in tiles:
        keep = up_keeps[i, j].astype(jnp.float32)
        kept = scales[rows, :] * up_here[rows, columns].astype(jnp.float32) * keep
        shifted = slice(width + columns.start, width + columns.stop)
        both_kept[rows, shifted] = kept.astype(both_kept.dtype)
    moves[5].wait()
    for i, j, rows, columns in tiles:
        keep = down_keeps[i, j].astype(jnp.float32)
        kept = down_here[rows, columns].astype(jnp.float32) * keep
        down_kept[rows, columns] = kept.astype(down_kept.dtype)
    ready[...] = scales[: ready.shape[0], :]


def quantize_kernel(squares, smoothed, scales, cotangent, ready, copies, slope):
    del ready
    width = smoothed.shape[1]
    mean_square = jnp.sum(add_parts(squares), axis=1, keepdims=True) / D
    limits = clip_ratio * jnp.sqrt(mean_square + 1e-06)
    squashed = jnp.tanh(smoothed[...] / limits)
    quantized = (limits * squashed).astype(jnp.bfloat16)
    slope[...] = (1.0 - squashed * squashed) / scales[...]
    for i in range(copies.shape[0]):
        copies[i, :, :width] = quantized
        copies[i, :, width:] = cotangent[...]


def copy_kernel(block, copies):
    for i in range(copies.shape[0]):
        copies[i] = block[0]


def forward_kernel(other, core, both_in, both_kept, down_kept, sums):
    rows = sums.shape[0]
    width = both_kept.shape[0]
    split = both_kept.shape[1]
    half = 1 - core[0] if other else core[0]
    picked = pl.ds(pl.multiple_of(half * rows, rows), rows)
    sums[:, :split] = matmul(both_in[picked, :width], both_kept[...]).astype(sums.dtype)
    sums[:, split:] = contract_last(both_in[picked, width:], down_kept[...]).astype(sums.dtype)


def pair_kernel(own, theirs, sums):
    sums[...] = (own[...] + theirs[...].astype(jnp.float32)).astype(sums.dtype)


def swiglu_kernel(parts, copies):
    pre = add_parts(parts)
    width = pre.shape[1] // 3
    gate_pre = pre[:, :width]
    up_pre = pre[:, width : 2 * width]
    hidden_grad = pre[:, 2 * width :]
    sigmoid_gate = 1.0 / (1.0 + jnp.exp(-gate_pre))
    silu_gate = gate_pre * sigmoid_gate
    gate_dir = hidden_grad * up_pre * sigmoid_gate * (1.0 + gate_pre * (1.0 - sigmoid_gate))
    up_dir = hidden_grad * silu_gate
    hidden = silu_gate * up_pre
    for k, value in enumerate((gate_dir, up_dir, hidden)):
        rounded = value.astype(copies.dtype)
        for i in range(copies.shape[0]):
            copies[i, :, k * width : (k + 1) * width] = rounded


def back_sums(mid, both_kept, down_kept, store):
    split = both_kept.shape[1]
    store(0, matmul(mid[:, split:], down_kept[...]))
    store(1, contract_last(mid[:, :split], both_kept[...]))


def own_back_kernel(mid, both_kept, down_kept, back):
    width = back.shape[1] // 2

    def store(k, value):
        back[:, k * width : (k + 1) * width] = value.astype(back.dtype)

    back_sums(mid, both_kept, down_kept, store)


def other_back_kernel(
    core,
    gate_mask,
    up_mask,
    down_mask,
    both_in,
    own_mid,
    other_mid,
    own,
    both_kept,
    down_kept,
    scales,
    back,
    gate_grad,
    up_grad,
    down_grad,
):
    rows = own.shape[0]
    width = back.shape[1] // 2
    split = both_kept.shape[1]
    own_rows = pl.ds(pl.multiple_of(core[0] * rows, rows), rows)
    other_rows = pl.ds(pl.multiple_of((1 - core[0]) * rows, rows), rows)
    back[own_rows, :] = own[...]

    def store(k, value):
        back[other_rows, k * width : (k + 1) * width] = value.astype(back.dtype)

    back_sums(other_mid, both_kept, down_kept, store)

    for i in range(width // TILE):
        block = slice(i * TILE, (i + 1) * TILE)
        product = contract_first(both_in[own_rows, block], own_mid[:, :split])
        product = product + contract_first(both_in[other_rows, block], other_mid[:, :split])
        for j in range(split // TILE):
            mask, grad = (gate_mask, gate_grad) if j < split // TILE // 2 else (up_mask, up_grad)
            column = j % (split // TILE // 2)
            tile = product[:, j * TILE : (j + 1) * TILE]
            keep = mask[i, column].astype(jnp.float32)
            grad[block, column * TILE : (column + 1) * TILE] = (
                scales[block, :] * tile * keep
            ).astype(grad.dtype)
    for i in range((other_mid.shape[1] - split) // TILE):
        units = slice(split + i * TILE, split + (i + 1) * TILE)
        product = contract_first(own_mid[:, units], both_in[own_rows, width:])
        product = product + contract_first(other_mid[:, units], both_in[other_rows, width:])
        for j in range(width // TILE):
            columns = slice(j * TILE, (j + 1) * TILE)
            keep = down_mask[i, j].astype(jnp.float32)
            down_grad[i * TILE : (i + 1) * TILE, columns] = (product[:, columns] * keep).astype(
                down_grad.dtype
            )


def add_kernel(parts, total):
    total[...] = add_parts(parts).astype(total.dtype)


def finish_kernel(parts, slope, output, input_grad):
    total = add_parts(parts)
    width = output.shape[1]
    output[...] = total[:, :width].astype(output.dtype)
    input_grad[...] = (total[:, width:] * slope[...]).astype(input_grad.dtype)


def per_device(
    tokens, scales, gate_weight, up_weight, down_weight, gate_mask, up_mask, down_mask, cotangent
):
    hidden_width = gate_weight.shape[1]
    own_tokens, width = tokens.shape
    all_tokens = own_tokens * N_COL
    half_tokens = all_tokens // N_CORE
    mid_tokens = half_tokens // N_Z
    bf16, f32 = jnp.bfloat16, jnp.float32
    core = lax.axis_index("core").astype(jnp.int32).reshape(1)
    masks = [gate_mask, up_mask, down_mask]
    scale_lanes = jnp.broadcast_to(scales[:, None], (width, TILE))

    squares, smoothed, scales_here, cotangent_here = local_kernel(
        squares_kernel,
        [
            shape((N_ROW, own_tokens, TILE), f32),
            shape((own_tokens, width), f32),
            shape((1, width), f32),
            shape((own_tokens, width), bf16),
        ],
        [core, tokens, scales[None, :], cotangent],
        1,
        stored=(1, 2, 3),
        room=60,
        scratch=[pltpu.VMEM((own_tokens, width), bf16), pltpu.SemaphoreType.DMA((3,))],
    )
    squares = exchange(squares, ROW)
    both_kept, down_kept, ready = local_kernel(
        prepare_kernel,
        [
            shape((width, 2 * hidden_width), bf16),
            shape((hidden_width, width), bf16),
            shape((8, TILE), f32),
        ],
        masks + [scale_lanes, gate_weight, up_weight, down_weight],
        stored=(0, 1, 2, 4, 5, 6),
        room=60,
        scratch=[pltpu.SMEM(mask.shape, mask.dtype) for mask in masks]
        + [pltpu.VMEM(w.shape, w.dtype) for w in (gate_weight, up_weight, down_weight)]
        + [pltpu.SemaphoreType.DMA((6,))],
    )
    copies, slope = local_kernel(
        quantize_kernel,
        [shape((N_Y, own_tokens, 2 * width), bf16), shape((own_tokens, width), f32)],
        [squares, smoothed, scales_here, cotangent_here, ready],
        apart=(4,),
    )
    gathered = exchange(copies, "y").reshape(1, N_Y * own_tokens, 2 * width)
    copies = local_kernel(copy_kernel, [shape((N_X,) + gathered.shape[1:], bf16)], [gathered])
    both_in = exchange(copies, "x").reshape(all_tokens, 2 * width)

    flops = 6 * half_tokens * width * hidden_width
    theirs = local_kernel(
        functools.partial(forward_kernel, True),
        [shape((half_tokens, 3 * hidden_width), bf16)],
        [core, both_in, both_kept, down_kept],
        1,
        flops,
    )
    theirs = swap_cores(theirs)
    own = local_kernel(
        functools.partial(forward_kernel, False),
        [shape((half_tokens, 3 * hidden_width), f32)],
        [core, both_in, both_kept, down_kept],
        1,
        flops,
    )
    pair_sum = local_kernel(
        pair_kernel, [shape((half_tokens, 3 * hidden_width), bf16)], [own, theirs]
    )
    parts = exchange(pair_sum.reshape(N_Z, mid_tokens, -1), "z")
    mid = local_kernel(swiglu_kernel, [shape(parts.shape, bf16)], [parts])
    own_mid = exchange(mid, "z").reshape(half_tokens, -1)
    other_mid = swap_cores(own_mid)
    own_back = local_kernel(
        own_back_kernel,
        [shape((half_tokens, 2 * width), bf16)],
        [own_mid, both_kept, down_kept],
        0,
        flops,
    )
    back, gate_grad, up_grad, down_grad = local_kernel(
        other_back_kernel,
        [
            shape((all_tokens, 2 * width), bf16),
            shape(gate_weight.shape, bf16),
            shape(up_weight.shape, bf16),
            shape(down_weight.shape, bf16),
        ],
        [core]
        + masks
        + [both_in, own_mid, other_mid, own_back, both_kept, down_kept, scale_lanes],
        4,
        4 * flops,
    )
    back = exchange(back.reshape(N_X, all_tokens // N_X, -1), "x")
    back = local_kernel(add_kernel, [shape(back.shape[1:], bf16)], [back])
    back = exchange(back.reshape(N_Y, own_tokens, -1), "y")
    output, input_grad = local_kernel(
        finish_kernel, [shape((own_tokens, width), bf16)] * 2, [back, slope]
    )
    return (output, input_grad, gate_grad, up_grad, down_grad)


def solution(mesh):
    fine = Mesh(mesh.devices.reshape(N_Z, N_CORE, N_X, N_Y), ROW + COL)
    placed = (
        P(COL, ROW),
        P(ROW),
        P(ROW, COL),
        P(ROW, COL),
        P(COL, ROW),
        P(ROW, COL),
        P(ROW, COL),
        P(COL, ROW),
        P(COL, ROW),
    )
    return jax.shard_map(
        per_device,
        mesh=fine,
        in_specs=placed,
        out_specs=(
            P(COL, ROW),
            P(COL, ROW),
            P(ROW, COL),
            P(ROW, COL),
            P(COL, ROW),
        ),
        check_vma=False,
    )
```

```python
import functools

import jax
import jax.numpy as jnp
from jax import lax
from jax.experimental import pallas as pl
from jax.experimental.pallas import tpu as pltpu
from jax.sharding import Mesh, PartitionSpec as P

D = 8192
TILE = 128
ROW = ("z", "core")
COL = ("x", "y")
N_Z, N_CORE, N_X, N_Y = 8, 2, 4, 8
N_ROW = N_Z * N_CORE
N_COL = N_X * N_Y
PLANE = ("core",) + COL
N_NEAR = 4
N_FAR = N_COL // N_NEAR


clip_ratio = 1.5


def matmul(left, right):
    return jnp.dot(left, right, preferred_element_type=jnp.float32)


def contract_last(left, right):
    return lax.dot_general(
        left, right, (((1,), (1,)), ((), ())), preferred_element_type=jnp.float32
    )


def contract_first(left, right):
    return lax.dot_general(
        left, right, (((0,), (0,)), ((), ())), preferred_element_type=jnp.float32
    )


def swap_cores(block):
    return lax.ppermute(block, "core", [(0, 1), (1, 0)])


def exchange(parts, axis):
    return lax.all_to_all(parts, axis, 0, 0, tiled=True)


def plane_place(core, x, y):
    return (core * N_X + x % N_X) * N_Y + y % N_Y


def near_groups():
    groups = []
    for core in range(N_CORE):
        for x in range(core, N_X + core, 2):
            for y in range(core, N_Y + core, 2):
                block = [(x + i, y + j) for i in range(2) for j in range(2)]
                block.sort(key=lambda at: (at[0] % 2, at[1] % 2))
                groups.append([plane_place(core, *at) for at in block])
    return groups


def far_groups():
    return [
        [
            plane_place(core, x, y)
            for x in range(x_parity, N_X, 2)
            for y in range(y_parity, N_Y, 2)
        ]
        for core in range(N_CORE)
        for x_parity in range(2)
        for y_parity in range(2)
    ]


def exchange_in(parts, groups):
    return lax.all_to_all(parts, PLANE, 0, 0, axis_index_groups=groups, tiled=True)


def add_parts(parts):
    total = parts[0].astype(jnp.float32)
    for i in range(1, parts.shape[0]):
        total = total + parts[i].astype(jnp.float32)
    return total


def local_kernel(body, outs, args, scalars=0, flops=0, apart=(), stored=(), scratch=(), room=32):
    moved = sum(a.size * a.dtype.itemsize for a in list(args) + list(outs))
    spaces = [pltpu.SMEM if i < scalars else pltpu.VMEM for i in range(len(args))]
    for i in apart:
        spaces[i] = pl.ANY
    for i in stored:
        spaces[i] = pltpu.HBM
    specs = [pl.BlockSpec(memory_space=pltpu.VMEM)] * len(outs)
    return pl.pallas_call(
        body,
        out_shape=outs if len(outs) > 1 else outs[0],
        in_specs=[pl.BlockSpec(memory_space=space) for space in spaces],
        out_specs=specs if len(outs) > 1 else specs[0],
        scratch_shapes=list(scratch),
        compiler_params=pltpu.CompilerParams(vmem_limit_bytes=room << 20),
        cost_estimate=pl.CostEstimate(flops=flops, transcendentals=0, bytes_accessed=moved),
    )(*args)


def shape(dims, dtype):
    return jax.ShapeDtypeStruct(dims, dtype)


def squares_kernel(
    core, tokens, scales, cotangent, copies, smoothed, scales_here, cotangent_here, tokens_here, arrived
):
    del core
    moves = [
        pltpu.make_async_copy(tokens, tokens_here, arrived.at[0]),
        pltpu.make_async_copy(scales, scales_here, arrived.at[1]),
        pltpu.make_async_copy(cotangent, cotangent_here, arrived.at[2]),
    ]
    for move in moves:
        move.start()
    for move in moves:
        move.wait()
    value = tokens_here[...].astype(jnp.float32) / scales_here[...]
    smoothed[...] = value
    squares = value * value
    lanes = copies.shape[2]
    total = squares[:, :lanes]
    for start in range(lanes, squares.shape[1], lanes):
        total = total + squares[:, start : start + lanes]
    for i in range(copies.shape[0]):
        copies[i] = total


def prepare_kernel(
    gate_mask,
    up_mask,
    down_mask,
    scales,
    gate,
    up,
    down,
    both_kept,
    down_kept,
    gate_keeps,
    up_keeps,
    down_keeps,
    gate_here,
    up_here,
    down_here,
    arrived,
):
    sources = (gate_mask, up_mask, down_mask, gate, up, down)
    places = (gate_keeps, up_keeps, down_keeps, gate_here, up_here, down_here)
    moves = [
        pltpu.make_async_copy(source, place, arrived.at[k])
        for k, (source, place) in enumerate(zip(sources, places))
    ]
    for move in moves:
        move.start()
    for move in moves[:4]:
        move.wait()
    width = gate.shape[1]
    count = gate.shape[0] // TILE
    tiles = [
        (i, j, slice(i * TILE, (i + 1) * TILE), slice(j * TILE, (j + 1) * TILE))
        for i in range(count)
        for j in range(width // TILE)
    ]
    for i, j, rows, columns in tiles:
        keep = gate_keeps[i, j].astype(jnp.float32)
        kept = scales[rows, :] * gate_here[rows, columns].astype(jnp.float32) * keep
        both_kept[rows, columns] = kept.astype(both_kept.dtype)
    moves[4].wait()
    for i, j, rows, columns in tiles:
        keep = up_keeps[i, j].astype(jnp.float32)
        kept = scales[rows, :] * up_here[rows, columns].astype(jnp.float32) * keep
        shifted = slice(width + columns.start, width + columns.stop)
        both_kept[rows, shifted] = kept.astype(both_kept.dtype)
    moves[5].wait()
    for i, j, rows, columns in tiles:
        keep = down_keeps[i, j].astype(jnp.float32)
        kept = down_here[rows, columns].astype(jnp.float32) * keep
        down_kept[rows, columns] = kept.astype(down_kept.dtype)


def quantize_kernel(squares, smoothed, scales, cotangent, copies, slope):
    width = smoothed.shape[1]
    mean_square = jnp.sum(add_parts(squares), axis=1, keepdims=True) / D
    limits = clip_ratio * jnp.sqrt(mean_square + 1e-06)
    squashed = jnp.tanh(smoothed[...] / limits)
    quantized = (limits * squashed).astype(jnp.bfloat16)
    slope[...] = (1.0 - squashed * squashed) / scales[...]
    for i in range(copies.shape[0]):
        copies[i, :, :width] = quantized
        copies[i, :, width:] = cotangent[...]


def copy_kernel(block, copies):
    for i in range(copies.shape[0]):
        copies[i] = block[0]


def forward_kernel(other, core, both_in, both_kept, down_kept, sums):
    rows = sums.shape[0]
    width = both_kept.shape[0]
    split = both_kept.shape[1]
    half = 1 - core[0] if other else core[0]
    picked = pl.ds(pl.multiple_of(half * rows, rows), rows)
    sums[:, :split] = matmul(both_in[picked, :width], both_kept[...]).astype(sums.dtype)
    sums[:, split:] = contract_last(both_in[picked, width:], down_kept[...]).astype(sums.dtype)


def pair_kernel(own, theirs, sums):
    sums[...] = (own[...] + theirs[...].astype(jnp.float32)).astype(sums.dtype)


def swiglu_kernel(parts, copies):
    pre = add_parts(parts)
    width = pre.shape[1] // 3
    gate_pre = pre[:, :width]
    up_pre = pre[:, width : 2 * width]
    hidden_grad = pre[:, 2 * width :]
    sigmoid_gate = 1.0 / (1.0 + jnp.exp(-gate_pre))
    silu_gate = gate_pre * sigmoid_gate
    gate_dir = hidden_grad * up_pre * sigmoid_gate * (1.0 + gate_pre * (1.0 - sigmoid_gate))
    up_dir = hidden_grad * silu_gate
    hidden = silu_gate * up_pre
    for k, value in enumerate((gate_dir, up_dir, hidden)):
        rounded = value.astype(copies.dtype)
        for i in range(copies.shape[0]):
            copies[i, :, k * width : (k + 1) * width] = rounded


def back_sums(mid, both_kept, down_kept, store):
    split = both_kept.shape[1]
    store(0, matmul(mid[:, split:], down_kept[...]))
    store(1, contract_last(mid[:, :split], both_kept[...]))


def own_back_kernel(mid, both_kept, down_kept, back):
    width = back.shape[1] // 2

    def store(k, value):
        back[:, k * width : (k + 1) * width] = value.astype(back.dtype)

    back_sums(mid, both_kept, down_kept, store)


def other_back_kernel(
    core,
    gate_mask,
    up_mask,
    down_mask,
    both_in,
    own_mid,
    other_mid,
    own,
    both_kept,
    down_kept,
    scales,
    back,
    gate_grad,
    up_grad,
    down_grad,
):
    rows = own.shape[0]
    width = back.shape[1] // 2
    split = both_kept.shape[1]
    own_rows = pl.ds(pl.multiple_of(core[0] * rows, rows), rows)
    other_rows = pl.ds(pl.multiple_of((1 - core[0]) * rows, rows), rows)
    back[own_rows, :] = own[...]

    def store(k, value):
        back[other_rows, k * width : (k + 1) * width] = value.astype(back.dtype)

    back_sums(other_mid, both_kept, down_kept, store)

    for i in range(width // TILE):
        block = slice(i * TILE, (i + 1) * TILE)
        product = contract_first(both_in[own_rows, block], own_mid[:, :split])
        product = product + contract_first(both_in[other_rows, block], other_mid[:, :split])
        for j in range(split // TILE):
            mask, grad = (gate_mask, gate_grad) if j < split // TILE // 2 else (up_mask, up_grad)
            column = j % (split // TILE // 2)
            tile = product[:, j * TILE : (j + 1) * TILE]
            keep = mask[i, column].astype(jnp.float32)
            grad[block, column * TILE : (column + 1) * TILE] = (
                scales[block, :] * tile * keep
            ).astype(grad.dtype)
    for i in range((other_mid.shape[1] - split) // TILE):
        units = slice(split + i * TILE, split + (i + 1) * TILE)
        product = contract_first(own_mid[:, units], both_in[own_rows, width:])
        product = product + contract_first(other_mid[:, units], both_in[other_rows, width:])
        for j in range(width // TILE):
            columns = slice(j * TILE, (j + 1) * TILE)
            keep = down_mask[i, j].astype(jnp.float32)
            down_grad[i * TILE : (i + 1) * TILE, columns] = (product[:, columns] * keep).astype(
                down_grad.dtype
            )


def add_kernel(parts, total):
    total[...] = add_parts(parts).astype(total.dtype)


def finish_kernel(parts, slope, output, input_grad):
    total = add_parts(parts)
    width = output.shape[1]
    output[...] = total[:, :width].astype(output.dtype)
    input_grad[...] = (total[:, width:] * slope[...]).astype(input_grad.dtype)


def per_device(
    tokens, scales, gate_weight, up_weight, down_weight, gate_mask, up_mask, down_mask, cotangent
):
    hidden_width = gate_weight.shape[1]
    own_tokens, width = tokens.shape
    all_tokens = own_tokens * N_COL
    half_tokens = all_tokens // N_CORE
    mid_tokens = half_tokens // N_Z
    bf16, f32 = jnp.bfloat16, jnp.float32
    core = lax.axis_index("core").astype(jnp.int32).reshape(1)
    masks = [gate_mask, up_mask, down_mask]
    scale_lanes = jnp.broadcast_to(scales[:, None], (width, TILE))

    squares, smoothed, scales_here, cotangent_here = local_kernel(
        squares_kernel,
        [
            shape((N_ROW, own_tokens, TILE), f32),
            shape((own_tokens, width), f32),
            shape((1, width), f32),
            shape((own_tokens, width), bf16),
        ],
        [core, tokens, scales[None, :], cotangent],
        1,
        stored=(1, 2, 3),
        room=60,
        scratch=[pltpu.VMEM((own_tokens, width), bf16), pltpu.SemaphoreType.DMA((3,))],
    )
    squares = exchange(squares, ROW)
    both_kept, down_kept = local_kernel(
        prepare_kernel,
        [
            shape((width, 2 * hidden_width), bf16),
            shape((hidden_width, width), bf16),
        ],
        masks + [scale_lanes, gate_weight, up_weight, down_weight],
        stored=(0, 1, 2, 4, 5, 6),
        room=60,
        scratch=[pltpu.SMEM(mask.shape, mask.dtype) for mask in masks]
        + [pltpu.VMEM(w.shape, w.dtype) for w in (gate_weight, up_weight, down_weight)]
        + [pltpu.SemaphoreType.DMA((6,))],
    )
    squares, both_kept, down_kept = lax.optimization_barrier((squares, both_kept, down_kept))
    copies, slope = local_kernel(
        quantize_kernel,
        [shape((N_FAR, own_tokens, 2 * width), bf16), shape((own_tokens, width), f32)],
        [squares, smoothed, scales_here, cotangent_here],
    )
    gathered = exchange_in(copies, far_groups()).reshape(1, N_FAR * own_tokens, 2 * width)
    copies = local_kernel(copy_kernel, [shape((N_NEAR,) + gathered.shape[1:], bf16)], [gathered])
    both_in = exchange_in(copies, near_groups()).reshape(all_tokens, 2 * width)

    flops = 6 * half_tokens * width * hidden_width
    theirs = local_kernel(
        functools.partial(forward_kernel, True),
        [shape((half_tokens, 3 * hidden_width), bf16)],
        [core, both_in, both_kept, down_kept],
        1,
        flops,
    )
    theirs = swap_cores(theirs)
    own = local_kernel(
        functools.partial(forward_kernel, False),
        [shape((half_tokens, 3 * hidden_width), f32)],
        [core, both_in, both_kept, down_kept],
        1,
        flops,
    )
    pair_sum = local_kernel(
        pair_kernel, [shape((half_tokens, 3 * hidden_width), bf16)], [own, theirs]
    )
    parts = exchange(pair_sum.reshape(N_Z, mid_tokens, -1), "z")
    mid = local_kernel(swiglu_kernel, [shape(parts.shape, bf16)], [parts])
    own_mid = exchange(mid, "z").reshape(half_tokens, -1)
    other_mid = swap_cores(own_mid)
    own_back = local_kernel(
        own_back_kernel,
        [shape((half_tokens, 2 * width), bf16)],
        [own_mid, both_kept, down_kept],
        0,
        flops,
    )
    back, gate_grad, up_grad, down_grad = local_kernel(
        other_back_kernel,
        [
            shape((all_tokens, 2 * width), bf16),
            shape(gate_weight.shape, bf16),
            shape(up_weight.shape, bf16),
            shape(down_weight.shape, bf16),
        ],
        [core]
        + masks
        + [both_in, own_mid, other_mid, own_back, both_kept, down_kept, scale_lanes],
        4,
        4 * flops,
    )
    back = exchange_in(back.reshape(N_NEAR, all_tokens // N_NEAR, -1), near_groups())
    back = local_kernel(add_kernel, [shape(back.shape[1:], bf16)], [back])
    back = exchange_in(back.reshape(N_FAR, own_tokens, -1), far_groups())
    output, input_grad = local_kernel(
        finish_kernel, [shape((own_tokens, width), bf16)] * 2, [back, slope]
    )
    return (output, input_grad, gate_grad, up_grad, down_grad)


def solution(mesh):
    fine = Mesh(mesh.devices.reshape(N_Z, N_CORE, N_X, N_Y), ROW + COL)
    placed = (
        P(COL, ROW),
        P(ROW),
        P(ROW, COL),
        P(ROW, COL),
        P(COL, ROW),
        P(ROW, COL),
        P(ROW, COL),
        P(COL, ROW),
        P(COL, ROW),
    )
    return jax.shard_map(
        per_device,
        mesh=fine,
        in_specs=placed,
        out_specs=(
            P(COL, ROW),
            P(COL, ROW),
            P(ROW, COL),
            P(ROW, COL),
            P(COL, ROW),
        ),
        check_vma=False,
    )
```

```python
import functools

import jax
import jax.numpy as jnp
from jax import lax
from jax.experimental import pallas as pl
from jax.experimental.pallas import tpu as pltpu
from jax.sharding import Mesh, PartitionSpec as P

D = 8192
TILE = 128
ROW = ("z", "core")
COL = ("x", "y")
N_Z, N_CORE, N_X, N_Y = 8, 2, 4, 8
N_ROW = N_Z * N_CORE
N_COL = N_X * N_Y
PLANE = ("core",) + COL
N_NEAR = 4
N_FAR = N_COL // N_NEAR


clip_ratio = 1.5


def matmul(left, right):
    return jnp.dot(left, right, preferred_element_type=jnp.float32)


def contract_last(left, right):
    return lax.dot_general(
        left, right, (((1,), (1,)), ((), ())), preferred_element_type=jnp.float32
    )


def contract_first(left, right):
    return lax.dot_general(
        left, right, (((0,), (0,)), ((), ())), preferred_element_type=jnp.float32
    )


def swap_cores(block):
    return lax.ppermute(block, "core", [(0, 1), (1, 0)])


def exchange(parts, axis):
    return lax.all_to_all(parts, axis, 0, 0, tiled=True)


def plane_place(core, x, y):
    return (core * N_X + x % N_X) * N_Y + y % N_Y


def near_groups():
    groups = []
    for core in range(N_CORE):
        for x in range(core, N_X + core, 2):
            for y in range(core, N_Y + core, 2):
                block = [(x + i, y + j) for i in range(2) for j in range(2)]
                block.sort(key=lambda at: (at[0] % 2, at[1] % 2))
                groups.append([plane_place(core, *at) for at in block])
    return groups


def far_groups():
    return [
        [
            plane_place(core, x, y)
            for core in range(N_CORE)
            for x in range(x_parity, N_X, 2)
            for y in range(y_parity, N_Y, 2)
        ]
        for x_parity in range(2)
        for y_parity in range(2)
    ]


def exchange_in(parts, groups):
    return lax.all_to_all(parts, PLANE, 0, 0, axis_index_groups=groups, tiled=True)


def add_parts(parts):
    total = parts[0].astype(jnp.float32)
    for i in range(1, parts.shape[0]):
        total = total + parts[i].astype(jnp.float32)
    return total


def local_kernel(body, outs, args, scalars=0, flops=0, apart=(), stored=(), scratch=(), room=32):
    moved = sum(a.size * a.dtype.itemsize for a in list(args) + list(outs))
    spaces = [pltpu.SMEM if i < scalars else pltpu.VMEM for i in range(len(args))]
    for i in apart:
        spaces[i] = pl.ANY
    for i in stored:
        spaces[i] = pltpu.HBM
    specs = [pl.BlockSpec(memory_space=pltpu.VMEM)] * len(outs)
    return pl.pallas_call(
        body,
        out_shape=outs if len(outs) > 1 else outs[0],
        in_specs=[pl.BlockSpec(memory_space=space) for space in spaces],
        out_specs=specs if len(outs) > 1 else specs[0],
        scratch_shapes=list(scratch),
        compiler_params=pltpu.CompilerParams(vmem_limit_bytes=room << 20),
        cost_estimate=pl.CostEstimate(flops=flops, transcendentals=0, bytes_accessed=moved),
    )(*args)


def shape(dims, dtype):
    return jax.ShapeDtypeStruct(dims, dtype)


def squares_kernel(
    core, tokens, scales, cotangent, copies, smoothed, scales_here, cotangent_here, tokens_here, arrived
):
    del core
    moves = [
        pltpu.make_async_copy(tokens, tokens_here, arrived.at[0]),
        pltpu.make_async_copy(scales, scales_here, arrived.at[1]),
        pltpu.make_async_copy(cotangent, cotangent_here, arrived.at[2]),
    ]
    for move in moves:
        move.start()
    for move in moves:
        move.wait()
    value = tokens_here[...].astype(jnp.float32) / scales_here[...]
    smoothed[...] = value
    squares = value * value
    lanes = copies.shape[2]
    total = squares[:, :lanes]
    for start in range(lanes, squares.shape[1], lanes):
        total = total + squares[:, start : start + lanes]
    for i in range(copies.shape[0]):
        copies[i] = total


def prepare_kernel(
    gate_mask,
    up_mask,
    down_mask,
    scales,
    gate,
    up,
    down,
    weights,
    scale_lanes,
    gate_keeps,
    up_keeps,
    down_keeps,
    scales_here,
    gate_here,
    up_here,
    down_here,
    arrived,
):
    sources = (gate_mask, up_mask, down_mask, scales, gate, up, down)
    places = (gate_keeps, up_keeps, down_keeps, scales_here, gate_here, up_here, down_here)
    moves = [
        pltpu.make_async_copy(source, place, arrived.at[k])
        for k, (source, place) in enumerate(zip(sources, places))
    ]
    for move in moves:
        move.start()
    for move in moves[:5]:
        move.wait()
    width = gate.shape[1]
    count = gate.shape[0] // TILE
    for i in range(count):
        block = slice(i * TILE, (i + 1) * TILE)
        scale_lanes[block, :] = jnp.broadcast_to(scales_here[:, block], (TILE, TILE)).T
    tiles = [
        (i, j, slice(i * TILE, (i + 1) * TILE), slice(j * TILE, (j + 1) * TILE))
        for i in range(count)
        for j in range(width // TILE)
    ]
    for i, j, rows, columns in tiles:
        keep = gate_keeps[i, j].astype(jnp.float32)
        kept = scale_lanes[rows, :] * gate_here[rows, columns].astype(jnp.float32) * keep
        weights[rows, columns] = kept.astype(weights.dtype)
    moves[5].wait()
    for i, j, rows, columns in tiles:
        keep = up_keeps[i, j].astype(jnp.float32)
        kept = scale_lanes[rows, :] * up_here[rows, columns].astype(jnp.float32) * keep
        shifted = slice(width + columns.start, width + columns.stop)
        weights[rows, shifted] = kept.astype(weights.dtype)
    moves[6].wait()
    for i, j, rows, columns in tiles:
        keep = down_keeps[i, j].astype(jnp.float32)
        kept = down_here[rows, columns].astype(jnp.float32) * keep
        shifted = slice(2 * width + columns.start, 2 * width + columns.stop)
        weights[rows, shifted] = kept.astype(weights.dtype)


def quantize_kernel(squares, smoothed, scales, cotangent, copies, slope):
    rows, width = copies.shape[1], smoothed.shape[1]
    mean_square = jnp.sum(add_parts(squares), axis=1, keepdims=True) / D
    limits = clip_ratio * jnp.sqrt(mean_square + 1e-06)
    squashed = jnp.tanh(smoothed[...] / limits)
    quantized = limits * squashed
    slope[...] = (1.0 - squashed * squashed) / scales[...]
    gradient = cotangent[...].astype(jnp.float32)
    for core in range(N_CORE):
        own = slice(core * rows, (core + 1) * rows)
        quantized_half = quantized[own].astype(copies.dtype)
        gradient_half = gradient[own].astype(copies.dtype)
        for i in range(N_FAR):
            copies[core * N_FAR + i, :, :width] = quantized_half
            copies[core * N_FAR + i, :, width:] = gradient_half


def copy_kernel(blocks, copies):
    width = blocks.shape[2]
    for i in range(copies.shape[0]):
        for core in range(blocks.shape[0]):
            copies[i, :, core * width : (core + 1) * width] = blocks[core]


def lanes_of(core, start, width, count=1):
    return pl.ds(pl.multiple_of(core * 2 * width + start, TILE), count * width)


def forward_kernel(core, both_in, own_weights, other_weights, sums):
    width = own_weights.shape[0]
    split = sums.shape[1] - width
    gate_up = None
    for place, weights in ((core[0], own_weights), (1 - core[0], other_weights)):
        quantized = both_in[:, lanes_of(place, 0, width)]
        gradient = both_in[:, lanes_of(place, width, width)]
        first = matmul(quantized, weights[:, :split])
        second = contract_last(gradient, weights[:, split:])
        if gate_up is None:
            gate_up, hidden_grad = first, second
        else:
            gate_up, hidden_grad = gate_up + first, hidden_grad + second
    sums[:, :split] = gate_up.astype(sums.dtype)
    sums[:, split:] = hidden_grad.astype(sums.dtype)


def swiglu_kernel(parts, copies):
    pre = add_parts(parts)
    width = pre.shape[1] // 3
    gate_pre = pre[:, :width]
    up_pre = pre[:, width : 2 * width]
    hidden_grad = pre[:, 2 * width :]
    sigmoid_gate = 1.0 / (1.0 + jnp.exp(-gate_pre))
    silu_gate = gate_pre * sigmoid_gate
    gate_dir = hidden_grad * up_pre * sigmoid_gate * (1.0 + gate_pre * (1.0 - sigmoid_gate))
    up_dir = hidden_grad * silu_gate
    hidden = silu_gate * up_pre
    for k, value in enumerate((gate_dir, up_dir, hidden)):
        rounded = value.astype(copies.dtype)
        for i in range(copies.shape[0]):
            copies[i, :, k * width : (k + 1) * width] = rounded


def back_kernel(core, both_in, mid, own_weights, other_weights, back, parcel):
    width = own_weights.shape[0]
    split = mid.shape[1] - width
    parcel[:, : 2 * width] = both_in[:, lanes_of(1 - core[0], 0, width, 2)]
    parcel[:, 2 * width :] = mid[...]
    for place, weights in ((core[0], own_weights), (1 - core[0], other_weights)):
        output = matmul(mid[:, split:], weights[:, split:])
        back[:, lanes_of(place, 0, width)] = output.astype(back.dtype)
        quant_grad = contract_last(mid[:, :split], weights[:, :split])
        back[:, lanes_of(place, width, width)] = quant_grad.astype(back.dtype)


def weight_grads_kernel(
    core,
    gate_mask,
    up_mask,
    down_mask,
    both_in,
    mid,
    parcel,
    scales,
    gate_grad,
    up_grad,
    down_grad,
):
    width = gate_grad.shape[0]
    split = mid.shape[1] - width
    own_quantized = both_in[:, lanes_of(core[0], 0, width)]
    own_gradient = both_in[:, lanes_of(core[0], width, width)]
    start = 2 * width
    for i in range(width // TILE):
        block = slice(i * TILE, (i + 1) * TILE)
        product = contract_first(own_quantized[:, block], mid[:, :split])
        product = product + contract_first(parcel[:, block], parcel[:, start : start + split])
        for j in range(split // TILE):
            mask, grad = (gate_mask, gate_grad) if j < split // TILE // 2 else (up_mask, up_grad)
            column = j % (split // TILE // 2)
            tile = product[:, j * TILE : (j + 1) * TILE]
            keep = mask[i, column].astype(jnp.float32)
            grad[block, column * TILE : (column + 1) * TILE] = (
                scales[block, :] * tile * keep
            ).astype(grad.dtype)
    for i in range(down_grad.shape[0] // TILE):
        units = slice(split + i * TILE, split + (i + 1) * TILE)
        others = slice(start + units.start, start + units.stop)
        product = contract_first(mid[:, units], own_gradient)
        product = product + contract_first(parcel[:, others], parcel[:, width:start])
        for j in range(width // TILE):
            columns = slice(j * TILE, (j + 1) * TILE)
            keep = down_mask[i, j].astype(jnp.float32)
            down_grad[i * TILE : (i + 1) * TILE, columns] = (product[:, columns] * keep).astype(
                down_grad.dtype
            )


def add_kernel(parts, totals):
    total = add_parts(parts).astype(totals.dtype)
    width = totals.shape[2]
    for core in range(totals.shape[0]):
        totals[core] = total[:, core * width : (core + 1) * width]


def finish_kernel(parts, slope, output, input_grad):
    total = jnp.concatenate([add_parts(parts[:N_FAR]), add_parts(parts[N_FAR:])], axis=0)
    width = output.shape[1]
    output[...] = total[:, :width].astype(output.dtype)
    input_grad[...] = (total[:, width:] * slope[...]).astype(input_grad.dtype)


def per_device(
    tokens, scales, gate_weight, up_weight, down_weight, gate_mask, up_mask, down_mask, cotangent
):
    hidden_width = gate_weight.shape[1]
    own_tokens, width = tokens.shape
    all_tokens = own_tokens * N_COL
    half_tokens = all_tokens // N_CORE
    mid_tokens = half_tokens // N_Z
    bf16, f32 = jnp.bfloat16, jnp.float32
    core = lax.axis_index("core").astype(jnp.int32).reshape(1)
    masks = [gate_mask, up_mask, down_mask]

    squares, smoothed, scales_here, cotangent_here = local_kernel(
        squares_kernel,
        [
            shape((N_ROW, own_tokens, TILE), f32),
            shape((own_tokens, width), f32),
            shape((1, width), f32),
            shape((own_tokens, width), bf16),
        ],
        [core, tokens, scales[None, :], cotangent],
        1,
        stored=(1, 2, 3),
        room=60,
        scratch=[pltpu.VMEM((own_tokens, width), bf16), pltpu.SemaphoreType.DMA((3,))],
    )
    squares = exchange(squares, ROW)
    weights = (gate_weight, up_weight, down_weight)
    own_weights, scale_lanes = local_kernel(
        prepare_kernel,
        [shape((width, 3 * hidden_width), bf16), shape((width, TILE), f32)],
        masks + [scales_here] + list(weights),
        stored=range(7),
        room=60,
        scratch=[pltpu.SMEM(mask.shape, mask.dtype) for mask in masks]
        + [pltpu.VMEM((1, width), f32)]
        + [pltpu.VMEM(w.shape, w.dtype) for w in weights]
        + [pltpu.SemaphoreType.DMA((7,))],
    )
    squares, own_weights = lax.optimization_barrier((squares, own_weights))
    other_weights = swap_cores(own_weights)
    copies, slope = local_kernel(
        quantize_kernel,
        [
            shape((N_CORE * N_FAR, own_tokens // N_CORE, 2 * width), bf16),
            shape((own_tokens, width), f32),
        ],
        [squares, smoothed, scales_here, cotangent_here],
    )
    gathered = exchange_in(copies, far_groups())
    gathered, other_weights = lax.optimization_barrier((gathered, other_weights))
    gathered = gathered.reshape(N_CORE, half_tokens // N_NEAR, 2 * width)
    copies = local_kernel(
        copy_kernel, [shape((N_NEAR, half_tokens // N_NEAR, 4 * width), bf16)], [gathered]
    )
    both_in = exchange_in(copies, near_groups()).reshape(half_tokens, 4 * width)

    flops = 12 * half_tokens * width * hidden_width
    sums = local_kernel(
        forward_kernel,
        [shape((half_tokens, 3 * hidden_width), bf16)],
        [core, both_in, own_weights, other_weights],
        1,
        flops,
    )
    parts = exchange(sums.reshape(N_Z, mid_tokens, -1), "z")
    mid = local_kernel(swiglu_kernel, [shape(parts.shape, bf16)], [parts])
    mid = exchange(mid, "z").reshape(half_tokens, -1)
    back, parcel = local_kernel(
        back_kernel,
        [
            shape((half_tokens, 4 * width), bf16),
            shape((half_tokens, 2 * width + 3 * hidden_width), bf16),
        ],
        [core, both_in, mid, own_weights, other_weights],
        1,
        flops,
    )
    back = exchange_in(back.reshape(N_NEAR, half_tokens // N_NEAR, -1), near_groups())
    back, parcel = lax.optimization_barrier((back, parcel))
    parcel = swap_cores(parcel)
    back = local_kernel(
        add_kernel, [shape((N_CORE, half_tokens // N_NEAR, 2 * width), bf16)], [back]
    )
    back = exchange_in(back.reshape(N_CORE * N_FAR, -1, 2 * width), far_groups())
    gate_grad, up_grad, down_grad = local_kernel(
        weight_grads_kernel,
        [shape(w.shape, bf16) for w in weights],
        [core] + masks + [both_in, mid, parcel, scale_lanes],
        4,
        flops,
    )
    output, input_grad = local_kernel(
        finish_kernel, [shape((own_tokens, width), bf16)] * 2, [back, slope]
    )
    return (output, input_grad, gate_grad, up_grad, down_grad)


def solution(mesh):
    fine = Mesh(mesh.devices.reshape(N_Z, N_CORE, N_X, N_Y), ROW + COL)
    placed = (
        P(COL, ROW),
        P(ROW),
        P(ROW, COL),
        P(ROW, COL),
        P(COL, ROW),
        P(ROW, COL),
        P(ROW, COL),
        P(COL, ROW),
        P(COL, ROW),
    )
    return jax.shard_map(
        per_device,
        mesh=fine,
        in_specs=placed,
        out_specs=(
            P(COL, ROW),
            P(COL, ROW),
            P(ROW, COL),
            P(ROW, COL),
            P(COL, ROW),
        ),
        check_vma=False,
    )
```

```python
import functools

import jax
import jax.numpy as jnp
from jax import lax
from jax.experimental import pallas as pl
from jax.experimental.pallas import tpu as pltpu
from jax.sharding import Mesh, PartitionSpec as P

D = 8192
TILE = 128
ROW = ("z", "core")
COL = ("x", "y")
N_Z, N_CORE, N_X, N_Y = 8, 2, 4, 8
N_ROW = N_Z * N_CORE
N_COL = N_X * N_Y
PLANE = ("core",) + COL
N_NEAR = 4
N_FAR = N_COL // N_NEAR


clip_ratio = 1.5


def matmul(left, right):
    return jnp.dot(left, right, preferred_element_type=jnp.float32)


def contract_last(left, right):
    return lax.dot_general(
        left, right, (((1,), (1,)), ((), ())), preferred_element_type=jnp.float32
    )


def contract_first(left, right):
    return lax.dot_general(
        left, right, (((0,), (0,)), ((), ())), preferred_element_type=jnp.float32
    )


def swap_cores(block):
    return lax.ppermute(block, "core", [(0, 1), (1, 0)])


def exchange(parts, axis):
    return lax.all_to_all(parts, axis, 0, 0, tiled=True)


def plane_place(core, x, y):
    return (core * N_X + x % N_X) * N_Y + y % N_Y


def near_groups():
    groups = []
    for core in range(N_CORE):
        for x in range(core, N_X + core, 2):
            for y in range(core, N_Y + core, 2):
                block = [(x + i, y + j) for i in range(2) for j in range(2)]
                block.sort(key=lambda at: (at[0] % 2, at[1] % 2))
                groups.append([plane_place(core, *at) for at in block])
    return groups


def far_groups():
    return [
        [
            plane_place(core, x, y)
            for core in range(N_CORE)
            for x in range(x_parity, N_X, 2)
            for y in range(y_parity, N_Y, 2)
        ]
        for x_parity in range(2)
        for y_parity in range(2)
    ]


def exchange_in(parts, groups):
    return lax.all_to_all(parts, PLANE, 0, 0, axis_index_groups=groups, tiled=True)


def add_parts(parts):
    total = parts[0].astype(jnp.float32)
    for i in range(1, parts.shape[0]):
        total = total + parts[i].astype(jnp.float32)
    return total


def local_kernel(body, outs, args, scalars=0, flops=0, apart=(), stored=(), scratch=(), room=32):
    moved = sum(a.size * a.dtype.itemsize for a in list(args) + list(outs))
    spaces = [pltpu.SMEM if i < scalars else pltpu.VMEM for i in range(len(args))]
    for i in apart:
        spaces[i] = pl.ANY
    for i in stored:
        spaces[i] = pltpu.HBM
    specs = [pl.BlockSpec(memory_space=pltpu.VMEM)] * len(outs)
    return pl.pallas_call(
        body,
        out_shape=outs if len(outs) > 1 else outs[0],
        in_specs=[pl.BlockSpec(memory_space=space) for space in spaces],
        out_specs=specs if len(outs) > 1 else specs[0],
        scratch_shapes=list(scratch),
        compiler_params=pltpu.CompilerParams(vmem_limit_bytes=room << 20),
        cost_estimate=pl.CostEstimate(flops=flops, transcendentals=0, bytes_accessed=moved),
    )(*args)


def shape(dims, dtype):
    return jax.ShapeDtypeStruct(dims, dtype)


def squares_kernel(
    core, tokens, scales, cotangent, copies, smoothed, scales_here, cotangent_here, tokens_here, arrived
):
    del core
    moves = [
        pltpu.make_async_copy(tokens, tokens_here, arrived.at[0]),
        pltpu.make_async_copy(scales, scales_here, arrived.at[1]),
        pltpu.make_async_copy(cotangent, cotangent_here, arrived.at[2]),
    ]
    for move in moves:
        move.start()
    for move in moves:
        move.wait()
    value = tokens_here[...].astype(jnp.float32) / scales_here[...]
    smoothed[...] = value
    squares = value * value
    lanes = copies.shape[2]
    total = squares[:, :lanes]
    for start in range(lanes, squares.shape[1], lanes):
        total = total + squares[:, start : start + lanes]
    for i in range(copies.shape[0]):
        copies[i] = total


def prepare_kernel(
    gate_mask,
    up_mask,
    down_mask,
    scales,
    gate,
    up,
    down,
    weights,
    scale_lanes,
    gate_keeps,
    up_keeps,
    down_keeps,
    scales_here,
    gate_here,
    up_here,
    down_here,
    arrived,
):
    sources = (gate_mask, up_mask, down_mask, scales, gate, up, down)
    places = (gate_keeps, up_keeps, down_keeps, scales_here, gate_here, up_here, down_here)
    moves = [
        pltpu.make_async_copy(source, place, arrived.at[k])
        for k, (source, place) in enumerate(zip(sources, places))
    ]
    for move in moves:
        move.start()
    for move in moves[:5]:
        move.wait()
    width = gate.shape[1]
    count = gate.shape[0] // TILE
    for i in range(count):
        block = slice(i * TILE, (i + 1) * TILE)
        scale_lanes[block, :] = jnp.broadcast_to(scales_here[:, block], (TILE, TILE)).T
    tiles = [
        (i, j, slice(i * TILE, (i + 1) * TILE), slice(j * TILE, (j + 1) * TILE))
        for i in range(count)
        for j in range(width // TILE)
    ]
    for i, j, rows, columns in tiles:
        keep = gate_keeps[i, j].astype(jnp.float32)
        kept = scale_lanes[rows, :] * gate_here[rows, columns].astype(jnp.float32) * keep
        weights[rows, columns] = kept.astype(weights.dtype)
    moves[5].wait()
    for i, j, rows, columns in tiles:
        keep = up_keeps[i, j].astype(jnp.float32)
        kept = scale_lanes[rows, :] * up_here[rows, columns].astype(jnp.float32) * keep
        shifted = slice(width + columns.start, width + columns.stop)
        weights[rows, shifted] = kept.astype(weights.dtype)
    moves[6].wait()
    for i, j, rows, columns in tiles:
        keep = down_keeps[i, j].astype(jnp.float32)
        kept = down_here[rows, columns].astype(jnp.float32) * keep
        shifted = slice(2 * width + columns.start, 2 * width + columns.stop)
        weights[rows, shifted] = kept.astype(weights.dtype)


def quantize_kernel(squares, smoothed, scales, cotangent, copies, slope):
    rows, width = copies.shape[1], smoothed.shape[1]
    mean_square = jnp.sum(add_parts(squares), axis=1, keepdims=True) / D
    limits = clip_ratio * jnp.sqrt(mean_square + 1e-06)
    squashed = jnp.tanh(smoothed[...] / limits)
    quantized = limits * squashed
    slope[...] = (1.0 - squashed * squashed) / scales[...]
    gradient = cotangent[...].astype(jnp.float32)
    for core in range(N_CORE):
        own = slice(core * rows, (core + 1) * rows)
        quantized_half = quantized[own].astype(copies.dtype)
        gradient_half = gradient[own].astype(copies.dtype)
        for i in range(N_FAR):
            copies[core * N_FAR + i, :, :width] = quantized_half
            copies[core * N_FAR + i, :, width:] = gradient_half


def copy_kernel(blocks, copies):
    width = blocks.shape[2]
    for i in range(copies.shape[0]):
        for core in range(blocks.shape[0]):
            copies[i, :, core * width : (core + 1) * width] = blocks[core]


def lanes_of(core, start, width, count=1):
    return pl.ds(pl.multiple_of(core * 2 * width + start, TILE), count * width)


def forward_kernel(core, both_in, own_weights, other_weights, sums):
    width = own_weights.shape[0]
    split = sums.shape[1] - width
    gate_up = None
    for place, weights in ((core[0], own_weights), (1 - core[0], other_weights)):
        quantized = both_in[:, lanes_of(place, 0, width)]
        gradient = both_in[:, lanes_of(place, width, width)]
        first = matmul(quantized, weights[:, :split])
        second = contract_last(gradient, weights[:, split:])
        if gate_up is None:
            gate_up, hidden_grad = first, second
        else:
            gate_up, hidden_grad = gate_up + first, hidden_grad + second
    sums[:, :split] = gate_up.astype(sums.dtype)
    sums[:, split:] = hidden_grad.astype(sums.dtype)


def swiglu_kernel(parts, copies):
    pre = add_parts(parts)
    width = pre.shape[1] // 3
    gate_pre = pre[:, :width]
    up_pre = pre[:, width : 2 * width]
    hidden_grad = pre[:, 2 * width :]
    sigmoid_gate = 1.0 / (1.0 + jnp.exp(-gate_pre))
    silu_gate = gate_pre * sigmoid_gate
    gate_dir = hidden_grad * up_pre * sigmoid_gate * (1.0 + gate_pre * (1.0 - sigmoid_gate))
    up_dir = hidden_grad * silu_gate
    hidden = silu_gate * up_pre
    for k, value in enumerate((gate_dir, up_dir, hidden)):
        rounded = value.astype(copies.dtype)
        for i in range(copies.shape[0]):
            copies[i, :, k * width : (k + 1) * width] = rounded


def parcel_kernel(core, both_in, mid, parcel):
    width = both_in.shape[1] // 4
    parcel[:, : 2 * width] = both_in[:, lanes_of(1 - core[0], 0, width, 2)]
    parcel[:, 2 * width :] = mid[...]


def back_kernel(core, mid, own_weights, other_weights, back):
    width = own_weights.shape[0]
    split = mid.shape[1] - width
    for place, weights in ((core[0], own_weights), (1 - core[0], other_weights)):
        output = matmul(mid[:, split:], weights[:, split:])
        back[:, lanes_of(place, 0, width)] = output.astype(back.dtype)
        quant_grad = contract_last(mid[:, :split], weights[:, :split])
        back[:, lanes_of(place, width, width)] = quant_grad.astype(back.dtype)


def weight_grads_kernel(
    core,
    gate_mask,
    up_mask,
    down_mask,
    both_in,
    mid,
    parcel,
    scales,
    gate_grad,
    up_grad,
    down_grad,
):
    width = gate_grad.shape[0]
    split = mid.shape[1] - width
    own_quantized = both_in[:, lanes_of(core[0], 0, width)]
    own_gradient = both_in[:, lanes_of(core[0], width, width)]
    start = 2 * width
    for i in range(width // TILE):
        block = slice(i * TILE, (i + 1) * TILE)
        product = contract_first(own_quantized[:, block], mid[:, :split])
        product = product + contract_first(parcel[:, block], parcel[:, start : start + split])
        for j in range(split // TILE):
            mask, grad = (gate_mask, gate_grad) if j < split // TILE // 2 else (up_mask, up_grad)
            column = j % (split // TILE // 2)
            tile = product[:, j * TILE : (j + 1) * TILE]
            keep = mask[i, column].astype(jnp.float32)
            grad[block, column * TILE : (column + 1) * TILE] = (
                scales[block, :] * tile * keep
            ).astype(grad.dtype)
    for i in range(down_grad.shape[0] // TILE):
        units = slice(split + i * TILE, split + (i + 1) * TILE)
        others = slice(start + units.start, start + units.stop)
        product = contract_first(mid[:, units], own_gradient)
        product = product + contract_first(parcel[:, others], parcel[:, width:start])
        for j in range(width // TILE):
            columns = slice(j * TILE, (j + 1) * TILE)
            keep = down_mask[i, j].astype(jnp.float32)
            down_grad[i * TILE : (i + 1) * TILE, columns] = (product[:, columns] * keep).astype(
                down_grad.dtype
            )


def add_kernel(parts, totals):
    total = add_parts(parts).astype(totals.dtype)
    width = totals.shape[2]
    for core in range(totals.shape[0]):
        totals[core] = total[:, core * width : (core + 1) * width]


def finish_kernel(parts, slope, output, input_grad):
    total = jnp.concatenate([add_parts(parts[:N_FAR]), add_parts(parts[N_FAR:])], axis=0)
    width = output.shape[1]
    output[...] = total[:, :width].astype(output.dtype)
    input_grad[...] = (total[:, width:] * slope[...]).astype(input_grad.dtype)


def per_device(
    tokens, scales, gate_weight, up_weight, down_weight, gate_mask, up_mask, down_mask, cotangent
):
    hidden_width = gate_weight.shape[1]
    own_tokens, width = tokens.shape
    all_tokens = own_tokens * N_COL
    half_tokens = all_tokens // N_CORE
    mid_tokens = half_tokens // N_Z
    bf16, f32 = jnp.bfloat16, jnp.float32
    core = lax.axis_index("core").astype(jnp.int32).reshape(1)
    masks = [gate_mask, up_mask, down_mask]

    squares, smoothed, scales_here, cotangent_here = local_kernel(
        squares_kernel,
        [
            shape((N_ROW, own_tokens, TILE), f32),
            shape((own_tokens, width), f32),
            shape((1, width), f32),
            shape((own_tokens, width), bf16),
        ],
        [core, tokens, scales[None, :], cotangent],
        1,
        stored=(1, 2, 3),
        room=60,
        scratch=[pltpu.VMEM((own_tokens, width), bf16), pltpu.SemaphoreType.DMA((3,))],
    )
    squares = exchange(squares, ROW)
    weights = (gate_weight, up_weight, down_weight)
    own_weights, scale_lanes = local_kernel(
        prepare_kernel,
        [shape((width, 3 * hidden_width), bf16), shape((width, TILE), f32)],
        masks + [scales_here] + list(weights),
        stored=range(7),
        room=60,
        scratch=[pltpu.SMEM(mask.shape, mask.dtype) for mask in masks]
        + [pltpu.VMEM((1, width), f32)]
        + [pltpu.VMEM(w.shape, w.dtype) for w in weights]
        + [pltpu.SemaphoreType.DMA((7,))],
    )
    squares, own_weights = lax.optimization_barrier((squares, own_weights))
    other_weights = swap_cores(own_weights)
    copies, slope = local_kernel(
        quantize_kernel,
        [
            shape((N_CORE * N_FAR, own_tokens // N_CORE, 2 * width), bf16),
            shape((own_tokens, width), f32),
        ],
        [squares, smoothed, scales_here, cotangent_here],
    )
    gathered = exchange_in(copies, far_groups())
    gathered, other_weights = lax.optimization_barrier((gathered, other_weights))
    gathered = gathered.reshape(N_CORE, half_tokens // N_NEAR, 2 * width)
    copies = local_kernel(
        copy_kernel, [shape((N_NEAR, half_tokens // N_NEAR, 4 * width), bf16)], [gathered]
    )
    both_in = exchange_in(copies, near_groups()).reshape(half_tokens, 4 * width)

    flops = 12 * half_tokens * width * hidden_width
    sums = local_kernel(
        forward_kernel,
        [shape((half_tokens, 3 * hidden_width), bf16)],
        [core, both_in, own_weights, other_weights],
        1,
        flops,
    )
    parts = exchange(sums.reshape(N_Z, mid_tokens, -1), "z")
    mid = local_kernel(swiglu_kernel, [shape(parts.shape, bf16)], [parts])
    mid = exchange(mid, "z").reshape(half_tokens, -1)
    back = local_kernel(
        back_kernel,
        [shape((half_tokens, 4 * width), bf16)],
        [core, mid, own_weights, other_weights],
        1,
        flops,
    )
    parcel = local_kernel(
        parcel_kernel,
        [shape((half_tokens, 2 * width + 3 * hidden_width), bf16)],
        [core, both_in, mid],
        1,
    )
    back = exchange_in(back.reshape(N_NEAR, half_tokens // N_NEAR, -1), near_groups())
    parcel = swap_cores(parcel)
    back = local_kernel(
        add_kernel, [shape((N_CORE, half_tokens // N_NEAR, 2 * width), bf16)], [back]
    )
    back = exchange_in(back.reshape(N_CORE * N_FAR, -1, 2 * width), far_groups())
    gate_grad, up_grad, down_grad = local_kernel(
        weight_grads_kernel,
        [shape(w.shape, bf16) for w in weights],
        [core] + masks + [both_in, mid, parcel, scale_lanes],
        4,
        flops,
    )
    output, input_grad = local_kernel(
        finish_kernel, [shape((own_tokens, width), bf16)] * 2, [back, slope]
    )
    return (output, input_grad, gate_grad, up_grad, down_grad)


def solution(mesh):
    fine = Mesh(mesh.devices.reshape(N_Z, N_CORE, N_X, N_Y), ROW + COL)
    placed = (
        P(COL, ROW),
        P(ROW),
        P(ROW, COL),
        P(ROW, COL),
        P(COL, ROW),
        P(ROW, COL),
        P(ROW, COL),
        P(COL, ROW),
        P(COL, ROW),
    )
    return jax.shard_map(
        per_device,
        mesh=fine,
        in_specs=placed,
        out_specs=(
            P(COL, ROW),
            P(COL, ROW),
            P(ROW, COL),
            P(ROW, COL),
            P(COL, ROW),
        ),
        check_vma=False,
    )
```

```python
import functools

import jax
import jax.numpy as jnp
from jax import lax
from jax.experimental import pallas as pl
from jax.experimental.pallas import tpu as pltpu
from jax.sharding import Mesh, PartitionSpec as P

D = 8192
TILE = 128
ROW = ("z", "core")
COL = ("x", "y")
N_Z, N_CORE, N_X, N_Y = 8, 2, 4, 8
N_ROW = N_Z * N_CORE
N_COL = N_X * N_Y
PLANE = ("core",) + COL
N_NEAR = 4
N_FAR = N_COL // N_NEAR


clip_ratio = 1.5


def matmul(left, right):
    return jnp.dot(left, right, preferred_element_type=jnp.float32)


def contract_last(left, right):
    return lax.dot_general(
        left, right, (((1,), (1,)), ((), ())), preferred_element_type=jnp.float32
    )


def contract_first(left, right):
    return lax.dot_general(
        left, right, (((0,), (0,)), ((), ())), preferred_element_type=jnp.float32
    )


def swap_cores(block):
    return lax.ppermute(block, "core", [(0, 1), (1, 0)])


def exchange(parts, axis):
    return lax.all_to_all(parts, axis, 0, 0, tiled=True)


def plane_place(core, x, y):
    return (core * N_X + x % N_X) * N_Y + y % N_Y


def near_groups():
    groups = []
    for core in range(N_CORE):
        for x in range(core, N_X + core, 2):
            for y in range(core, N_Y + core, 2):
                block = [(x + i, y + j) for i in range(2) for j in range(2)]
                block.sort(key=lambda at: (at[0] % 2, at[1] % 2))
                groups.append([plane_place(core, *at) for at in block])
    return groups


def far_groups():
    return [
        [
            plane_place(core, x, y)
            for core in range(N_CORE)
            for x in range(x_parity, N_X, 2)
            for y in range(y_parity, N_Y, 2)
        ]
        for x_parity in range(2)
        for y_parity in range(2)
    ]


def exchange_in(parts, groups):
    return lax.all_to_all(parts, PLANE, 0, 0, axis_index_groups=groups, tiled=True)


def add_parts(parts):
    total = parts[0].astype(jnp.float32)
    for i in range(1, parts.shape[0]):
        total = total + parts[i].astype(jnp.float32)
    return total


def local_kernel(body, outs, args, scalars=0, flops=0, apart=(), stored=(), scratch=(), room=32):
    moved = sum(a.size * a.dtype.itemsize for a in list(args) + list(outs))
    spaces = [pltpu.SMEM if i < scalars else pltpu.VMEM for i in range(len(args))]
    for i in apart:
        spaces[i] = pl.ANY
    for i in stored:
        spaces[i] = pltpu.HBM
    specs = [pl.BlockSpec(memory_space=pltpu.VMEM)] * len(outs)
    return pl.pallas_call(
        body,
        out_shape=outs if len(outs) > 1 else outs[0],
        in_specs=[pl.BlockSpec(memory_space=space) for space in spaces],
        out_specs=specs if len(outs) > 1 else specs[0],
        scratch_shapes=list(scratch),
        compiler_params=pltpu.CompilerParams(vmem_limit_bytes=room << 20),
        cost_estimate=pl.CostEstimate(flops=flops, transcendentals=0, bytes_accessed=moved),
    )(*args)


def shape(dims, dtype):
    return jax.ShapeDtypeStruct(dims, dtype)


def on_diagonal(rows, lanes):
    row = lax.broadcasted_iota(jnp.int32, (rows, lanes), 0)
    return row == lax.broadcasted_iota(jnp.int32, (rows, lanes), 1)


def squares_kernel(
    core, tokens, scales, cotangent, copies, smoothed, scales_here, cotangent_here, tokens_here, arrived
):
    del core
    moves = [
        pltpu.make_async_copy(tokens, tokens_here, arrived.at[0]),
        pltpu.make_async_copy(scales, scales_here, arrived.at[1]),
        pltpu.make_async_copy(cotangent, cotangent_here, arrived.at[2]),
    ]
    for move in moves:
        move.start()
    for move in moves:
        move.wait()
    value = tokens_here[...].astype(jnp.float32) / scales_here[...]
    smoothed[...] = value
    squares = jnp.sum(value * value, axis=1, keepdims=True)
    rows, lanes = value.shape[0], copies.shape[2]
    total = jnp.sum(jnp.where(on_diagonal(rows, lanes), squares, 0.0), axis=0, keepdims=True)
    for i in range(copies.shape[0]):
        copies[i] = total


def prepare_kernel(
    gate_mask,
    up_mask,
    down_mask,
    scales,
    gate,
    up,
    down,
    weights,
    scale_lanes,
    gate_keeps,
    up_keeps,
    down_keeps,
    scales_here,
    gate_here,
    up_here,
    down_here,
    arrived,
):
    sources = (gate_mask, up_mask, down_mask, scales, gate, up, down)
    places = (gate_keeps, up_keeps, down_keeps, scales_here, gate_here, up_here, down_here)
    moves = [
        pltpu.make_async_copy(source, place, arrived.at[k])
        for k, (source, place) in enumerate(zip(sources, places))
    ]
    for move in moves:
        move.start()
    for move in moves[:5]:
        move.wait()
    width = gate.shape[1]
    count = gate.shape[0] // TILE
    for i in range(count):
        block = slice(i * TILE, (i + 1) * TILE)
        scale_lanes[block, :] = jnp.broadcast_to(scales_here[:, block], (TILE, TILE)).T
    tiles = [
        (i, j, slice(i * TILE, (i + 1) * TILE), slice(j * TILE, (j + 1) * TILE))
        for i in range(count)
        for j in range(width // TILE)
    ]
    for i, j, rows, columns in tiles:
        keep = gate_keeps[i, j].astype(jnp.float32)
        kept = scale_lanes[rows, :] * gate_here[rows, columns].astype(jnp.float32) * keep
        weights[rows, columns] = kept.astype(weights.dtype)
    moves[5].wait()
    for i, j, rows, columns in tiles:
        keep = up_keeps[i, j].astype(jnp.float32)
        kept = scale_lanes[rows, :] * up_here[rows, columns].astype(jnp.float32) * keep
        shifted = slice(width + columns.start, width + columns.stop)
        weights[rows, shifted] = kept.astype(weights.dtype)
    moves[6].wait()
    for i, j, rows, columns in tiles:
        keep = down_keeps[i, j].astype(jnp.float32)
        kept = down_here[rows, columns].astype(jnp.float32) * keep
        shifted = slice(2 * width + columns.start, 2 * width + columns.stop)
        weights[rows, shifted] = kept.astype(weights.dtype)


def quantize_kernel(squares, smoothed, scales, cotangent, copies, slope):
    rows, width = copies.shape[1], smoothed.shape[1]
    total = jnp.where(on_diagonal(smoothed.shape[0], TILE), add_parts(squares), 0.0)
    mean_square = jnp.sum(total, axis=1, keepdims=True) / D
    limits = clip_ratio * jnp.sqrt(mean_square + 1e-06)
    squashed = jnp.tanh(smoothed[...] / limits)
    quantized = limits * squashed
    slope[...] = (1.0 - squashed * squashed) / scales[...]
    gradient = cotangent[...].astype(jnp.float32)
    for core in range(N_CORE):
        own = slice(core * rows, (core + 1) * rows)
        quantized_half = quantized[own].astype(copies.dtype)
        gradient_half = gradient[own].astype(copies.dtype)
        for i in range(N_FAR):
            copies[core * N_FAR + i, :, :width] = quantized_half
            copies[core * N_FAR + i, :, width:] = gradient_half


def copy_kernel(blocks, copies):
    width = blocks.shape[2]
    for i in range(copies.shape[0]):
        for core in range(blocks.shape[0]):
            copies[i, :, core * width : (core + 1) * width] = blocks[core]


def lanes_of(core, start, width, count=1):
    return pl.ds(pl.multiple_of(core * 2 * width + start, TILE), count * width)


def forward_kernel(core, both_in, own_weights, other_weights, sums):
    width = own_weights.shape[0]
    split = sums.shape[1] - width
    gate_up = None
    for place, weights in ((core[0], own_weights), (1 - core[0], other_weights)):
        quantized = both_in[:, lanes_of(place, 0, width)]
        gradient = both_in[:, lanes_of(place, width, width)]
        first = matmul(quantized, weights[:, :split])
        second = contract_last(gradient, weights[:, split:])
        if gate_up is None:
            gate_up, hidden_grad = first, second
        else:
            gate_up, hidden_grad = gate_up + first, hidden_grad + second
    sums[:, :split] = gate_up.astype(sums.dtype)
    sums[:, split:] = hidden_grad.astype(sums.dtype)


def swiglu_kernel(parts, copies):
    pre = add_parts(parts)
    width = pre.shape[1] // 3
    gate_pre = pre[:, :width]
    up_pre = pre[:, width : 2 * width]
    hidden_grad = pre[:, 2 * width :]
    sigmoid_gate = 1.0 / (1.0 + jnp.exp(-gate_pre))
    silu_gate = gate_pre * sigmoid_gate
    gate_dir = hidden_grad * up_pre * sigmoid_gate * (1.0 + gate_pre * (1.0 - sigmoid_gate))
    up_dir = hidden_grad * silu_gate
    hidden = silu_gate * up_pre
    for k, value in enumerate((gate_dir, up_dir, hidden)):
        rounded = value.astype(copies.dtype)
        for i in range(copies.shape[0]):
            copies[i, :, k * width : (k + 1) * width] = rounded


def parcel_kernel(core, both_in, mid, parcel):
    width = both_in.shape[1] // 4
    parcel[:, : 2 * width] = both_in[:, lanes_of(1 - core[0], 0, width, 2)]
    parcel[:, 2 * width :] = mid[...]


def back_kernel(core, mid, own_weights, other_weights, back):
    width = own_weights.shape[0]
    split = mid.shape[1] - width
    for place, weights in ((core[0], own_weights), (1 - core[0], other_weights)):
        output = matmul(mid[:, split:], weights[:, split:])
        back[:, lanes_of(place, 0, width)] = output.astype(back.dtype)
        quant_grad = contract_last(mid[:, :split], weights[:, :split])
        back[:, lanes_of(place, width, width)] = quant_grad.astype(back.dtype)


def weight_grads_kernel(
    core,
    gate_mask,
    up_mask,
    down_mask,
    both_in,
    mid,
    parcel,
    scales,
    gate_grad,
    up_grad,
    down_grad,
):
    width = gate_grad.shape[0]
    split = mid.shape[1] - width
    own_quantized = both_in[:, lanes_of(core[0], 0, width)]
    own_gradient = both_in[:, lanes_of(core[0], width, width)]
    start = 2 * width
    for i in range(width // TILE):
        block = slice(i * TILE, (i + 1) * TILE)
        product = contract_first(own_quantized[:, block], mid[:, :split])
        product = product + contract_first(parcel[:, block], parcel[:, start : start + split])
        for j in range(split // TILE):
            mask, grad = (gate_mask, gate_grad) if j < split // TILE // 2 else (up_mask, up_grad)
            column = j % (split // TILE // 2)
            tile = product[:, j * TILE : (j + 1) * TILE]
            keep = mask[i, column].astype(jnp.float32)
            grad[block, column * TILE : (column + 1) * TILE] = (
                scales[block, :] * tile * keep
            ).astype(grad.dtype)
    for i in range(down_grad.shape[0] // TILE):
        units = slice(split + i * TILE, split + (i + 1) * TILE)
        others = slice(start + units.start, start + units.stop)
        product = contract_first(mid[:, units], own_gradient)
        product = product + contract_first(parcel[:, others], parcel[:, width:start])
        for j in range(width // TILE):
            columns = slice(j * TILE, (j + 1) * TILE)
            keep = down_mask[i, j].astype(jnp.float32)
            down_grad[i * TILE : (i + 1) * TILE, columns] = (product[:, columns] * keep).astype(
                down_grad.dtype
            )


def add_kernel(parts, totals):
    total = add_parts(parts).astype(totals.dtype)
    width = totals.shape[2]
    for core in range(totals.shape[0]):
        totals[core] = total[:, core * width : (core + 1) * width]


def finish_kernel(parts, slope, output, input_grad):
    total = jnp.concatenate([add_parts(parts[:N_FAR]), add_parts(parts[N_FAR:])], axis=0)
    width = output.shape[1]
    output[...] = total[:, :width].astype(output.dtype)
    input_grad[...] = (total[:, width:] * slope[...]).astype(input_grad.dtype)


def per_device(
    tokens, scales, gate_weight, up_weight, down_weight, gate_mask, up_mask, down_mask, cotangent
):
    hidden_width = gate_weight.shape[1]
    own_tokens, width = tokens.shape
    all_tokens = own_tokens * N_COL
    half_tokens = all_tokens // N_CORE
    mid_tokens = half_tokens // N_Z
    bf16, f32 = jnp.bfloat16, jnp.float32
    core = lax.axis_index("core").astype(jnp.int32).reshape(1)
    masks = [gate_mask, up_mask, down_mask]

    squares, smoothed, scales_here, cotangent_here = local_kernel(
        squares_kernel,
        [
            shape((N_ROW, 1, TILE), f32),
            shape((own_tokens, width), f32),
            shape((1, width), f32),
            shape((own_tokens, width), bf16),
        ],
        [core, tokens, scales[None, :], cotangent],
        1,
        stored=(1, 2, 3),
        room=60,
        scratch=[pltpu.VMEM((own_tokens, width), bf16), pltpu.SemaphoreType.DMA((3,))],
    )
    squares = exchange(squares, ROW)
    weights = (gate_weight, up_weight, down_weight)
    own_weights, scale_lanes = local_kernel(
        prepare_kernel,
        [shape((width, 3 * hidden_width), bf16), shape((width, TILE), f32)],
        masks + [scales_here] + list(weights),
        stored=range(7),
        room=60,
        scratch=[pltpu.SMEM(mask.shape, mask.dtype) for mask in masks]
        + [pltpu.VMEM((1, width), f32)]
        + [pltpu.VMEM(w.shape, w.dtype) for w in weights]
        + [pltpu.SemaphoreType.DMA((7,))],
    )
    squares, own_weights = lax.optimization_barrier((squares, own_weights))
    copies, slope = local_kernel(
        quantize_kernel,
        [
            shape((N_CORE * N_FAR, own_tokens // N_CORE, 2 * width), bf16),
            shape((own_tokens, width), f32),
        ],
        [squares, smoothed, scales_here, cotangent_here],
    )
    gathered = exchange_in(copies, far_groups())
    gathered = gathered.reshape(N_CORE, half_tokens // N_NEAR, 2 * width)
    copies = local_kernel(
        copy_kernel, [shape((N_NEAR, half_tokens // N_NEAR, 4 * width), bf16)], [gathered]
    )
    copies, own_weights = lax.optimization_barrier((copies, own_weights))
    other_weights = swap_cores(own_weights)
    both_in = exchange_in(copies, near_groups()).reshape(half_tokens, 4 * width)

    flops = 12 * half_tokens * width * hidden_width
    sums = local_kernel(
        forward_kernel,
        [shape((half_tokens, 3 * hidden_width), bf16)],
        [core, both_in, own_weights, other_weights],
        1,
        flops,
    )
    parts = exchange(sums.reshape(N_Z, mid_tokens, -1), "z")
    mid = local_kernel(swiglu_kernel, [shape(parts.shape, bf16)], [parts])
    mid = exchange(mid, "z").reshape(half_tokens, -1)
    back = local_kernel(
        back_kernel,
        [shape((half_tokens, 4 * width), bf16)],
        [core, mid, own_weights, other_weights],
        1,
        flops,
    )
    parcel = local_kernel(
        parcel_kernel,
        [shape((half_tokens, 2 * width + 3 * hidden_width), bf16)],
        [core, both_in, mid],
        1,
    )
    back = exchange_in(back.reshape(N_NEAR, half_tokens // N_NEAR, -1), near_groups())
    parcel = swap_cores(parcel)
    back = local_kernel(
        add_kernel, [shape((N_CORE, half_tokens // N_NEAR, 2 * width), bf16)], [back]
    )
    back = exchange_in(back.reshape(N_CORE * N_FAR, -1, 2 * width), far_groups())
    gate_grad, up_grad, down_grad = local_kernel(
        weight_grads_kernel,
        [shape(w.shape, bf16) for w in weights],
        [core] + masks + [both_in, mid, parcel, scale_lanes],
        4,
        flops,
    )
    output, input_grad = local_kernel(
        finish_kernel, [shape((own_tokens, width), bf16)] * 2, [back, slope]
    )
    return (output, input_grad, gate_grad, up_grad, down_grad)


def solution(mesh):
    fine = Mesh(mesh.devices.reshape(N_Z, N_CORE, N_X, N_Y), ROW + COL)
    placed = (
        P(COL, ROW),
        P(ROW),
        P(ROW, COL),
        P(ROW, COL),
        P(COL, ROW),
        P(ROW, COL),
        P(ROW, COL),
        P(COL, ROW),
        P(COL, ROW),
    )
    return jax.shard_map(
        per_device,
        mesh=fine,
        in_specs=placed,
        out_specs=(
            P(COL, ROW),
            P(COL, ROW),
            P(ROW, COL),
            P(ROW, COL),
            P(COL, ROW),
        ),
        check_vma=False,
    )
```

```python
import functools

import jax
import jax.numpy as jnp
from jax import lax
from jax.experimental import pallas as pl
from jax.experimental.pallas import tpu as pltpu
from jax.sharding import Mesh, PartitionSpec as P

D = 8192
TILE = 128
ROW = ("z", "core")
COL = ("x", "y")
N_Z, N_CORE, N_X, N_Y = 8, 2, 4, 8
N_ROW = N_Z * N_CORE
N_COL = N_X * N_Y
PLANE = ("core",) + COL
N_NEAR = 4
N_FAR = N_COL // N_NEAR


clip_ratio = 1.5


def matmul(left, right):
    return jnp.dot(left, right, preferred_element_type=jnp.float32)


def contract_last(left, right):
    return lax.dot_general(
        left, right, (((1,), (1,)), ((), ())), preferred_element_type=jnp.float32
    )


def contract_first(left, right):
    return lax.dot_general(
        left, right, (((0,), (0,)), ((), ())), preferred_element_type=jnp.float32
    )


def swap_cores(block):
    return lax.ppermute(block, "core", [(0, 1), (1, 0)])


def exchange(parts, axis):
    return lax.all_to_all(parts, axis, 0, 0, tiled=True)


def plane_place(core, x, y):
    return (core * N_X + x % N_X) * N_Y + y % N_Y


def near_groups():
    groups = []
    for core in range(N_CORE):
        for x in range(core, N_X + core, 2):
            for y in range(core, N_Y + core, 2):
                block = [(x + i, y + j) for i in range(2) for j in range(2)]
                block.sort(key=lambda at: (at[0] % 2, at[1] % 2))
                groups.append([plane_place(core, *at) for at in block])
    return groups


def far_groups():
    return [
        [
            plane_place(core, x, y)
            for core in range(N_CORE)
            for x in range(x_parity, N_X, 2)
            for y in range(y_parity, N_Y, 2)
        ]
        for x_parity in range(2)
        for y_parity in range(2)
    ]


def exchange_in(parts, groups):
    return lax.all_to_all(parts, PLANE, 0, 0, axis_index_groups=groups, tiled=True)


def add_parts(parts):
    total = parts[0].astype(jnp.float32)
    for i in range(1, parts.shape[0]):
        total = total + parts[i].astype(jnp.float32)
    return total


def local_kernel(body, outs, args, scalars=0, flops=0, apart=(), stored=(), scratch=(), room=32):
    moved = sum(a.size * a.dtype.itemsize for a in list(args) + list(outs))
    spaces = [pltpu.SMEM if i < scalars else pltpu.VMEM for i in range(len(args))]
    for i in apart:
        spaces[i] = pl.ANY
    for i in stored:
        spaces[i] = pltpu.HBM
    specs = [pl.BlockSpec(memory_space=pltpu.VMEM)] * len(outs)
    return pl.pallas_call(
        body,
        out_shape=outs if len(outs) > 1 else outs[0],
        in_specs=[pl.BlockSpec(memory_space=space) for space in spaces],
        out_specs=specs if len(outs) > 1 else specs[0],
        scratch_shapes=list(scratch),
        compiler_params=pltpu.CompilerParams(vmem_limit_bytes=room << 20),
        cost_estimate=pl.CostEstimate(flops=flops, transcendentals=0, bytes_accessed=moved),
    )(*args)


def shape(dims, dtype):
    return jax.ShapeDtypeStruct(dims, dtype)


def on_diagonal(rows, lanes):
    row = lax.broadcasted_iota(jnp.int32, (rows, lanes), 0)
    return row == lax.broadcasted_iota(jnp.int32, (rows, lanes), 1)


def spread_kernel(core, tokens, cotangent, copies, tokens_here, cotangent_here, arrived):
    del core
    moves = [
        pltpu.make_async_copy(tokens, tokens_here, arrived.at[0]),
        pltpu.make_async_copy(cotangent, cotangent_here, arrived.at[1]),
    ]
    for move in moves:
        move.start()
    for move in moves:
        move.wait()
    rows, width = copies.shape[1], tokens.shape[1]
    for k, source in enumerate((tokens_here, cotangent_here)):
        value = source[...].astype(jnp.float32)
        for half in range(N_CORE):
            block = value[half * rows : (half + 1) * rows].astype(copies.dtype)
            for i in range(N_FAR):
                copies[half * N_FAR + i, :, k * width : (k + 1) * width] = block


def smoothed_of(core, blocks, scales, other_scales, place):
    width = scales.shape[1]
    scale = jnp.where(core[0] == place, scales[...], other_scales[...])
    return blocks[place, :, :width].astype(jnp.float32) / scale, scale


def squares_kernel(core, blocks, scales, other_scales, copies):
    squares = None
    for place in range(N_CORE):
        value, _ = smoothed_of(core, blocks, scales, other_scales, place)
        added = jnp.sum(value * value, axis=1, keepdims=True)
        squares = added if squares is None else squares + added
    rows, lanes = blocks.shape[1], copies.shape[2]
    total = jnp.sum(jnp.where(on_diagonal(rows, lanes), squares, 0.0), axis=0, keepdims=True)
    for i in range(copies.shape[0]):
        copies[i] = total


def prepare_kernel(
    gate_mask,
    up_mask,
    down_mask,
    scales,
    gate,
    up,
    down,
    order,
    weights,
    scale_lanes,
    gate_keeps,
    up_keeps,
    down_keeps,
    scales_here,
    gate_here,
    up_here,
    down_here,
    arrived,
):
    del order
    sources = (gate_mask, up_mask, down_mask, scales, gate, up, down)
    places = (gate_keeps, up_keeps, down_keeps, scales_here, gate_here, up_here, down_here)
    moves = [
        pltpu.make_async_copy(source, place, arrived.at[k])
        for k, (source, place) in enumerate(zip(sources, places))
    ]
    for move in moves:
        move.start()
    for move in moves[:5]:
        move.wait()
    width = gate.shape[1]
    count = gate.shape[0] // TILE
    for i in range(count):
        block = slice(i * TILE, (i + 1) * TILE)
        scale_lanes[block, :] = jnp.broadcast_to(scales_here[:, block], (TILE, TILE)).T
    tiles = [
        (i, j, slice(i * TILE, (i + 1) * TILE), slice(j * TILE, (j + 1) * TILE))
        for i in range(count)
        for j in range(width // TILE)
    ]
    for i, j, rows, columns in tiles:
        keep = gate_keeps[i, j].astype(jnp.float32)
        kept = scale_lanes[rows, :] * gate_here[rows, columns].astype(jnp.float32) * keep
        weights[rows, columns] = kept.astype(weights.dtype)
    moves[5].wait()
    for i, j, rows, columns in tiles:
        keep = up_keeps[i, j].astype(jnp.float32)
        kept = scale_lanes[rows, :] * up_here[rows, columns].astype(jnp.float32) * keep
        shifted = slice(width + columns.start, width + columns.stop)
        weights[rows, shifted] = kept.astype(weights.dtype)
    moves[6].wait()
    for i, j, rows, columns in tiles:
        keep = down_keeps[i, j].astype(jnp.float32)
        kept = down_here[rows, columns].astype(jnp.float32) * keep
        shifted = slice(2 * width + columns.start, 2 * width + columns.stop)
        weights[rows, shifted] = kept.astype(weights.dtype)


def quantize_kernel(core, squares, blocks, scales, other_scales, copies, slope):
    rows, width = blocks.shape[1], scales.shape[1]
    total = jnp.where(on_diagonal(rows, TILE), add_parts(squares), 0.0)
    mean_square = jnp.sum(total, axis=1, keepdims=True) / D
    limits = clip_ratio * jnp.sqrt(mean_square + 1e-06)
    for place in range(N_CORE):
        value, scale = smoothed_of(core, blocks, scales, other_scales, place)
        squashed = jnp.tanh(value / limits)
        quantized = (limits * squashed).astype(copies.dtype)
        slope[:, place * width : (place + 1) * width] = (1.0 - squashed * squashed) / scale
        start = 2 * place * width
        for i in range(copies.shape[0]):
            copies[i, :, start : start + width] = quantized
            copies[i, :, start + width : start + 2 * width] = blocks[place, :, width:]


def lanes_of(core, start, width, count=1):
    return pl.ds(pl.multiple_of(core * 2 * width + start, TILE), count * width)


def forward_kernel(core, both_in, own_weights, other_weights, sums):
    width = own_weights.shape[0]
    split = sums.shape[1] - width
    gate_up = None
    for place, weights in ((core[0], own_weights), (1 - core[0], other_weights)):
        quantized = both_in[:, lanes_of(place, 0, width)]
        gradient = both_in[:, lanes_of(place, width, width)]
        first = matmul(quantized, weights[:, :split])
        second = contract_last(gradient, weights[:, split:])
        if gate_up is None:
            gate_up, hidden_grad = first, second
        else:
            gate_up, hidden_grad = gate_up + first, hidden_grad + second
    sums[:, :split] = gate_up.astype(sums.dtype)
    sums[:, split:] = hidden_grad.astype(sums.dtype)


def swiglu_kernel(parts, copies):
    pre = add_parts(parts)
    width = pre.shape[1] // 3
    gate_pre = pre[:, :width]
    up_pre = pre[:, width : 2 * width]
    hidden_grad = pre[:, 2 * width :]
    sigmoid_gate = 1.0 / (1.0 + jnp.exp(-gate_pre))
    silu_gate = gate_pre * sigmoid_gate
    gate_dir = hidden_grad * up_pre * sigmoid_gate * (1.0 + gate_pre * (1.0 - sigmoid_gate))
    up_dir = hidden_grad * silu_gate
    hidden = silu_gate * up_pre
    for k, value in enumerate((gate_dir, up_dir, hidden)):
        rounded = value.astype(copies.dtype)
        for i in range(copies.shape[0]):
            copies[i, :, k * width : (k + 1) * width] = rounded


def parcel_kernel(core, both_in, mid, parcel):
    width = both_in.shape[1] // 4
    parcel[:, : 2 * width] = both_in[:, lanes_of(1 - core[0], 0, width, 2)]
    parcel[:, 2 * width :] = mid[...]


def back_kernel(core, mid, own_weights, other_weights, back):
    width = own_weights.shape[0]
    split = mid.shape[1] - width
    for place, weights in ((core[0], own_weights), (1 - core[0], other_weights)):
        output = matmul(mid[:, split:], weights[:, split:])
        back[:, lanes_of(place, 0, width)] = output.astype(back.dtype)
        quant_grad = contract_last(mid[:, :split], weights[:, :split])
        back[:, lanes_of(place, width, width)] = quant_grad.astype(back.dtype)


def weight_grads_kernel(
    core,
    gate_mask,
    up_mask,
    down_mask,
    both_in,
    mid,
    parcel,
    scales,
    gate_grad,
    up_grad,
    down_grad,
):
    width = gate_grad.shape[0]
    split = mid.shape[1] - width
    own_quantized = both_in[:, lanes_of(core[0], 0, width)]
    own_gradient = both_in[:, lanes_of(core[0], width, width)]
    start = 2 * width
    for i in range(width // TILE):
        block = slice(i * TILE, (i + 1) * TILE)
        product = contract_first(own_quantized[:, block], mid[:, :split])
        product = product + contract_first(parcel[:, block], parcel[:, start : start + split])
        for j in range(split // TILE):
            mask, grad = (gate_mask, gate_grad) if j < split // TILE // 2 else (up_mask, up_grad)
            column = j % (split // TILE // 2)
            tile = product[:, j * TILE : (j + 1) * TILE]
            keep = mask[i, column].astype(jnp.float32)
            grad[block, column * TILE : (column + 1) * TILE] = (
                scales[block, :] * tile * keep
            ).astype(grad.dtype)
    for i in range(down_grad.shape[0] // TILE):
        units = slice(split + i * TILE, split + (i + 1) * TILE)
        others = slice(start + units.start, start + units.stop)
        product = contract_first(mid[:, units], own_gradient)
        product = product + contract_first(parcel[:, others], parcel[:, width:start])
        for j in range(width // TILE):
            columns = slice(j * TILE, (j + 1) * TILE)
            keep = down_mask[i, j].astype(jnp.float32)
            down_grad[i * TILE : (i + 1) * TILE, columns] = (product[:, columns] * keep).astype(
                down_grad.dtype
            )


def add_kernel(parts, slope, totals):
    total = add_parts(parts)
    width = totals.shape[2] // 2
    for core in range(totals.shape[0]):
        start = 2 * core * width
        output = total[:, start : start + width]
        quant_grad = total[:, start + width : start + 2 * width]
        factor = slope[:, core * width : (core + 1) * width]
        totals[core, :, :width] = output.astype(totals.dtype)
        totals[core, :, width:] = (quant_grad * factor).astype(totals.dtype)


def finish_kernel(parts, output, input_grad):
    total = jnp.concatenate([add_parts(parts[:N_FAR]), add_parts(parts[N_FAR:])], axis=0)
    width = output.shape[1]
    output[...] = total[:, :width].astype(output.dtype)
    input_grad[...] = total[:, width:].astype(input_grad.dtype)


def per_device(
    tokens, scales, gate_weight, up_weight, down_weight, gate_mask, up_mask, down_mask, cotangent
):
    hidden_width = gate_weight.shape[1]
    own_tokens, width = tokens.shape
    all_tokens = own_tokens * N_COL
    half_tokens = all_tokens // N_CORE
    mid_tokens = half_tokens // N_Z
    bf16, f32 = jnp.bfloat16, jnp.float32
    core = lax.axis_index("core").astype(jnp.int32).reshape(1)
    masks = [gate_mask, up_mask, down_mask]

    class_tokens = half_tokens // N_NEAR
    copies = local_kernel(
        spread_kernel,
        [shape((N_CORE * N_FAR, own_tokens // N_CORE, 2 * width), bf16)],
        [core, tokens, cotangent],
        1,
        stored=(1, 2),
        room=60,
        scratch=[pltpu.VMEM(tokens.shape, bf16)] * 2 + [pltpu.SemaphoreType.DMA((2,))],
    )
    scale_row = scales[None, :]
    weights = (gate_weight, up_weight, down_weight)
    own_weights, scale_lanes = local_kernel(
        prepare_kernel,
        [shape((width, 3 * hidden_width), bf16), shape((width, TILE), f32)],
        masks + [scale_row] + list(weights) + [copies],
        stored=range(8),
        room=60,
        scratch=[pltpu.SMEM(mask.shape, mask.dtype) for mask in masks]
        + [pltpu.VMEM((1, width), f32)]
        + [pltpu.VMEM(w.shape, w.dtype) for w in weights]
        + [pltpu.SemaphoreType.DMA((7,))],
    )
    blocks = exchange_in(copies, far_groups())
    other_scales = swap_cores(scale_row)
    blocks, own_weights, other_scales = lax.optimization_barrier(
        (blocks, own_weights, other_scales)
    )
    other_weights = swap_cores(own_weights)
    blocks = blocks.reshape(N_CORE, class_tokens, 2 * width)
    squares = local_kernel(
        squares_kernel,
        [shape((N_Z, 1, TILE), f32)],
        [core, blocks, scale_row, other_scales],
        1,
    )
    squares = exchange(squares, "z")
    copies, slope = local_kernel(
        quantize_kernel,
        [
            shape((N_NEAR, class_tokens, 4 * width), bf16),
            shape((class_tokens, N_CORE * width), f32),
        ],
        [core, squares, blocks, scale_row, other_scales],
        1,
    )
    copies, other_weights = lax.optimization_barrier((copies, other_weights))
    both_in = exchange_in(copies, near_groups()).reshape(half_tokens, 4 * width)

    flops = 12 * half_tokens * width * hidden_width
    sums = local_kernel(
        forward_kernel,
        [shape((half_tokens, 3 * hidden_width), bf16)],
        [core, both_in, own_weights, other_weights],
        1,
        flops,
    )
    parts = exchange(sums.reshape(N_Z, mid_tokens, -1), "z")
    mid = local_kernel(swiglu_kernel, [shape(parts.shape, bf16)], [parts])
    mid = exchange(mid, "z").reshape(half_tokens, -1)
    back = local_kernel(
        back_kernel,
        [shape((half_tokens, 4 * width), bf16)],
        [core, mid, own_weights, other_weights],
        1,
        flops,
    )
    parcel = local_kernel(
        parcel_kernel,
        [shape((half_tokens, 2 * width + 3 * hidden_width), bf16)],
        [core, both_in, mid],
        1,
    )
    back = exchange_in(back.reshape(N_NEAR, class_tokens, -1), near_groups())
    parcel = swap_cores(parcel)
    back = local_kernel(
        add_kernel, [shape((N_CORE, class_tokens, 2 * width), bf16)], [back, slope]
    )
    back = exchange_in(back.reshape(N_CORE * N_FAR, -1, 2 * width), far_groups())
    gate_grad, up_grad, down_grad = local_kernel(
        weight_grads_kernel,
        [shape(w.shape, bf16) for w in weights],
        [core] + masks + [both_in, mid, parcel, scale_lanes],
        4,
        flops,
    )
    output, input_grad = local_kernel(
        finish_kernel, [shape((own_tokens, width), bf16)] * 2, [back]
    )
    return (output, input_grad, gate_grad, up_grad, down_grad)


def solution(mesh):
    fine = Mesh(mesh.devices.reshape(N_Z, N_CORE, N_X, N_Y), ROW + COL)
    placed = (
        P(COL, ROW),
        P(ROW),
        P(ROW, COL),
        P(ROW, COL),
        P(COL, ROW),
        P(ROW, COL),
        P(ROW, COL),
        P(COL, ROW),
        P(COL, ROW),
    )
    return jax.shard_map(
        per_device,
        mesh=fine,
        in_specs=placed,
        out_specs=(
            P(COL, ROW),
            P(COL, ROW),
            P(ROW, COL),
            P(ROW, COL),
            P(COL, ROW),
        ),
        check_vma=False,
    )
```

```python
import functools

import jax
import jax.numpy as jnp
from jax import lax
from jax.experimental import pallas as pl
from jax.experimental.pallas import tpu as pltpu
from jax.sharding import Mesh, PartitionSpec as P

D = 8192
TILE = 128
ROW = ("z", "core")
COL = ("x", "y")
N_Z, N_CORE, N_X, N_Y = 8, 2, 4, 8
N_ROW = N_Z * N_CORE
N_COL = N_X * N_Y
PLANE = ("core",) + COL
N_NEAR = 4
N_FAR = N_COL // N_NEAR


clip_ratio = 1.5


def matmul(left, right):
    return jnp.dot(left, right, preferred_element_type=jnp.float32)


def contract_last(left, right):
    return lax.dot_general(
        left, right, (((1,), (1,)), ((), ())), preferred_element_type=jnp.float32
    )


def contract_first(left, right):
    return lax.dot_general(
        left, right, (((0,), (0,)), ((), ())), preferred_element_type=jnp.float32
    )


def swap_cores(block):
    return lax.ppermute(block, "core", [(0, 1), (1, 0)])


def exchange(parts, axis):
    return lax.all_to_all(parts, axis, 0, 0, tiled=True)


def plane_place(core, x, y):
    return (core * N_X + x % N_X) * N_Y + y % N_Y


def near_groups():
    groups = []
    for core in range(N_CORE):
        for x in range(core, N_X + core, 2):
            for y in range(core, N_Y + core, 2):
                block = [(x + i, y + j) for i in range(2) for j in range(2)]
                block.sort(key=lambda at: (at[0] % 2, at[1] % 2))
                groups.append([plane_place(core, *at) for at in block])
    return groups


def far_groups():
    return [
        [
            plane_place(core, x, y)
            for core in range(N_CORE)
            for x in range(x_parity, N_X, 2)
            for y in range(y_parity, N_Y, 2)
        ]
        for x_parity in range(2)
        for y_parity in range(2)
    ]


def exchange_in(parts, groups):
    return lax.all_to_all(parts, PLANE, 0, 0, axis_index_groups=groups, tiled=True)


def add_parts(parts):
    total = parts[0].astype(jnp.float32)
    for i in range(1, parts.shape[0]):
        total = total + parts[i].astype(jnp.float32)
    return total


def local_kernel(body, outs, args, scalars=0, flops=0, apart=(), stored=(), scratch=(), room=32):
    moved = sum(a.size * a.dtype.itemsize for a in list(args) + list(outs))
    spaces = [pltpu.SMEM if i < scalars else pltpu.VMEM for i in range(len(args))]
    for i in apart:
        spaces[i] = pl.ANY
    for i in stored:
        spaces[i] = pltpu.HBM
    specs = [pl.BlockSpec(memory_space=pltpu.VMEM)] * len(outs)
    return pl.pallas_call(
        body,
        out_shape=outs if len(outs) > 1 else outs[0],
        in_specs=[pl.BlockSpec(memory_space=space) for space in spaces],
        out_specs=specs if len(outs) > 1 else specs[0],
        scratch_shapes=list(scratch),
        compiler_params=pltpu.CompilerParams(vmem_limit_bytes=room << 20),
        cost_estimate=pl.CostEstimate(flops=flops, transcendentals=0, bytes_accessed=moved),
    )(*args)


def shape(dims, dtype):
    return jax.ShapeDtypeStruct(dims, dtype)


def on_diagonal(rows, lanes):
    row = lax.broadcasted_iota(jnp.int32, (rows, lanes), 0)
    return row == lax.broadcasted_iota(jnp.int32, (rows, lanes), 1)


def spread_kernel(core, tokens, cotangent, copies, tokens_here, cotangent_here, arrived):
    del core
    moves = [
        pltpu.make_async_copy(tokens, tokens_here, arrived.at[0]),
        pltpu.make_async_copy(cotangent, cotangent_here, arrived.at[1]),
    ]
    for move in moves:
        move.start()
    for move in moves:
        move.wait()
    rows, width = copies.shape[1], tokens.shape[1]
    for k, source in enumerate((tokens_here, cotangent_here)):
        value = source[...].astype(jnp.float32)
        for half in range(N_CORE):
            block = value[half * rows : (half + 1) * rows].astype(copies.dtype)
            for i in range(N_FAR):
                copies[half * N_FAR + i, :, k * width : (k + 1) * width] = block


def smoothed_of(core, blocks, scales, other_scales, place):
    width = scales.shape[1]
    scale = jnp.where(core[0] == place, scales[...], other_scales[...])
    return blocks[place, :, :width].astype(jnp.float32) / scale, scale


def squares_kernel(core, blocks, scales, other_scales, copies):
    squares = None
    for place in range(N_CORE):
        value, _ = smoothed_of(core, blocks, scales, other_scales, place)
        added = jnp.sum(value * value, axis=1, keepdims=True)
        squares = added if squares is None else squares + added
    rows, lanes = blocks.shape[1], copies.shape[2]
    total = jnp.sum(jnp.where(on_diagonal(rows, lanes), squares, 0.0), axis=0, keepdims=True)
    for i in range(copies.shape[0]):
        copies[i] = total


def prepare_kernel(
    gate_mask,
    up_mask,
    down_mask,
    scales,
    gate,
    up,
    down,
    order,
    weights,
    scale_lanes,
    gate_keeps,
    up_keeps,
    down_keeps,
    scales_here,
    gate_here,
    up_here,
    down_here,
    arrived,
):
    del order
    sources = (gate_mask, up_mask, down_mask, scales, gate, up, down)
    places = (gate_keeps, up_keeps, down_keeps, scales_here, gate_here, up_here, down_here)
    moves = [
        pltpu.make_async_copy(source, place, arrived.at[k])
        for k, (source, place) in enumerate(zip(sources, places))
    ]
    for move in moves:
        move.start()
    for move in moves[:5]:
        move.wait()
    width = gate.shape[1]
    count = gate.shape[0] // TILE
    for i in range(count):
        block = slice(i * TILE, (i + 1) * TILE)
        scale_lanes[block, :] = jnp.broadcast_to(scales_here[:, block], (TILE, TILE)).T
    tiles = [
        (i, j, slice(i * TILE, (i + 1) * TILE), slice(j * TILE, (j + 1) * TILE))
        for i in range(count)
        for j in range(width // TILE)
    ]
    for i, j, rows, columns in tiles:
        keep = gate_keeps[i, j].astype(jnp.float32)
        kept = scale_lanes[rows, :] * gate_here[rows, columns].astype(jnp.float32) * keep
        weights[rows, columns] = kept.astype(weights.dtype)
    moves[5].wait()
    for i, j, rows, columns in tiles:
        keep = up_keeps[i, j].astype(jnp.float32)
        kept = scale_lanes[rows, :] * up_here[rows, columns].astype(jnp.float32) * keep
        shifted = slice(width + columns.start, width + columns.stop)
        weights[rows, shifted] = kept.astype(weights.dtype)
    moves[6].wait()
    for i, j, rows, columns in tiles:
        keep = down_keeps[i, j].astype(jnp.float32)
        kept = down_here[rows, columns].astype(jnp.float32) * keep
        shifted = slice(2 * width + columns.start, 2 * width + columns.stop)
        weights[rows, shifted] = kept.astype(weights.dtype)


def limits_of(squares, rows):
    total = jnp.where(on_diagonal(rows, TILE), add_parts(squares), 0.0)
    mean_square = jnp.sum(total, axis=1, keepdims=True) / D
    return clip_ratio * jnp.sqrt(mean_square + 1e-06)


def quantize_kernel(core, squares, blocks, scales, other_scales, copies):
    rows, width = blocks.shape[1], scales.shape[1]
    limits = limits_of(squares, rows)
    for place in range(N_CORE):
        value, _ = smoothed_of(core, blocks, scales, other_scales, place)
        squashed = jnp.tanh(value / limits)
        quantized = (limits * squashed).astype(copies.dtype)
        start = 2 * place * width
        for i in range(copies.shape[0]):
            copies[i, :, start : start + width] = quantized
            copies[i, :, start + width : start + 2 * width] = blocks[place, :, width:]


def lanes_of(core, start, width, count=1):
    return pl.ds(pl.multiple_of(core * 2 * width + start, TILE), count * width)


def forward_kernel(core, both_in, own_weights, other_weights, sums):
    width = own_weights.shape[0]
    split = sums.shape[1] - width
    gate_up = None
    for place, weights in ((core[0], own_weights), (1 - core[0], other_weights)):
        quantized = both_in[:, lanes_of(place, 0, width)]
        gradient = both_in[:, lanes_of(place, width, width)]
        first = matmul(quantized, weights[:, :split])
        second = contract_last(gradient, weights[:, split:])
        if gate_up is None:
            gate_up, hidden_grad = first, second
        else:
            gate_up, hidden_grad = gate_up + first, hidden_grad + second
    sums[:, :split] = gate_up.astype(sums.dtype)
    sums[:, split:] = hidden_grad.astype(sums.dtype)


def swiglu_kernel(parts, copies):
    pre = add_parts(parts)
    width = pre.shape[1] // 3
    gate_pre = pre[:, :width]
    up_pre = pre[:, width : 2 * width]
    hidden_grad = pre[:, 2 * width :]
    sigmoid_gate = 1.0 / (1.0 + jnp.exp(-gate_pre))
    silu_gate = gate_pre * sigmoid_gate
    gate_dir = hidden_grad * up_pre * sigmoid_gate * (1.0 + gate_pre * (1.0 - sigmoid_gate))
    up_dir = hidden_grad * silu_gate
    hidden = silu_gate * up_pre
    for k, value in enumerate((gate_dir, up_dir, hidden)):
        rounded = value.astype(copies.dtype)
        for i in range(copies.shape[0]):
            copies[i, :, k * width : (k + 1) * width] = rounded


def parcel_kernel(core, both_in, mid, parcel):
    width = both_in.shape[1] // 4
    parcel[:, : 2 * width] = both_in[:, lanes_of(1 - core[0], 0, width, 2)]
    parcel[:, 2 * width :] = mid[...]


def back_kernel(core, mid, own_weights, other_weights, back):
    width = own_weights.shape[0]
    split = mid.shape[1] - width
    for place, weights in ((core[0], own_weights), (1 - core[0], other_weights)):
        output = matmul(mid[:, split:], weights[:, split:])
        back[:, lanes_of(place, 0, width)] = output.astype(back.dtype)
        quant_grad = contract_last(mid[:, :split], weights[:, :split])
        back[:, lanes_of(place, width, width)] = quant_grad.astype(back.dtype)


def weight_grads_kernel(
    core,
    gate_mask,
    up_mask,
    down_mask,
    both_in,
    mid,
    parcel,
    scales,
    gate_grad,
    up_grad,
    down_grad,
):
    width = gate_grad.shape[0]
    split = mid.shape[1] - width
    own_quantized = both_in[:, lanes_of(core[0], 0, width)]
    own_gradient = both_in[:, lanes_of(core[0], width, width)]
    start = 2 * width
    for i in range(width // TILE):
        block = slice(i * TILE, (i + 1) * TILE)
        product = contract_first(own_quantized[:, block], mid[:, :split])
        product = product + contract_first(parcel[:, block], parcel[:, start : start + split])
        for j in range(split // TILE):
            mask, grad = (gate_mask, gate_grad) if j < split // TILE // 2 else (up_mask, up_grad)
            column = j % (split // TILE // 2)
            tile = product[:, j * TILE : (j + 1) * TILE]
            keep = mask[i, column].astype(jnp.float32)
            grad[block, column * TILE : (column + 1) * TILE] = (
                scales[block, :] * tile * keep
            ).astype(grad.dtype)
    for i in range(down_grad.shape[0] // TILE):
        units = slice(split + i * TILE, split + (i + 1) * TILE)
        others = slice(start + units.start, start + units.stop)
        product = contract_first(mid[:, units], own_gradient)
        product = product + contract_first(parcel[:, others], parcel[:, width:start])
        for j in range(width // TILE):
            columns = slice(j * TILE, (j + 1) * TILE)
            keep = down_mask[i, j].astype(jnp.float32)
            down_grad[i * TILE : (i + 1) * TILE, columns] = (product[:, columns] * keep).astype(
                down_grad.dtype
            )


def add_kernel(core, parts, squares, blocks, scales, other_scales, totals):
    total = add_parts(parts)
    limits = limits_of(squares, blocks.shape[1])
    width = totals.shape[2] // 2
    for place in range(totals.shape[0]):
        start = 2 * place * width
        output = total[:, start : start + width]
        quant_grad = total[:, start + width : start + 2 * width]
        value, scale = smoothed_of(core, blocks, scales, other_scales, place)
        squashed = jnp.tanh(value / limits)
        factor = (1.0 - squashed * squashed) / scale
        totals[place, :, :width] = output.astype(totals.dtype)
        totals[place, :, width:] = (quant_grad * factor).astype(totals.dtype)


def finish_kernel(parts, output, input_grad):
    total = jnp.concatenate([add_parts(parts[:N_FAR]), add_parts(parts[N_FAR:])], axis=0)
    width = output.shape[1]
    output[...] = total[:, :width].astype(output.dtype)
    input_grad[...] = total[:, width:].astype(input_grad.dtype)


def per_device(
    tokens, scales, gate_weight, up_weight, down_weight, gate_mask, up_mask, down_mask, cotangent
):
    hidden_width = gate_weight.shape[1]
    own_tokens, width = tokens.shape
    all_tokens = own_tokens * N_COL
    half_tokens = all_tokens // N_CORE
    mid_tokens = half_tokens // N_Z
    bf16, f32 = jnp.bfloat16, jnp.float32
    core = lax.axis_index("core").astype(jnp.int32).reshape(1)
    masks = [gate_mask, up_mask, down_mask]

    class_tokens = half_tokens // N_NEAR
    copies = local_kernel(
        spread_kernel,
        [shape((N_CORE * N_FAR, own_tokens // N_CORE, 2 * width), bf16)],
        [core, tokens, cotangent],
        1,
        stored=(1, 2),
        room=60,
        scratch=[pltpu.VMEM(tokens.shape, bf16)] * 2 + [pltpu.SemaphoreType.DMA((2,))],
    )
    scale_row = scales[None, :]
    weights = (gate_weight, up_weight, down_weight)
    own_weights, scale_lanes = local_kernel(
        prepare_kernel,
        [shape((width, 3 * hidden_width), bf16), shape((width, TILE), f32)],
        masks + [scale_row] + list(weights) + [copies],
        stored=range(8),
        room=60,
        scratch=[pltpu.SMEM(mask.shape, mask.dtype) for mask in masks]
        + [pltpu.VMEM((1, width), f32)]
        + [pltpu.VMEM(w.shape, w.dtype) for w in weights]
        + [pltpu.SemaphoreType.DMA((7,))],
    )
    blocks = exchange_in(copies, far_groups())
    other_scales = swap_cores(scale_row)
    blocks, own_weights, other_scales = lax.optimization_barrier(
        (blocks, own_weights, other_scales)
    )
    other_weights = swap_cores(own_weights)
    blocks = blocks.reshape(N_CORE, class_tokens, 2 * width)
    squares = local_kernel(
        squares_kernel,
        [shape((N_Z, 1, TILE), f32)],
        [core, blocks, scale_row, other_scales],
        1,
    )
    squares = exchange(squares, "z")
    copies = local_kernel(
        quantize_kernel,
        [shape((N_NEAR, class_tokens, 4 * width), bf16)],
        [core, squares, blocks, scale_row, other_scales],
        1,
    )
    copies, other_weights = lax.optimization_barrier((copies, other_weights))
    both_in = exchange_in(copies, near_groups()).reshape(half_tokens, 4 * width)

    flops = 12 * half_tokens * width * hidden_width
    sums = local_kernel(
        forward_kernel,
        [shape((half_tokens, 3 * hidden_width), bf16)],
        [core, both_in, own_weights, other_weights],
        1,
        flops,
    )
    parts = exchange(sums.reshape(N_Z, mid_tokens, -1), "z")
    mid = local_kernel(swiglu_kernel, [shape(parts.shape, bf16)], [parts])
    mid = exchange(mid, "z").reshape(half_tokens, -1)
    back = local_kernel(
        back_kernel,
        [shape((half_tokens, 4 * width), bf16)],
        [core, mid, own_weights, other_weights],
        1,
        flops,
    )
    parcel = local_kernel(
        parcel_kernel,
        [shape((half_tokens, 2 * width + 3 * hidden_width), bf16)],
        [core, both_in, mid],
        1,
    )
    back = exchange_in(back.reshape(N_NEAR, class_tokens, -1), near_groups())
    parcel = swap_cores(parcel)
    back = local_kernel(
        add_kernel, [shape((N_CORE, class_tokens, 2 * width), bf16)],
        [core, back, squares, blocks, scale_row, other_scales],
        1,
    )
    back = exchange_in(back.reshape(N_CORE * N_FAR, -1, 2 * width), far_groups())
    gate_grad, up_grad, down_grad = local_kernel(
        weight_grads_kernel,
        [shape(w.shape, bf16) for w in weights],
        [core] + masks + [both_in, mid, parcel, scale_lanes],
        4,
        flops,
    )
    output, input_grad = local_kernel(
        finish_kernel, [shape((own_tokens, width), bf16)] * 2, [back]
    )
    return (output, input_grad, gate_grad, up_grad, down_grad)


def solution(mesh):
    fine = Mesh(mesh.devices.reshape(N_Z, N_CORE, N_X, N_Y), ROW + COL)
    placed = (
        P(COL, ROW),
        P(ROW),
        P(ROW, COL),
        P(ROW, COL),
        P(COL, ROW),
        P(ROW, COL),
        P(ROW, COL),
        P(COL, ROW),
        P(COL, ROW),
    )
    return jax.shard_map(
        per_device,
        mesh=fine,
        in_specs=placed,
        out_specs=(
            P(COL, ROW),
            P(COL, ROW),
            P(ROW, COL),
            P(ROW, COL),
            P(COL, ROW),
        ),
        check_vma=False,
    )
```

```python
import functools

import jax
import jax.numpy as jnp
from jax import lax
from jax.experimental import pallas as pl
from jax.experimental.pallas import tpu as pltpu
from jax.sharding import Mesh, PartitionSpec as P

D = 8192
TILE = 128
ROW = ("z", "core")
COL = ("x", "y")
N_Z, N_CORE, N_X, N_Y = 8, 2, 4, 8
N_ROW = N_Z * N_CORE
N_COL = N_X * N_Y
PLANE = ("core",) + COL
N_NEAR = 4
N_FAR = N_COL // N_NEAR


clip_ratio = 1.5


def matmul(left, right):
    return jnp.dot(left, right, preferred_element_type=jnp.float32)


def contract_last(left, right):
    return lax.dot_general(
        left, right, (((1,), (1,)), ((), ())), preferred_element_type=jnp.float32
    )


def contract_first(left, right):
    return lax.dot_general(
        left, right, (((0,), (0,)), ((), ())), preferred_element_type=jnp.float32
    )


def swap_cores(block):
    return lax.ppermute(block, "core", [(0, 1), (1, 0)])


def exchange(parts, axis):
    return lax.all_to_all(parts, axis, 0, 0, tiled=True)


def plane_place(core, x, y):
    return (core * N_X + x % N_X) * N_Y + y % N_Y


def near_groups():
    groups = []
    for core in range(N_CORE):
        for x in range(core, N_X + core, 2):
            for y in range(core, N_Y + core, 2):
                block = [(x + i, y + j) for i in range(2) for j in range(2)]
                block.sort(key=lambda at: (at[0] % 2, at[1] % 2))
                groups.append([plane_place(core, *at) for at in block])
    return groups


def far_groups():
    return [
        [
            plane_place(core, x, y)
            for core in range(N_CORE)
            for x in range(x_parity, N_X, 2)
            for y in range(y_parity, N_Y, 2)
        ]
        for x_parity in range(2)
        for y_parity in range(2)
    ]


def exchange_in(parts, groups):
    return lax.all_to_all(parts, PLANE, 0, 0, axis_index_groups=groups, tiled=True)


def add_parts(parts):
    total = parts[0].astype(jnp.float32)
    for i in range(1, parts.shape[0]):
        total = total + parts[i].astype(jnp.float32)
    return total


def local_kernel(body, outs, args, scalars=0, flops=0, apart=(), stored=(), scratch=(), room=32):
    moved = sum(a.size * a.dtype.itemsize for a in list(args) + list(outs))
    spaces = [pltpu.SMEM if i < scalars else pltpu.VMEM for i in range(len(args))]
    for i in apart:
        spaces[i] = pl.ANY
    for i in stored:
        spaces[i] = pltpu.HBM
    specs = [pl.BlockSpec(memory_space=pltpu.VMEM)] * len(outs)
    return pl.pallas_call(
        body,
        out_shape=outs if len(outs) > 1 else outs[0],
        in_specs=[pl.BlockSpec(memory_space=space) for space in spaces],
        out_specs=specs if len(outs) > 1 else specs[0],
        scratch_shapes=list(scratch),
        compiler_params=pltpu.CompilerParams(vmem_limit_bytes=room << 20),
        cost_estimate=pl.CostEstimate(flops=flops, transcendentals=0, bytes_accessed=moved),
    )(*args)


def shape(dims, dtype):
    return jax.ShapeDtypeStruct(dims, dtype)


def on_diagonal(rows, lanes):
    row = lax.broadcasted_iota(jnp.int32, (rows, lanes), 0)
    return row == lax.broadcasted_iota(jnp.int32, (rows, lanes), 1)


def spread_kernel(core, tokens, cotangent, copies, tokens_here, cotangent_here, arrived):
    del core
    moves = [
        pltpu.make_async_copy(tokens, tokens_here, arrived.at[0]),
        pltpu.make_async_copy(cotangent, cotangent_here, arrived.at[1]),
    ]
    for move in moves:
        move.start()
    for move in moves:
        move.wait()
    rows, width = copies.shape[1], tokens.shape[1]
    for k, source in enumerate((tokens_here, cotangent_here)):
        value = source[...].astype(jnp.float32)
        for half in range(N_CORE):
            block = value[half * rows : (half + 1) * rows].astype(copies.dtype)
            for i in range(N_FAR):
                copies[half * N_FAR + i, :, k * width : (k + 1) * width] = block


def smoothed_of(core, blocks, scales, other_scales, place):
    width = scales.shape[1]
    scale = jnp.where(core[0] == place, scales[...], other_scales[...])
    return blocks[place, :, :width].astype(jnp.float32) / scale, scale


def squares_kernel(core, blocks, scales, other_scales, copies):
    squares = None
    for place in range(N_CORE):
        value, _ = smoothed_of(core, blocks, scales, other_scales, place)
        added = jnp.sum(value * value, axis=1, keepdims=True)
        squares = added if squares is None else squares + added
    rows, lanes = blocks.shape[1], copies.shape[2]
    total = jnp.sum(jnp.where(on_diagonal(rows, lanes), squares, 0.0), axis=0, keepdims=True)
    for i in range(copies.shape[0]):
        copies[i] = total


def prepare_kernel(
    gate_mask,
    up_mask,
    down_mask,
    scales,
    gate,
    up,
    down,
    order,
    weights,
    scale_lanes,
    gate_keeps,
    up_keeps,
    down_keeps,
    scales_here,
    gate_here,
    up_here,
    down_here,
    arrived,
):
    del order
    sources = (gate_mask, up_mask, down_mask, scales, gate, up, down)
    places = (gate_keeps, up_keeps, down_keeps, scales_here, gate_here, up_here, down_here)
    moves = [
        pltpu.make_async_copy(source, place, arrived.at[k])
        for k, (source, place) in enumerate(zip(sources, places))
    ]
    for move in moves:
        move.start()
    for move in moves[:5]:
        move.wait()
    width = gate.shape[1]
    count = gate.shape[0] // TILE
    for i in range(count):
        block = slice(i * TILE, (i + 1) * TILE)
        scale_lanes[block, :] = jnp.broadcast_to(scales_here[:, block], (TILE, TILE)).T
    tiles = [
        (i, j, slice(i * TILE, (i + 1) * TILE), slice(j * TILE, (j + 1) * TILE))
        for i in range(count)
        for j in range(width // TILE)
    ]
    for i, j, rows, columns in tiles:
        keep = gate_keeps[i, j].astype(jnp.float32)
        kept = scale_lanes[rows, :] * gate_here[rows, columns].astype(jnp.float32) * keep
        weights[rows, columns] = kept.astype(weights.dtype)
    moves[5].wait()
    for i, j, rows, columns in tiles:
        keep = up_keeps[i, j].astype(jnp.float32)
        kept = scale_lanes[rows, :] * up_here[rows, columns].astype(jnp.float32) * keep
        shifted = slice(width + columns.start, width + columns.stop)
        weights[rows, shifted] = kept.astype(weights.dtype)
    moves[6].wait()
    for i, j, rows, columns in tiles:
        keep = down_keeps[i, j].astype(jnp.float32)
        kept = down_here[rows, columns].astype(jnp.float32) * keep
        shifted = slice(2 * width + columns.start, 2 * width + columns.stop)
        weights[rows, shifted] = kept.astype(weights.dtype)


def limits_of(squares, rows):
    total = jnp.where(on_diagonal(rows, TILE), add_parts(squares), 0.0)
    mean_square = jnp.sum(total, axis=1, keepdims=True) / D
    return clip_ratio * jnp.sqrt(mean_square + 1e-06)


def quantize_kernel(core, squares, blocks, scales, other_scales, copies):
    rows, width = blocks.shape[1], scales.shape[1]
    limits = limits_of(squares, rows)
    for place in range(N_CORE):
        value, _ = smoothed_of(core, blocks, scales, other_scales, place)
        squashed = jnp.tanh(value / limits)
        quantized = (limits * squashed).astype(copies.dtype)
        start = 2 * place * width
        for i in range(copies.shape[0]):
            copies[i, :, start : start + width] = quantized
            copies[i, :, start + width : start + 2 * width] = blocks[place, :, width:]


def lanes_of(core, start, width, count=1):
    return pl.ds(pl.multiple_of(core * 2 * width + start, TILE), count * width)


def forward_kernel(core, both_in, own_weights, other_stored, sums, other_weights, arrived):
    move = pltpu.make_async_copy(other_stored, other_weights, arrived)
    move.start()
    width = own_weights.shape[0]
    split = sums.shape[1] - width
    gate_up = None
    for place, weights in ((core[0], own_weights), (1 - core[0], other_weights)):
        if weights is other_weights:
            move.wait()
        quantized = both_in[:, lanes_of(place, 0, width)]
        gradient = both_in[:, lanes_of(place, width, width)]
        first = matmul(quantized, weights[:, :split])
        second = contract_last(gradient, weights[:, split:])
        if gate_up is None:
            gate_up, hidden_grad = first, second
        else:
            gate_up, hidden_grad = gate_up + first, hidden_grad + second
    sums[:, :split] = gate_up.astype(sums.dtype)
    sums[:, split:] = hidden_grad.astype(sums.dtype)


def swiglu_kernel(parts, copies):
    pre = add_parts(parts)
    width = pre.shape[1] // 3
    gate_pre = pre[:, :width]
    up_pre = pre[:, width : 2 * width]
    hidden_grad = pre[:, 2 * width :]
    sigmoid_gate = 1.0 / (1.0 + jnp.exp(-gate_pre))
    silu_gate = gate_pre * sigmoid_gate
    gate_dir = hidden_grad * up_pre * sigmoid_gate * (1.0 + gate_pre * (1.0 - sigmoid_gate))
    up_dir = hidden_grad * silu_gate
    hidden = silu_gate * up_pre
    for k, value in enumerate((gate_dir, up_dir, hidden)):
        rounded = value.astype(copies.dtype)
        for i in range(copies.shape[0]):
            copies[i, :, k * width : (k + 1) * width] = rounded


def parcel_kernel(core, both_in, mid, parcel):
    width = both_in.shape[1] // 4
    parcel[:, : 2 * width] = both_in[:, lanes_of(1 - core[0], 0, width, 2)]
    parcel[:, 2 * width :] = mid[...]


def back_kernel(core, mid, own_weights, other_stored, back, other_weights, arrived):
    move = pltpu.make_async_copy(other_stored, other_weights, arrived)
    move.start()
    width = own_weights.shape[0]
    split = mid.shape[1] - width
    for place, weights in ((core[0], own_weights), (1 - core[0], other_weights)):
        if weights is other_weights:
            move.wait()
        output = matmul(mid[:, split:], weights[:, split:])
        back[:, lanes_of(place, 0, width)] = output.astype(back.dtype)
        quant_grad = contract_last(mid[:, :split], weights[:, :split])
        back[:, lanes_of(place, width, width)] = quant_grad.astype(back.dtype)


def weight_grads_kernel(
    core,
    gate_mask,
    up_mask,
    down_mask,
    both_in,
    mid,
    parcel,
    scales,
    gate_grad,
    up_grad,
    down_grad,
):
    width = gate_grad.shape[0]
    split = mid.shape[1] - width
    own_quantized = both_in[:, lanes_of(core[0], 0, width)]
    own_gradient = both_in[:, lanes_of(core[0], width, width)]
    start = 2 * width
    for i in range(width // TILE):
        block = slice(i * TILE, (i + 1) * TILE)
        product = contract_first(own_quantized[:, block], mid[:, :split])
        product = product + contract_first(parcel[:, block], parcel[:, start : start + split])
        for j in range(split // TILE):
            mask, grad = (gate_mask, gate_grad) if j < split // TILE // 2 else (up_mask, up_grad)
            column = j % (split // TILE // 2)
            tile = product[:, j * TILE : (j + 1) * TILE]
            keep = mask[i, column].astype(jnp.float32)
            grad[block, column * TILE : (column + 1) * TILE] = (
                scales[block, :] * tile * keep
            ).astype(grad.dtype)
    for i in range(down_grad.shape[0] // TILE):
        units = slice(split + i * TILE, split + (i + 1) * TILE)
        others = slice(start + units.start, start + units.stop)
        product = contract_first(mid[:, units], own_gradient)
        product = product + contract_first(parcel[:, others], parcel[:, width:start])
        for j in range(width // TILE):
            columns = slice(j * TILE, (j + 1) * TILE)
            keep = down_mask[i, j].astype(jnp.float32)
            down_grad[i * TILE : (i + 1) * TILE, columns] = (product[:, columns] * keep).astype(
                down_grad.dtype
            )


def add_kernel(core, parts, squares, blocks, scales, other_scales, totals):
    total = add_parts(parts)
    limits = limits_of(squares, blocks.shape[1])
    width = totals.shape[2] // 2
    for place in range(totals.shape[0]):
        start = 2 * place * width
        output = total[:, start : start + width]
        quant_grad = total[:, start + width : start + 2 * width]
        value, scale = smoothed_of(core, blocks, scales, other_scales, place)
        squashed = jnp.tanh(value / limits)
        factor = (1.0 - squashed * squashed) / scale
        totals[place, :, :width] = output.astype(totals.dtype)
        totals[place, :, width:] = (quant_grad * factor).astype(totals.dtype)


def finish_kernel(parts, output, input_grad):
    total = jnp.concatenate([add_parts(parts[:N_FAR]), add_parts(parts[N_FAR:])], axis=0)
    width = output.shape[1]
    output[...] = total[:, :width].astype(output.dtype)
    input_grad[...] = total[:, width:].astype(input_grad.dtype)


def per_device(
    tokens, scales, gate_weight, up_weight, down_weight, gate_mask, up_mask, down_mask, cotangent
):
    hidden_width = gate_weight.shape[1]
    own_tokens, width = tokens.shape
    all_tokens = own_tokens * N_COL
    half_tokens = all_tokens // N_CORE
    mid_tokens = half_tokens // N_Z
    bf16, f32 = jnp.bfloat16, jnp.float32
    core = lax.axis_index("core").astype(jnp.int32).reshape(1)
    masks = [gate_mask, up_mask, down_mask]

    class_tokens = half_tokens // N_NEAR
    copies = local_kernel(
        spread_kernel,
        [shape((N_CORE * N_FAR, own_tokens // N_CORE, 2 * width), bf16)],
        [core, tokens, cotangent],
        1,
        stored=(1, 2),
        room=60,
        scratch=[pltpu.VMEM(tokens.shape, bf16)] * 2 + [pltpu.SemaphoreType.DMA((2,))],
    )
    scale_row = scales[None, :]
    weights = (gate_weight, up_weight, down_weight)
    own_weights, scale_lanes = local_kernel(
        prepare_kernel,
        [shape((width, 3 * hidden_width), bf16), shape((width, TILE), f32)],
        masks + [scale_row] + list(weights) + [copies],
        stored=range(8),
        room=60,
        scratch=[pltpu.SMEM(mask.shape, mask.dtype) for mask in masks]
        + [pltpu.VMEM((1, width), f32)]
        + [pltpu.VMEM(w.shape, w.dtype) for w in weights]
        + [pltpu.SemaphoreType.DMA((7,))],
    )
    blocks = exchange_in(copies, far_groups())
    other_scales = swap_cores(scale_row)
    blocks, own_weights, other_scales = lax.optimization_barrier(
        (blocks, own_weights, other_scales)
    )
    blocks = blocks.reshape(N_CORE, class_tokens, 2 * width)
    squares = local_kernel(
        squares_kernel,
        [shape((N_Z, 1, TILE), f32)],
        [core, blocks, scale_row, other_scales],
        1,
    )
    squares = exchange(squares, "z")
    copies = local_kernel(
        quantize_kernel,
        [shape((N_NEAR, class_tokens, 4 * width), bf16)],
        [core, squares, blocks, scale_row, other_scales],
        1,
    )
    copies, own_weights = lax.optimization_barrier((copies, own_weights))
    other_weights = swap_cores(own_weights)
    both_in = exchange_in(copies, near_groups()).reshape(half_tokens, 4 * width)

    flops = 12 * half_tokens * width * hidden_width
    sums = local_kernel(
        forward_kernel,
        [shape((half_tokens, 3 * hidden_width), bf16)],
        [core, both_in, own_weights, other_weights],
        1,
        flops,
        stored=(3,),
        scratch=[pltpu.VMEM(own_weights.shape, bf16), pltpu.SemaphoreType.DMA],
    )
    parts = exchange(sums.reshape(N_Z, mid_tokens, -1), "z")
    mid = local_kernel(swiglu_kernel, [shape(parts.shape, bf16)], [parts])
    mid = exchange(mid, "z").reshape(half_tokens, -1)
    back = local_kernel(
        back_kernel,
        [shape((half_tokens, 4 * width), bf16)],
        [core, mid, own_weights, other_weights],
        1,
        flops,
        stored=(3,),
        scratch=[pltpu.VMEM(own_weights.shape, bf16), pltpu.SemaphoreType.DMA],
    )
    parcel = local_kernel(
        parcel_kernel,
        [shape((half_tokens, 2 * width + 3 * hidden_width), bf16)],
        [core, both_in, mid],
        1,
    )
    back = exchange_in(back.reshape(N_NEAR, class_tokens, -1), near_groups())
    parcel = swap_cores(parcel)
    back = local_kernel(
        add_kernel, [shape((N_CORE, class_tokens, 2 * width), bf16)],
        [core, back, squares, blocks, scale_row, other_scales],
        1,
    )
    back = exchange_in(back.reshape(N_CORE * N_FAR, -1, 2 * width), far_groups())
    gate_grad, up_grad, down_grad = local_kernel(
        weight_grads_kernel,
        [shape(w.shape, bf16) for w in weights],
        [core] + masks + [both_in, mid, parcel, scale_lanes],
        4,
        flops,
    )
    output, input_grad = local_kernel(
        finish_kernel, [shape((own_tokens, width), bf16)] * 2, [back]
    )
    return (output, input_grad, gate_grad, up_grad, down_grad)


def solution(mesh):
    fine = Mesh(mesh.devices.reshape(N_Z, N_CORE, N_X, N_Y), ROW + COL)
    placed = (
        P(COL, ROW),
        P(ROW),
        P(ROW, COL),
        P(ROW, COL),
        P(COL, ROW),
        P(ROW, COL),
        P(ROW, COL),
        P(COL, ROW),
        P(COL, ROW),
    )
    return jax.shard_map(
        per_device,
        mesh=fine,
        in_specs=placed,
        out_specs=(
            P(COL, ROW),
            P(COL, ROW),
            P(ROW, COL),
            P(ROW, COL),
            P(COL, ROW),
        ),
        check_vma=False,
    )
```

```python
import functools

import jax
import jax.numpy as jnp
from jax import lax
from jax.experimental import pallas as pl
from jax.experimental.pallas import tpu as pltpu
from jax.sharding import Mesh, PartitionSpec as P

D = 8192
TILE = 128
ROW = ("z", "core")
COL = ("x", "y")
N_Z, N_CORE, N_X, N_Y = 8, 2, 4, 8
N_ROW = N_Z * N_CORE
N_COL = N_X * N_Y
PLANE = ("core",) + COL
N_NEAR = 4
N_FAR = N_COL // N_NEAR


clip_ratio = 1.5


def matmul(left, right):
    return jnp.dot(left, right, preferred_element_type=jnp.float32)


def contract_last(left, right):
    return lax.dot_general(
        left, right, (((1,), (1,)), ((), ())), preferred_element_type=jnp.float32
    )


def contract_first(left, right):
    return lax.dot_general(
        left, right, (((0,), (0,)), ((), ())), preferred_element_type=jnp.float32
    )


def swap_cores(block):
    return lax.ppermute(block, "core", [(0, 1), (1, 0)])


def exchange(parts, axis):
    return lax.all_to_all(parts, axis, 0, 0, tiled=True)


def plane_place(core, x, y):
    return (core * N_X + x % N_X) * N_Y + y % N_Y


def near_groups():
    groups = []
    for core in range(N_CORE):
        for x in range(core, N_X + core, 2):
            for y in range(core, N_Y + core, 2):
                block = [(x + i, y + j) for i in range(2) for j in range(2)]
                block.sort(key=lambda at: (at[0] % 2, at[1] % 2))
                groups.append([plane_place(core, *at) for at in block])
    return groups


def far_groups():
    return [
        [
            plane_place(core, x, y)
            for core in range(N_CORE)
            for x in range(x_parity, N_X, 2)
            for y in range(y_parity, N_Y, 2)
        ]
        for x_parity in range(2)
        for y_parity in range(2)
    ]


def exchange_in(parts, groups):
    return lax.all_to_all(parts, PLANE, 0, 0, axis_index_groups=groups, tiled=True)


def add_parts(parts):
    total = parts[0].astype(jnp.float32)
    for i in range(1, parts.shape[0]):
        total = total + parts[i].astype(jnp.float32)
    return total


def local_kernel(body, outs, args, scalars=0, flops=0, apart=(), stored=(), scratch=(), room=32):
    moved = sum(a.size * a.dtype.itemsize for a in list(args) + list(outs))
    spaces = [pltpu.SMEM if i < scalars else pltpu.VMEM for i in range(len(args))]
    for i in apart:
        spaces[i] = pl.ANY
    for i in stored:
        spaces[i] = pltpu.HBM
    specs = [pl.BlockSpec(memory_space=pltpu.VMEM)] * len(outs)
    return pl.pallas_call(
        body,
        out_shape=outs if len(outs) > 1 else outs[0],
        in_specs=[pl.BlockSpec(memory_space=space) for space in spaces],
        out_specs=specs if len(outs) > 1 else specs[0],
        scratch_shapes=list(scratch),
        compiler_params=pltpu.CompilerParams(vmem_limit_bytes=room << 20),
        cost_estimate=pl.CostEstimate(flops=flops, transcendentals=0, bytes_accessed=moved),
    )(*args)


def shape(dims, dtype):
    return jax.ShapeDtypeStruct(dims, dtype)


def on_diagonal(rows, lanes):
    row = lax.broadcasted_iota(jnp.int32, (rows, lanes), 0)
    return row == lax.broadcasted_iota(jnp.int32, (rows, lanes), 1)


def spread_kernel(core, tokens, cotangent, copies, tokens_here, cotangent_here, arrived):
    del core
    moves = [
        pltpu.make_async_copy(tokens, tokens_here, arrived.at[0]),
        pltpu.make_async_copy(cotangent, cotangent_here, arrived.at[1]),
    ]
    for move in moves:
        move.start()
    for move in moves:
        move.wait()
    rows, width = copies.shape[1], tokens.shape[1]
    for k, source in enumerate((tokens_here, cotangent_here)):
        value = source[...].astype(jnp.float32)
        for half in range(N_CORE):
            block = value[half * rows : (half + 1) * rows].astype(copies.dtype)
            for i in range(N_FAR):
                copies[half * N_FAR + i, :, k * width : (k + 1) * width] = block


def smoothed_of(core, blocks, scales, other_scales, place):
    width = scales.shape[1]
    scale = jnp.where(core[0] == place, scales[...], other_scales[...])
    return blocks[place, :, :width].astype(jnp.float32) / scale, scale


def squares_kernel(core, blocks, scales, other_scales, copies):
    squares = None
    for place in range(N_CORE):
        value, _ = smoothed_of(core, blocks, scales, other_scales, place)
        added = jnp.sum(value * value, axis=1, keepdims=True)
        squares = added if squares is None else squares + added
    rows, lanes = blocks.shape[1], copies.shape[2]
    total = jnp.sum(jnp.where(on_diagonal(rows, lanes), squares, 0.0), axis=0, keepdims=True)
    for i in range(copies.shape[0]):
        copies[i] = total


def prepare_kernel(
    gate_mask,
    up_mask,
    down_mask,
    scales,
    gate,
    up,
    down,
    order,
    weights,
    scale_lanes,
    gate_keeps,
    up_keeps,
    down_keeps,
    scales_here,
    gate_here,
    up_here,
    down_here,
    arrived,
):
    del order
    sources = (gate_mask, up_mask, down_mask, scales, gate, up, down)
    places = (gate_keeps, up_keeps, down_keeps, scales_here, gate_here, up_here, down_here)
    moves = [
        pltpu.make_async_copy(source, place, arrived.at[k])
        for k, (source, place) in enumerate(zip(sources, places))
    ]
    for move in moves:
        move.start()
    for move in moves[:5]:
        move.wait()
    width = gate.shape[1]
    count = gate.shape[0] // TILE
    for i in range(count):
        block = slice(i * TILE, (i + 1) * TILE)
        scale_lanes[block, :] = jnp.broadcast_to(scales_here[:, block], (TILE, TILE)).T
    tiles = [
        (i, j, slice(i * TILE, (i + 1) * TILE), slice(j * TILE, (j + 1) * TILE))
        for i in range(count)
        for j in range(width // TILE)
    ]
    for i, j, rows, columns in tiles:
        keep = gate_keeps[i, j].astype(jnp.float32)
        kept = scale_lanes[rows, :] * gate_here[rows, columns].astype(jnp.float32) * keep
        weights[rows, columns] = kept.astype(weights.dtype)
    moves[5].wait()
    for i, j, rows, columns in tiles:
        keep = up_keeps[i, j].astype(jnp.float32)
        kept = scale_lanes[rows, :] * up_here[rows, columns].astype(jnp.float32) * keep
        shifted = slice(width + columns.start, width + columns.stop)
        weights[rows, shifted] = kept.astype(weights.dtype)
    moves[6].wait()
    for i, j, rows, columns in tiles:
        keep = down_keeps[i, j].astype(jnp.float32)
        kept = down_here[rows, columns].astype(jnp.float32) * keep
        shifted = slice(2 * width + columns.start, 2 * width + columns.stop)
        weights[rows, shifted] = kept.astype(weights.dtype)


def limits_of(squares, rows):
    total = jnp.where(on_diagonal(rows, TILE), add_parts(squares), 0.0)
    mean_square = jnp.sum(total, axis=1, keepdims=True) / D
    return clip_ratio * jnp.sqrt(mean_square + 1e-06)


def quantize_kernel(core, squares, blocks, scales, other_scales, copies):
    rows, width = blocks.shape[1], scales.shape[1]
    limits = limits_of(squares, rows)
    for place in range(N_CORE):
        value, _ = smoothed_of(core, blocks, scales, other_scales, place)
        squashed = jnp.tanh(value / limits)
        quantized = (limits * squashed).astype(copies.dtype)
        start = 2 * place * width
        for i in range(copies.shape[0]):
            copies[i, :, start : start + width] = quantized
            copies[i, :, start + width : start + 2 * width] = blocks[place, :, width:]


def lanes_of(core, start, width, count=1):
    return pl.ds(pl.multiple_of(core * 2 * width + start, TILE), count * width)


def fetch(source, place, arrived):
    pieces = arrived.shape[0]
    rows = source.shape[0] // pieces
    moves = []
    for k in range(pieces):
        piece = pl.ds(k * rows, rows)
        moves.append(pltpu.make_async_copy(source.at[piece], place.at[piece], arrived.at[k]))
    for move in moves:
        move.start()
    return moves


def forward_kernel(core, both_in, own_weights, other_stored, sums, other_weights, arrived):
    moves = fetch(other_stored, other_weights, arrived)
    width = own_weights.shape[0]
    split = sums.shape[1] - width
    gate_up = None
    for place, weights in ((core[0], own_weights), (1 - core[0], other_weights)):
        if weights is other_weights:
            for move in moves:
                move.wait()
        quantized = both_in[:, lanes_of(place, 0, width)]
        gradient = both_in[:, lanes_of(place, width, width)]
        first = matmul(quantized, weights[:, :split])
        second = contract_last(gradient, weights[:, split:])
        if gate_up is None:
            gate_up, hidden_grad = first, second
        else:
            gate_up, hidden_grad = gate_up + first, hidden_grad + second
    sums[:, :split] = gate_up.astype(sums.dtype)
    sums[:, split:] = hidden_grad.astype(sums.dtype)


def swiglu_kernel(parts, copies):
    pre = add_parts(parts)
    width = pre.shape[1] // 3
    gate_pre = pre[:, :width]
    up_pre = pre[:, width : 2 * width]
    hidden_grad = pre[:, 2 * width :]
    sigmoid_gate = 1.0 / (1.0 + jnp.exp(-gate_pre))
    silu_gate = gate_pre * sigmoid_gate
    gate_dir = hidden_grad * up_pre * sigmoid_gate * (1.0 + gate_pre * (1.0 - sigmoid_gate))
    up_dir = hidden_grad * silu_gate
    hidden = silu_gate * up_pre
    for k, value in enumerate((gate_dir, up_dir, hidden)):
        rounded = value.astype(copies.dtype)
        for i in range(copies.shape[0]):
            copies[i, :, k * width : (k + 1) * width] = rounded


def parcel_kernel(core, both_in, mid, parcel):
    width = both_in.shape[1] // 4
    parcel[:, : 2 * width] = both_in[:, lanes_of(1 - core[0], 0, width, 2)]
    parcel[:, 2 * width :] = mid[...]


def back_kernel(core, mid, own_weights, other_stored, back, other_weights, arrived):
    moves = fetch(other_stored, other_weights, arrived)
    width = own_weights.shape[0]
    split = mid.shape[1] - width
    for place, weights in ((core[0], own_weights), (1 - core[0], other_weights)):
        if weights is other_weights:
            for move in moves:
                move.wait()
        output = matmul(mid[:, split:], weights[:, split:])
        back[:, lanes_of(place, 0, width)] = output.astype(back.dtype)
        quant_grad = contract_last(mid[:, :split], weights[:, :split])
        back[:, lanes_of(place, width, width)] = quant_grad.astype(back.dtype)


def weight_grads_kernel(
    core,
    gate_mask,
    up_mask,
    down_mask,
    both_in,
    mid,
    parcel,
    scales,
    gate_grad,
    up_grad,
    down_grad,
):
    width = gate_grad.shape[0]
    split = mid.shape[1] - width
    own_quantized = both_in[:, lanes_of(core[0], 0, width)]
    own_gradient = both_in[:, lanes_of(core[0], width, width)]
    start = 2 * width
    for i in range(width // TILE):
        block = slice(i * TILE, (i + 1) * TILE)
        product = contract_first(own_quantized[:, block], mid[:, :split])
        product = product + contract_first(parcel[:, block], parcel[:, start : start + split])
        for j in range(split // TILE):
            mask, grad = (gate_mask, gate_grad) if j < split // TILE // 2 else (up_mask, up_grad)
            column = j % (split // TILE // 2)
            tile = product[:, j * TILE : (j + 1) * TILE]
            keep = mask[i, column].astype(jnp.float32)
            grad[block, column * TILE : (column + 1) * TILE] = (
                scales[block, :] * tile * keep
            ).astype(grad.dtype)
    for i in range(down_grad.shape[0] // TILE):
        units = slice(split + i * TILE, split + (i + 1) * TILE)
        others = slice(start + units.start, start + units.stop)
        product = contract_first(mid[:, units], own_gradient)
        product = product + contract_first(parcel[:, others], parcel[:, width:start])
        for j in range(width // TILE):
            columns = slice(j * TILE, (j + 1) * TILE)
            keep = down_mask[i, j].astype(jnp.float32)
            down_grad[i * TILE : (i + 1) * TILE, columns] = (product[:, columns] * keep).astype(
                down_grad.dtype
            )


def add_kernel(core, parts, squares, blocks, scales, other_scales, totals):
    total = add_parts(parts)
    limits = limits_of(squares, blocks.shape[1])
    width = totals.shape[2] // 2
    for place in range(totals.shape[0]):
        start = 2 * place * width
        output = total[:, start : start + width]
        quant_grad = total[:, start + width : start + 2 * width]
        value, scale = smoothed_of(core, blocks, scales, other_scales, place)
        squashed = jnp.tanh(value / limits)
        factor = (1.0 - squashed * squashed) / scale
        totals[place, :, :width] = output.astype(totals.dtype)
        totals[place, :, width:] = (quant_grad * factor).astype(totals.dtype)


def finish_kernel(parts, output, input_grad):
    total = jnp.concatenate([add_parts(parts[:N_FAR]), add_parts(parts[N_FAR:])], axis=0)
    width = output.shape[1]
    output[...] = total[:, :width].astype(output.dtype)
    input_grad[...] = total[:, width:].astype(input_grad.dtype)


def per_device(
    tokens, scales, gate_weight, up_weight, down_weight, gate_mask, up_mask, down_mask, cotangent
):
    hidden_width = gate_weight.shape[1]
    own_tokens, width = tokens.shape
    all_tokens = own_tokens * N_COL
    half_tokens = all_tokens // N_CORE
    mid_tokens = half_tokens // N_Z
    bf16, f32 = jnp.bfloat16, jnp.float32
    core = lax.axis_index("core").astype(jnp.int32).reshape(1)
    masks = [gate_mask, up_mask, down_mask]

    class_tokens = half_tokens // N_NEAR
    copies = local_kernel(
        spread_kernel,
        [shape((N_CORE * N_FAR, own_tokens // N_CORE, 2 * width), bf16)],
        [core, tokens, cotangent],
        1,
        stored=(1, 2),
        room=60,
        scratch=[pltpu.VMEM(tokens.shape, bf16)] * 2 + [pltpu.SemaphoreType.DMA((2,))],
    )
    scale_row = scales[None, :]
    weights = (gate_weight, up_weight, down_weight)
    own_weights, scale_lanes = local_kernel(
        prepare_kernel,
        [shape((width, 3 * hidden_width), bf16), shape((width, TILE), f32)],
        masks + [scale_row] + list(weights) + [copies],
        stored=range(8),
        room=60,
        scratch=[pltpu.SMEM(mask.shape, mask.dtype) for mask in masks]
        + [pltpu.VMEM((1, width), f32)]
        + [pltpu.VMEM(w.shape, w.dtype) for w in weights]
        + [pltpu.SemaphoreType.DMA((7,))],
    )
    blocks = exchange_in(copies, far_groups())
    other_scales = swap_cores(scale_row)
    blocks, own_weights, other_scales = lax.optimization_barrier(
        (blocks, own_weights, other_scales)
    )
    blocks = blocks.reshape(N_CORE, class_tokens, 2 * width)
    squares = local_kernel(
        squares_kernel,
        [shape((N_Z, 1, TILE), f32)],
        [core, blocks, scale_row, other_scales],
        1,
    )
    squares = exchange(squares, "z")
    copies = local_kernel(
        quantize_kernel,
        [shape((N_NEAR, class_tokens, 4 * width), bf16)],
        [core, squares, blocks, scale_row, other_scales],
        1,
    )
    copies, own_weights = lax.optimization_barrier((copies, own_weights))
    other_weights = swap_cores(own_weights)
    both_in = exchange_in(copies, near_groups()).reshape(half_tokens, 4 * width)

    flops = 12 * half_tokens * width * hidden_width
    sums = local_kernel(
        forward_kernel,
        [shape((half_tokens, 3 * hidden_width), bf16)],
        [core, both_in, own_weights, other_weights],
        1,
        flops,
        stored=(3,),
        scratch=[pltpu.VMEM(own_weights.shape, bf16), pltpu.SemaphoreType.DMA((8,))],
    )
    parts = exchange(sums.reshape(N_Z, mid_tokens, -1), "z")
    mid = local_kernel(swiglu_kernel, [shape(parts.shape, bf16)], [parts])
    mid = exchange(mid, "z").reshape(half_tokens, -1)
    back = local_kernel(
        back_kernel,
        [shape((half_tokens, 4 * width), bf16)],
        [core, mid, own_weights, other_weights],
        1,
        flops,
        stored=(3,),
        scratch=[pltpu.VMEM(own_weights.shape, bf16), pltpu.SemaphoreType.DMA((8,))],
    )
    parcel = local_kernel(
        parcel_kernel,
        [shape((half_tokens, 2 * width + 3 * hidden_width), bf16)],
        [core, both_in, mid],
        1,
    )
    back = exchange_in(back.reshape(N_NEAR, class_tokens, -1), near_groups())
    parcel = swap_cores(parcel)
    back = local_kernel(
        add_kernel, [shape((N_CORE, class_tokens, 2 * width), bf16)],
        [core, back, squares, blocks, scale_row, other_scales],
        1,
    )
    back = exchange_in(back.reshape(N_CORE * N_FAR, -1, 2 * width), far_groups())
    gate_grad, up_grad, down_grad = local_kernel(
        weight_grads_kernel,
        [shape(w.shape, bf16) for w in weights],
        [core] + masks + [both_in, mid, parcel, scale_lanes],
        4,
        flops,
    )
    output, input_grad = local_kernel(
        finish_kernel, [shape((own_tokens, width), bf16)] * 2, [back]
    )
    return (output, input_grad, gate_grad, up_grad, down_grad)


def solution(mesh):
    fine = Mesh(mesh.devices.reshape(N_Z, N_CORE, N_X, N_Y), ROW + COL)
    placed = (
        P(COL, ROW),
        P(ROW),
        P(ROW, COL),
        P(ROW, COL),
        P(COL, ROW),
        P(ROW, COL),
        P(ROW, COL),
        P(COL, ROW),
        P(COL, ROW),
    )
    return jax.shard_map(
        per_device,
        mesh=fine,
        in_specs=placed,
        out_specs=(
            P(COL, ROW),
            P(COL, ROW),
            P(ROW, COL),
            P(ROW, COL),
            P(COL, ROW),
        ),
        check_vma=False,
    )
```

```python
import functools

import jax
import jax.numpy as jnp
from jax import lax
from jax.experimental import pallas as pl
from jax.experimental.pallas import tpu as pltpu
from jax.sharding import Mesh, PartitionSpec as P

D = 8192
TILE = 128
ROW = ("z", "core")
COL = ("x", "y")
N_Z, N_CORE, N_X, N_Y = 8, 2, 4, 8
N_ROW = N_Z * N_CORE
N_COL = N_X * N_Y
PLANE = ("core",) + COL
N_NEAR = 4
N_FAR = N_COL // N_NEAR


clip_ratio = 1.5


def matmul(left, right):
    return jnp.dot(left, right, preferred_element_type=jnp.float32)


def contract_last(left, right):
    return lax.dot_general(
        left, right, (((1,), (1,)), ((), ())), preferred_element_type=jnp.float32
    )


def contract_first(left, right):
    return lax.dot_general(
        left, right, (((0,), (0,)), ((), ())), preferred_element_type=jnp.float32
    )


def swap_cores(block):
    return lax.ppermute(block, "core", [(0, 1), (1, 0)])


def exchange(parts, axis):
    return lax.all_to_all(parts, axis, 0, 0, tiled=True)


def plane_place(core, x, y):
    return (core * N_X + x % N_X) * N_Y + y % N_Y


def near_groups():
    groups = []
    for core in range(N_CORE):
        for x in range(core, N_X + core, 2):
            for y in range(core, N_Y + core, 2):
                block = [(x + i, y + j) for i in range(2) for j in range(2)]
                block.sort(key=lambda at: (at[0] % 2, at[1] % 2))
                groups.append([plane_place(core, *at) for at in block])
    return groups


def far_groups():
    return [
        [
            plane_place(core, x, y)
            for core in range(N_CORE)
            for x in range(x_parity, N_X, 2)
            for y in range(y_parity, N_Y, 2)
        ]
        for x_parity in range(2)
        for y_parity in range(2)
    ]


def exchange_in(parts, groups):
    return lax.all_to_all(parts, PLANE, 0, 0, axis_index_groups=groups, tiled=True)


def add_parts(parts):
    total = parts[0].astype(jnp.float32)
    for i in range(1, parts.shape[0]):
        total = total + parts[i].astype(jnp.float32)
    return total


def local_kernel(body, outs, args, scalars=0, flops=0, apart=(), stored=(), scratch=(), room=32):
    moved = sum(a.size * a.dtype.itemsize for a in list(args) + list(outs))
    spaces = [pltpu.SMEM if i < scalars else pltpu.VMEM for i in range(len(args))]
    for i in apart:
        spaces[i] = pl.ANY
    for i in stored:
        spaces[i] = pltpu.HBM
    specs = [pl.BlockSpec(memory_space=pltpu.VMEM)] * len(outs)
    return pl.pallas_call(
        body,
        out_shape=outs if len(outs) > 1 else outs[0],
        in_specs=[pl.BlockSpec(memory_space=space) for space in spaces],
        out_specs=specs if len(outs) > 1 else specs[0],
        scratch_shapes=list(scratch),
        compiler_params=pltpu.CompilerParams(vmem_limit_bytes=room << 20),
        cost_estimate=pl.CostEstimate(flops=flops, transcendentals=0, bytes_accessed=moved),
    )(*args)


def shape(dims, dtype):
    return jax.ShapeDtypeStruct(dims, dtype)


def on_diagonal(rows, lanes):
    row = lax.broadcasted_iota(jnp.int32, (rows, lanes), 0)
    return row == lax.broadcasted_iota(jnp.int32, (rows, lanes), 1)


def spread_kernel(core, tokens, cotangent, copies, tokens_here, cotangent_here, arrived):
    del core
    moves = [
        pltpu.make_async_copy(tokens, tokens_here, arrived.at[0]),
        pltpu.make_async_copy(cotangent, cotangent_here, arrived.at[1]),
    ]
    for move in moves:
        move.start()
    rows, width = copies.shape[1], tokens.shape[1]
    for k, source in enumerate((tokens_here, cotangent_here)):
        moves[k].wait()
        value = source[...].astype(jnp.float32)
        for half in range(N_CORE):
            block = value[half * rows : (half + 1) * rows].astype(copies.dtype)
            for i in range(N_FAR):
                copies[half * N_FAR + i, :, k * width : (k + 1) * width] = block


def smoothed_of(core, blocks, scales, other_scales, place):
    width = scales.shape[1]
    scale = jnp.where(core[0] == place, scales[...], other_scales[...])
    return blocks[place, :, :width].astype(jnp.float32) / scale, scale


def squares_kernel(core, blocks, scales, other_scales, copies):
    squares = None
    for place in range(N_CORE):
        value, _ = smoothed_of(core, blocks, scales, other_scales, place)
        added = jnp.sum(value * value, axis=1, keepdims=True)
        squares = added if squares is None else squares + added
    rows, lanes = blocks.shape[1], copies.shape[2]
    total = jnp.sum(jnp.where(on_diagonal(rows, lanes), squares, 0.0), axis=0, keepdims=True)
    for i in range(copies.shape[0]):
        copies[i] = total


def prepare_kernel(
    gate_mask,
    up_mask,
    down_mask,
    scales,
    gate,
    up,
    down,
    order,
    weights,
    scale_lanes,
    gate_keeps,
    up_keeps,
    down_keeps,
    scales_here,
    gate_here,
    up_here,
    down_here,
    arrived,
):
    del order
    sources = (gate_mask, up_mask, down_mask, scales, gate, up, down)
    places = (gate_keeps, up_keeps, down_keeps, scales_here, gate_here, up_here, down_here)
    moves = [
        pltpu.make_async_copy(source, place, arrived.at[k])
        for k, (source, place) in enumerate(zip(sources, places))
    ]
    for move in moves:
        move.start()
    for move in moves[:5]:
        move.wait()
    width = gate.shape[1]
    count = gate.shape[0] // TILE
    for i in range(count):
        block = slice(i * TILE, (i + 1) * TILE)
        scale_lanes[block, :] = jnp.broadcast_to(scales_here[:, block], (TILE, TILE)).T
    tiles = [
        (i, j, slice(i * TILE, (i + 1) * TILE), slice(j * TILE, (j + 1) * TILE))
        for i in range(count)
        for j in range(width // TILE)
    ]
    for i, j, rows, columns in tiles:
        keep = gate_keeps[i, j].astype(jnp.float32)
        kept = scale_lanes[rows, :] * gate_here[rows, columns].astype(jnp.float32) * keep
        weights[rows, columns] = kept.astype(weights.dtype)
    moves[5].wait()
    for i, j, rows, columns in tiles:
        keep = up_keeps[i, j].astype(jnp.float32)
        kept = scale_lanes[rows, :] * up_here[rows, columns].astype(jnp.float32) * keep
        shifted = slice(width + columns.start, width + columns.stop)
        weights[rows, shifted] = kept.astype(weights.dtype)
    moves[6].wait()
    for i, j, rows, columns in tiles:
        keep = down_keeps[i, j].astype(jnp.float32)
        kept = down_here[rows, columns].astype(jnp.float32) * keep
        shifted = slice(2 * width + columns.start, 2 * width + columns.stop)
        weights[rows, shifted] = kept.astype(weights.dtype)


def limits_of(squares, rows):
    total = jnp.where(on_diagonal(rows, TILE), add_parts(squares), 0.0)
    mean_square = jnp.sum(total, axis=1, keepdims=True) / D
    return clip_ratio * jnp.sqrt(mean_square + 1e-06)


def quantize_kernel(core, squares, blocks, scales, other_scales, copies):
    rows, width = blocks.shape[1], scales.shape[1]
    limits = limits_of(squares, rows)
    for place in range(N_CORE):
        value, _ = smoothed_of(core, blocks, scales, other_scales, place)
        squashed = jnp.tanh(value / limits)
        quantized = (limits * squashed).astype(copies.dtype)
        start = 2 * place * width
        for i in range(copies.shape[0]):
            copies[i, :, start : start + width] = quantized
            copies[i, :, start + width : start + 2 * width] = blocks[place, :, width:]


def lanes_of(core, start, width, count=1):
    return pl.ds(pl.multiple_of(core * 2 * width + start, TILE), count * width)


def forward_kernel(core, both_in, own_weights, other_weights, sums):
    width = own_weights.shape[0]
    split = sums.shape[1] - width
    gate_up = None
    for place, weights in ((core[0], own_weights), (1 - core[0], other_weights)):
        quantized = both_in[:, lanes_of(place, 0, width)]
        gradient = both_in[:, lanes_of(place, width, width)]
        first = matmul(quantized, weights[:, :split])
        second = contract_last(gradient, weights[:, split:])
        if gate_up is None:
            gate_up, hidden_grad = first, second
        else:
            gate_up, hidden_grad = gate_up + first, hidden_grad + second
    sums[:, :split] = gate_up.astype(sums.dtype)
    sums[:, split:] = hidden_grad.astype(sums.dtype)


def swiglu_kernel(parts, copies):
    pre = add_parts(parts)
    width = pre.shape[1] // 3
    gate_pre = pre[:, :width]
    up_pre = pre[:, width : 2 * width]
    hidden_grad = pre[:, 2 * width :]
    sigmoid_gate = 1.0 / (1.0 + jnp.exp(-gate_pre))
    silu_gate = gate_pre * sigmoid_gate
    gate_dir = hidden_grad * up_pre * sigmoid_gate * (1.0 + gate_pre * (1.0 - sigmoid_gate))
    up_dir = hidden_grad * silu_gate
    hidden = silu_gate * up_pre
    for k, value in enumerate((gate_dir, up_dir, hidden)):
        rounded = value.astype(copies.dtype)
        for i in range(copies.shape[0]):
            copies[i, :, k * width : (k + 1) * width] = rounded


def parcel_kernel(core, both_in, mid, parcel):
    width = both_in.shape[1] // 4
    parcel[:, : 2 * width] = both_in[:, lanes_of(1 - core[0], 0, width, 2)]
    parcel[:, 2 * width :] = mid[...]


def back_kernel(core, mid, own_weights, other_weights, back):
    width = own_weights.shape[0]
    split = mid.shape[1] - width
    for place, weights in ((core[0], own_weights), (1 - core[0], other_weights)):
        output = matmul(mid[:, split:], weights[:, split:])
        back[:, lanes_of(place, 0, width)] = output.astype(back.dtype)
        quant_grad = contract_last(mid[:, :split], weights[:, :split])
        back[:, lanes_of(place, width, width)] = quant_grad.astype(back.dtype)


def weight_grads_kernel(
    core,
    gate_mask,
    up_mask,
    down_mask,
    both_in,
    mid,
    parcel,
    scales,
    gate_grad,
    up_grad,
    down_grad,
):
    width = gate_grad.shape[0]
    split = mid.shape[1] - width
    own_quantized = both_in[:, lanes_of(core[0], 0, width)]
    own_gradient = both_in[:, lanes_of(core[0], width, width)]
    start = 2 * width
    for i in range(width // TILE):
        block = slice(i * TILE, (i + 1) * TILE)
        product = contract_first(own_quantized[:, block], mid[:, :split])
        product = product + contract_first(parcel[:, block], parcel[:, start : start + split])
        for j in range(split // TILE):
            mask, grad = (gate_mask, gate_grad) if j < split // TILE // 2 else (up_mask, up_grad)
            column = j % (split // TILE // 2)
            tile = product[:, j * TILE : (j + 1) * TILE]
            keep = mask[i, column].astype(jnp.float32)
            grad[block, column * TILE : (column + 1) * TILE] = (
                scales[block, :] * tile * keep
            ).astype(grad.dtype)
    for i in range(down_grad.shape[0] // TILE):
        units = slice(split + i * TILE, split + (i + 1) * TILE)
        others = slice(start + units.start, start + units.stop)
        product = contract_first(mid[:, units], own_gradient)
        product = product + contract_first(parcel[:, others], parcel[:, width:start])
        for j in range(width // TILE):
            columns = slice(j * TILE, (j + 1) * TILE)
            keep = down_mask[i, j].astype(jnp.float32)
            down_grad[i * TILE : (i + 1) * TILE, columns] = (product[:, columns] * keep).astype(
                down_grad.dtype
            )


def add_kernel(core, parts, squares, blocks, scales, other_scales, totals):
    total = add_parts(parts)
    limits = limits_of(squares, blocks.shape[1])
    width = totals.shape[2] // 2
    for place in range(totals.shape[0]):
        start = 2 * place * width
        output = total[:, start : start + width]
        quant_grad = total[:, start + width : start + 2 * width]
        value, scale = smoothed_of(core, blocks, scales, other_scales, place)
        squashed = jnp.tanh(value / limits)
        factor = (1.0 - squashed * squashed) / scale
        totals[place, :, :width] = output.astype(totals.dtype)
        totals[place, :, width:] = (quant_grad * factor).astype(totals.dtype)


def finish_kernel(parts, output, input_grad):
    total = jnp.concatenate([add_parts(parts[:N_FAR]), add_parts(parts[N_FAR:])], axis=0)
    width = output.shape[1]
    output[...] = total[:, :width].astype(output.dtype)
    input_grad[...] = total[:, width:].astype(input_grad.dtype)


def per_device(
    tokens, scales, gate_weight, up_weight, down_weight, gate_mask, up_mask, down_mask, cotangent
):
    hidden_width = gate_weight.shape[1]
    own_tokens, width = tokens.shape
    all_tokens = own_tokens * N_COL
    half_tokens = all_tokens // N_CORE
    mid_tokens = half_tokens // N_Z
    bf16, f32 = jnp.bfloat16, jnp.float32
    core = lax.axis_index("core").astype(jnp.int32).reshape(1)
    masks = [gate_mask, up_mask, down_mask]

    class_tokens = half_tokens // N_NEAR
    copies = local_kernel(
        spread_kernel,
        [shape((N_CORE * N_FAR, own_tokens // N_CORE, 2 * width), bf16)],
        [core, tokens, cotangent],
        1,
        stored=(1, 2),
        room=60,
        scratch=[pltpu.VMEM(tokens.shape, bf16)] * 2 + [pltpu.SemaphoreType.DMA((2,))],
    )
    scale_row = scales[None, :]
    weights = (gate_weight, up_weight, down_weight)
    own_weights, scale_lanes = local_kernel(
        prepare_kernel,
        [shape((width, 3 * hidden_width), bf16), shape((width, TILE), f32)],
        masks + [scale_row] + list(weights) + [copies],
        stored=range(8),
        room=60,
        scratch=[pltpu.SMEM(mask.shape, mask.dtype) for mask in masks]
        + [pltpu.VMEM((1, width), f32)]
        + [pltpu.VMEM(w.shape, w.dtype) for w in weights]
        + [pltpu.SemaphoreType.DMA((7,))],
    )
    blocks = exchange_in(copies, far_groups())
    other_scales = swap_cores(scale_row)
    blocks, own_weights, other_scales = lax.optimization_barrier(
        (blocks, own_weights, other_scales)
    )
    other_weights = swap_cores(own_weights)
    blocks = blocks.reshape(N_CORE, class_tokens, 2 * width)
    squares = local_kernel(
        squares_kernel,
        [shape((N_Z, 1, TILE), f32)],
        [core, blocks, scale_row, other_scales],
        1,
    )
    squares = exchange(squares, "z")
    copies = local_kernel(
        quantize_kernel,
        [shape((N_NEAR, class_tokens, 4 * width), bf16)],
        [core, squares, blocks, scale_row, other_scales],
        1,
    )
    copies, other_weights = lax.optimization_barrier((copies, other_weights))
    both_in = exchange_in(copies, near_groups()).reshape(half_tokens, 4 * width)

    flops = 12 * half_tokens * width * hidden_width
    sums = local_kernel(
        forward_kernel,
        [shape((half_tokens, 3 * hidden_width), bf16)],
        [core, both_in, own_weights, other_weights],
        1,
        flops,
    )
    parts = exchange(sums.reshape(N_Z, mid_tokens, -1), "z")
    mid = local_kernel(swiglu_kernel, [shape(parts.shape, bf16)], [parts])
    mid = exchange(mid, "z").reshape(half_tokens, -1)
    back = local_kernel(
        back_kernel,
        [shape((half_tokens, 4 * width), bf16)],
        [core, mid, own_weights, other_weights],
        1,
        flops,
    )
    parcel = local_kernel(
        parcel_kernel,
        [shape((half_tokens, 2 * width + 3 * hidden_width), bf16)],
        [core, both_in, mid],
        1,
    )
    back = exchange_in(back.reshape(N_NEAR, class_tokens, -1), near_groups())
    parcel = swap_cores(parcel)
    back = local_kernel(
        add_kernel, [shape((N_CORE, class_tokens, 2 * width), bf16)],
        [core, back, squares, blocks, scale_row, other_scales],
        1,
    )
    back = exchange_in(back.reshape(N_CORE * N_FAR, -1, 2 * width), far_groups())
    gate_grad, up_grad, down_grad = local_kernel(
        weight_grads_kernel,
        [shape(w.shape, bf16) for w in weights],
        [core] + masks + [both_in, mid, parcel, scale_lanes],
        4,
        flops,
    )
    output, input_grad = local_kernel(
        finish_kernel, [shape((own_tokens, width), bf16)] * 2, [back]
    )
    return (output, input_grad, gate_grad, up_grad, down_grad)


def solution(mesh):
    fine = Mesh(mesh.devices.reshape(N_Z, N_CORE, N_X, N_Y), ROW + COL)
    placed = (
        P(COL, ROW),
        P(ROW),
        P(ROW, COL),
        P(ROW, COL),
        P(COL, ROW),
        P(ROW, COL),
        P(ROW, COL),
        P(COL, ROW),
        P(COL, ROW),
    )
    return jax.shard_map(
        per_device,
        mesh=fine,
        in_specs=placed,
        out_specs=(
            P(COL, ROW),
            P(COL, ROW),
            P(ROW, COL),
            P(ROW, COL),
            P(COL, ROW),
        ),
        check_vma=False,
    )
```
